32 devices in a mesh: rep: 8 (over z, x), shard: 4 (over y, core).
Axes of the slice: x: 2, y: 2, z: 4, core: 2. Of those that a mesh axis runs over, the one named last changes fastest.
Arguments:
- latent_tokens: bfloat16 [256, 256, 384], P(('rep', 'shard')), may hold values from -6 to 6
- cond: bfloat16 [256, 384], P(('rep', 'shard')), may hold values from -6 to 6
- w_ada: bfloat16 [384, 2304], P('shard'), may hold values from -0.3125 to 0.3125
- b_ada: bfloat16 [2304], P('shard'), may hold values from -3 to 3
- w_qkv: bfloat16 [384, 1152], P('shard'), may hold values from -0.3125 to 0.3125
- b_qv: bfloat16 [768], P('shard'), may hold values from -3 to 3
- w_o: bfloat16 [384, 384], P('shard'), may hold values from -0.875 to 0.875
- b_o: bfloat16 [384], P('shard'), may hold values from -3 to 3
- w_1: bfloat16 [384, 1536], P('shard'), may hold values from -0.3125 to 0.3125
- b_1: bfloat16 [1536], P('shard'), may hold values from -3 to 3
- w_2: bfloat16 [1536, 384], P('shard'), may hold values from -0.15625 to 0.15625
- b_2: bfloat16 [384], P('shard'), may hold values from -3 to 3
- grad_out: bfloat16 [256, 256, 384], P(('rep', 'shard')), may hold values from -6 to 6
Outputs:
- block_out: bfloat16 [256, 256, 384], P(('rep', 'shard'))
- grad_tokens: float32 [256, 256, 384], P(('rep', 'shard'))
- grad_cond: float32 [256, 384], P(('rep', 'shard'))
- grad_w_ada: float32 [384, 2304], P('shard')
- grad_b_ada: float32 [2304], P('shard')
- grad_w_qkv: float32 [384, 1152], P('shard')
- grad_b_qv: float32 [768], P('shard')
- grad_w_o: float32 [384, 384], P('shard')
- grad_b_o: float32 [384], P('shard')
- grad_w_1: float32 [384, 1536], P('shard')
- grad_b_1: float32 [1536], P('shard')
- grad_w_2: float32 [1536, 384], P('shard')
- grad_b_2: float32 [384], P('shard')
The draws below stay inside these ranges and needn't reach their ends.
All inputs are finite; a program needn't handle non-finite values.
Results may differ from the reference program's by a relative error of at most 0.019.
The reference program's roundings to bfloat16 on the way count: a program that leaves them out, or rounds other values in their place, can miss the bound.
Values may be sent and summed in bfloat16 or wider, within the bound.
No kernel may reach another device: no remote copies, remote signals or barrier semaphores. Data moves between devices by JAX's collectives and lax.ppermute only.
A program may use at most 128 MiB of HBM per device.

```python
import jax
import jax.numpy as jnp
from jax import lax

D = 384
HEADS = 6
FF = 1536
SEQ = 256
LAT_DEV = 8
HD = 64
ADA = 2304
LAT = 256


def block_levels(own_key, extent, shards, least, top_value):
    def one(axis_at, shards_of):
        draws = jax.random.uniform(jax.random.fold_in(jax.random.fold_in(own_key, 6), axis_at), (shards_of,), jnp.float32, least / len(shards), top_value / len(shards))
        return jnp.repeat(jnp.exp(draws), extent[axis_at] // shards_of).reshape((-1,) + (1,) * (len(extent) - axis_at - 1))

    loudness = one(*shards[0])
    for cut in shards[1:]:
        loudness = loudness * one(*cut)
    return loudness


def gaussian(rng, shape, deviation, limit, cuts=(), kind=jnp.bfloat16):
    loudness = block_levels(rng, shape, cuts, -0.22, 0.18) if cuts else 1.0
    values = jax.random.normal(rng, shape, jnp.float32) * deviation * loudness
    return jnp.minimum(jnp.maximum(values, -limit), limit).astype(kind)


def setup_inputs(seed: int = 0) -> dict:
    key_of = jax.random.split(jax.random.key(seed), 14)
    latent_tokens = gaussian(key_of[0], (LAT, SEQ, D), 1.0, 6.0, ((0, 32),))
    cond = gaussian(key_of[1], (LAT, D), 1.0, 6.0, ((0, 32),))
    w_ada = gaussian(key_of[2], (D, ADA), D ** -0.5, 0.3125, ((0, 4),))
    b_ada = gaussian(key_of[3], (ADA,), 0.5, 3.0, ((0, 4),))
    w_qkv = gaussian(key_of[4], (D, 3 * D), D ** -0.5, 0.3125, ((0, 4),))
    b_qv = gaussian(key_of[5], (2 * D,), 0.5, 3.0, ((0, 4),))
    w_o = gaussian(key_of[6], (D, D), (D // 8) ** -0.5, 0.875, ((0, 4),))
    b_o = gaussian(key_of[7], (D,), 0.5, 3.0, ((0, 4),))
    w_1 = gaussian(key_of[8], (D, FF), D ** -0.5, 0.3125, ((0, 4),))
    b_1 = gaussian(key_of[9], (FF,), 0.5, 3.0, ((0, 4),))
    w_2 = gaussian(key_of[10], (FF, D), FF ** -0.5, 0.15625, ((0, 4),))
    b_2 = gaussian(key_of[11], (D,), 0.5, 3.0, ((0, 4),))
    grad_out = gaussian(key_of[12], (LAT, SEQ, D), 1.0, 6.0, ((0, 32),))
    return {"latent_tokens": latent_tokens, "cond": cond, "w_ada": w_ada, "b_ada": b_ada, "w_qkv": w_qkv, "b_qv": b_qv, "w_o": w_o, "b_o": b_o, "w_1": w_1, "b_1": b_1, "w_2": w_2, "b_2": b_2, "grad_out": grad_out}


@jax.custom_vjp
def low(v):
    return lax.optimization_barrier(v.astype(jnp.bfloat16)).astype(jnp.float32)

@jax.custom_vjp
def low_back(v):
    return v

def low_keep(v):
    return (low(v), None)

def low_pass(kept, grad):
    return (grad,)

def back_keep(v):
    return (v, None)

def back_low(kept, grad):
    return (low(grad),)
low.defvjp(low_keep, low_pass)
low_back.defvjp(back_keep, back_low)

def matmul(left, right):
    return jnp.einsum('...d,de->...e', left, right, precision=lax.Precision.HIGHEST)

def layer_norm(value):
    centred = value - lax.optimization_barrier(jnp.mean(value, axis=-1, keepdims=True))
    return centred * lax.rsqrt(lax.optimization_barrier(jnp.mean(centred * centred, axis=-1, keepdims=True)) + 1e-06)

def forward(params, tokens, condition):
    w_ada, b_ada, w_qkv, b_qv, w_o, b_o, w_1, b_1, w_2, b_2 = params
    count = tokens.shape[0]
    cs = low(jax.nn.silu(condition))
    ada = low_back(matmul(cs, w_ada) + b_ada)
    shift1, scale1, gate1, shift2, scale2, gate2 = jnp.split(ada, 6, axis=-1)
    m1 = low(layer_norm(tokens) * (1.0 + scale1[:, None]) + shift1[:, None])
    qkv = matmul(m1, w_qkv)
    query = low_back(low(qkv[..., :D] + b_qv[:D])).reshape(count, SEQ, HEADS, HD)
    key = low_back(low(qkv[..., D:2 * D])).reshape(count, SEQ, HEADS, HD)
    value = low_back(low(qkv[..., 2 * D:] + b_qv[D:])).reshape(count, SEQ, HEADS, HD)
    scores = low_back(jnp.einsum('gqhd,gkhd->ghqk', query, key, precision=lax.Precision.HIGHEST) * 0.125)
    probs = low(jax.nn.softmax(scores, axis=-1))
    attended = jnp.einsum('ghqk,gkhd->gqhd', probs, value, precision=lax.Precision.HIGHEST).reshape(count, SEQ, D)
    attended = low_back(low(attended))
    branch = low_back(matmul(attended, w_o) + b_o)
    x1 = tokens + gate1[:, None] * branch
    m2 = low(layer_norm(x1) * (1.0 + scale2[:, None]) + shift2[:, None])
    hidden = low_back(matmul(m2, w_1) + b_1)
    gelu_out = low(jax.nn.gelu(hidden, approximate=True))
    ffn = low_back(matmul(gelu_out, w_2) + b_2)
    return x1 + gate2[:, None] * ffn

def reference(latent_tokens, cond, w_ada, b_ada, w_qkv, b_qv, w_o, b_o, w_1, b_1, w_2, b_2, grad_out):
    params = tuple((w.astype(jnp.float32) for w in (w_ada, b_ada, w_qkv, b_qv, w_o, b_o, w_1, b_1, w_2, b_2)))
    steps_count = LAT // LAT_DEV
    tokens = latent_tokens.astype(jnp.float32).reshape(steps_count, LAT_DEV, SEQ, D)
    condition = cond.astype(jnp.float32).reshape(steps_count, LAT_DEV, D)
    cotangent = grad_out.astype(jnp.float32).reshape(steps_count, LAT_DEV, SEQ, D)

    def step(totals, items):
        tok_group, cond_group, cot_group = items
        result, vjp_fn = jax.vjp(forward, params, tok_group, cond_group)
        grads, grad_tok, grad_cnd = vjp_fn(cot_group)
        totals = tuple((a + b for a, b in zip(totals, grads)))
        return (totals, (result.astype(jnp.bfloat16), grad_tok, grad_cnd))
    zeros = tuple((jnp.zeros(w.shape, jnp.float32) for w in params))
    totals, (outputs, grad_tok, grad_cnd) = lax.scan(step, zeros, (tokens, condition, cotangent))
    return (outputs.reshape(LAT, SEQ, D), grad_tok.reshape(LAT, SEQ, D), grad_cnd.reshape(LAT, D), totals[0], totals[1], totals[2], totals[3], totals[4], totals[5], totals[6], totals[7], totals[8], totals[9])
```

```python
import functools
import math

import jax
import jax.numpy as jnp
from jax import lax
from jax.experimental import pallas as pl
from jax.experimental.pallas import tpu as pltpu
from jax.sharding import PartitionSpec as P

HEADS = 6
F32 = jnp.float32
BF16 = jnp.bfloat16
EPS = 1e-06
GELU_C = math.sqrt(2.0 / math.pi)
GELU_A = 0.044715
VMEM_LIMIT = 56 * 1024 * 1024


def nn(a, b):
    return lax.dot_general(a, b, (((1,), (0,)), ((), ())), preferred_element_type=F32)


def nt(a, b):
    return lax.dot_general(a, b, (((1,), (1,)), ((), ())), preferred_element_type=F32)


def tn(a, b):
    return lax.dot_general(a, b, (((0,), (0,)), ((), ())), preferred_element_type=F32)


def norm_parts(x):
    centred = x - jnp.mean(x, axis=-1, keepdims=True)
    rstd = lax.rsqrt(jnp.mean(centred * centred, axis=-1, keepdims=True) + EPS)
    return centred * rstd, rstd


def norm_back(normed, rstd, grad):
    inner = jnp.mean(grad, axis=-1, keepdims=True)
    along = jnp.mean(grad * normed, axis=-1, keepdims=True)
    return rstd * (grad - inner - normed * along)


def piece_copies(mine, pieces, whole, sems):
    rows = pieces[0].shape[0]
    return [
        pltpu.make_async_copy(
            piece,
            whole.at[pl.ds(pl.multiple_of(jnp.bitwise_xor(mine, k) * rows, 32), rows)],
            sems.at[k],
        )
        for k, piece in enumerate(pieces)
    ]


def half_mask(shape, half):
    lane = lax.broadcasted_iota(jnp.int32, shape, len(shape) - 1)
    return (lane < shape[-1] // 2) if half == 0 else (lane >= shape[-1] // 2)


def attn_fwd(info, tok, cond, b_ada, b_qkv, *refs, per):
    wa, wq = refs[0:4], refs[4:8]
    ada_o, m1_o, qkv_o, p_o, att_o = refs[8:13]
    wa_s, wq_s, sem_a, sem_q = refs[13:]
    step = pl.program_id(0)
    width = tok.shape[-1]

    @pl.when(step == 0)
    def _():
        ca = piece_copies(info[0], wa, wa_s, sem_a)
        cq = piece_copies(info[0], wq, wq_s, sem_q)
        for copy in ca + cq:
            copy.start()
        c = cond[...].astype(F32)
        cs = (c / (1.0 + jnp.exp(-c))).astype(BF16)
        for copy in ca:
            copy.wait()
        ada_o[...] = nn(cs, wa_s[...]) + b_ada[...]
        for copy in cq:
            copy.wait()

    for l in range(per):
        row = pl.ds(step * per + l, 1)
        shift = ada_o[row, 0:width]
        scale = ada_o[row, width : 2 * width]
        n1, _ = norm_parts(tok[l].astype(F32))
        m1 = (n1 * (1.0 + scale) + shift).astype(BF16)
        m1_o[l] = m1
        qkv = (nn(m1, wq_s[...]) + b_qkv[...]).astype(BF16)
        qkv_o[l] = qkv
        for j in range(HEADS // 2):
            q = qkv[:, 128 * j : 128 * j + 128]
            k = qkv[:, width + 128 * j : width + 128 * j + 128]
            v = qkv[:, 2 * width + 128 * j : 2 * width + 128 * j + 128]
            both = []
            for h in range(2):
                km = jnp.where(half_mask(k.shape, h), k, jnp.zeros_like(k))
                s = nt(km, q)
                top = jnp.max(s, axis=0, keepdims=True)
                e = jnp.exp((s - top) * 0.125)
                total = jnp.sum(e, axis=0, keepdims=True)
                p = (e * (1.0 / total)).astype(BF16)
                p_o[l, 2 * j + h] = p
                both.append(tn(p, v))
            att = jnp.where(half_mask(both[0].shape, 0), both[0], both[1])
            att_o[l, :, 128 * j : 128 * j + 128] = att.astype(BF16)


def ffn_both(info, tok, att_i, dy_i, ada, cond, b_o, b_1, b_2, *refs, per, chunk):
    wo, w1, w2 = refs[0:4], refs[4:8], refs[8:12]
    out_o, dx1_o, datt_o, early_o, keep_a, send_a, keep_b, send_b = refs[12:20]
    wo_s, w1_s, w2_s, go_s, g1_s, g2_s, small_s, gb_s, sem_o, sem_1, sem_2 = refs[20:]
    step = pl.program_id(0)
    length, width = tok.shape[1:]
    hidden = w1_s.shape[1]

    @pl.when(step == 0)
    def _():
        copies = (
            piece_copies(info[0], wo, wo_s, sem_o)
            + piece_copies(info[0], w1, w1_s, sem_1)
            + piece_copies(info[0], w2, w2_s, sem_2)
        )
        for copy in copies:
            copy.start()
        go_s[...] = jnp.zeros_like(go_s)
        g1_s[...] = jnp.zeros_like(g1_s)
        g2_s[...] = jnp.zeros_like(g2_s)
        gb_s[...] = jnp.zeros_like(gb_s)
        c = cond[...].astype(F32)
        small_s[:, 4 * width : 5 * width] = c / (1.0 + jnp.exp(-c))
        for copy in copies:
            copy.wait()

    def rows_of(at):
        return jnp.stack(
            [ada[pl.ds(step * per + l, 1), at * width : (at + 1) * width] for l in range(per)]
        )

    def flat(v):
        return v.reshape(per * length, v.shape[-1])

    def deep(v):
        return v.reshape(per, length, v.shape[-1])

    gate1, shift2, scale2, gate2 = rows_of(2), rows_of(3), rows_of(4), rows_of(5)
    att = flat(att_i[...])
    branch = deep(nn(att, wo_s[...]) + b_o[...])
    x1 = tok[...].astype(F32) + gate1 * branch
    n2, rstd2 = norm_parts(x1)
    m2 = flat((n2 * (1.0 + scale2) + shift2).astype(BF16))
    dy = dy_i[...].astype(F32)
    df = flat((dy * gate2).astype(BF16))
    df_t = df.T
    m2_t = m2.T
    ffn = None
    dm2 = None
    for j in range(hidden // chunk):
        cols = slice(j * chunk, (j + 1) * chunk)
        h = nn(m2, w1_s[:, cols]) + b_1[:, cols]
        hh = h * h
        t = jnp.tanh(h * (GELU_C + (GELU_C * GELU_A) * hh))
        half_t = 0.5 + 0.5 * t
        g = (h * half_t).astype(BF16)
        slope = half_t + (0.5 * h) * (1.0 - t * t) * (GELU_C + (3.0 * GELU_C * GELU_A) * hh)
        part = nn(g, w2_s[cols, :])
        ffn = part if ffn is None else ffn + part
        g2_s[:, cols] += nn(df_t, g)
        dh32 = nt(df, w2_s[cols, :]) * slope
        dh = dh32.astype(BF16)
        gb_s[0:1, cols] += jnp.sum(dh.astype(F32), axis=0, keepdims=True)
        g1_s[:, cols] += nn(m2_t, dh)
        part = nt(dh, w1_s[:, cols])
        dm2 = part if dm2 is None else dm2 + part
    ffn = deep(ffn + b_2[...])
    dm2 = deep(dm2)
    out_o[...] = (x1 + gate2 * ffn).astype(BF16)
    gb_s[1:2, width : 2 * width] += jnp.sum(df.astype(F32), axis=0, keepdims=True)
    d_gate2 = jnp.sum(dy * ffn, axis=1)
    d_scale2 = jnp.sum(dm2 * n2, axis=1)
    d_shift2 = jnp.sum(dm2, axis=1)
    dx1 = dy + norm_back(n2, rstd2, dm2 * (1.0 + scale2))
    dx1_o[...] = dx1
    do = flat((dx1 * gate1).astype(BF16))
    d_gate1 = jnp.sum(dx1 * branch, axis=1)
    for l in range(per):
        row = pl.ds(step * per + l, 1)
        small_s[row, 0:width] = d_gate1[l : l + 1]
        small_s[row, width : 2 * width] = d_shift2[l : l + 1]
        small_s[row, 2 * width : 3 * width] = d_scale2[l : l + 1]
        small_s[row, 3 * width : 4 * width] = d_gate2[l : l + 1]
    gb_s[1:2, 0:width] += jnp.sum(do.astype(F32), axis=0, keepdims=True)
    go_s[...] += tn(att, do)
    datt_o[...] = deep(nt(do, wo_s[...]).astype(BF16))

    @pl.when(step == pl.num_programs(0) - 1)
    def _():
        early_o[0:8, :] = small_s[...].astype(BF16)
        early_o[8:16, :] = gb_s[...].astype(BF16)
        core = jnp.bitwise_and(info[0], 1)
        rows = width // 4
        g2_t = w2_s.shape[0] // 4
        for y in range(2):
            for which, (ra, rb) in enumerate(((keep_a, keep_b), (send_a, send_b))):
                shard = 2 * y + jnp.bitwise_xor(core, which)
                take = pl.ds(pl.multiple_of(shard * rows, 8), rows)
                ra[y, :, 0:width] = go_s[take, :].astype(BF16)
                ra[y, :, width : width + hidden] = g1_s[take, :].astype(BF16)
                at = pl.ds(pl.multiple_of(shard * g2_t, 128), g2_t)
                rb[y] = g2_s[:, at].astype(BF16)


def attn_bwd(info, tok, m1_i, qkv_i, p_i, datt_i, dx1_i, ada, cond, early, *refs, per):
    wa, wq = refs[0:4], refs[4:8]
    gtok_o, gcond_o, late_o, keep_o, send_o = refs[8:13]
    wa_s, wq_s, g_s, small_s, gb_s, sem_a, sem_q = refs[13:]
    step = pl.program_id(0)
    length, width = tok.shape[1:]

    @pl.when(step == 0)
    def _():
        ca = piece_copies(info[0], wa, wa_s, sem_a)
        cq = piece_copies(info[0], wq, wq_s, sem_q)
        for copy in cq + ca:
            copy.start()
        g_s[...] = jnp.zeros_like(g_s)
        gb_s[...] = jnp.zeros_like(gb_s)
        for copy in cq + ca:
            copy.wait()

    for l in range(per):
        row = pl.ds(step * per + l, 1)
        scale = ada[row, width : 2 * width]
        n1, rstd1 = norm_parts(tok[l].astype(F32))
        m1 = m1_i[l]
        grads = [[], [], []]
        for j in range(HEADS // 2):
            q = qkv_i[l, :, 128 * j : 128 * j + 128]
            k = qkv_i[l, :, width + 128 * j : width + 128 * j + 128]
            v = qkv_i[l, :, 2 * width + 128 * j : 2 * width + 128 * j + 128]
            datt = datt_i[l, :, 128 * j : 128 * j + 128]
            both = [[], [], []]
            for h in range(2):
                p = p_i[l, 2 * j + h]
                vm = jnp.where(half_mask(v.shape, h), v, jnp.zeros_like(v))
                both[2].append(nn(p, datt))
                dp = nt(vm, datt)
                p32 = p.astype(F32)
                pd = p32 * dp
                ds = (pd - p32 * jnp.sum(pd, axis=0, keepdims=True)).astype(BF16)
                both[1].append(nn(ds, q) * 0.125)
                both[0].append(tn(ds, k) * 0.125)
            for at in range(3):
                pair = both[at]
                grads[at].append(
                    jnp.where(half_mask(pair[0].shape, 0), pair[0], pair[1]).astype(BF16)
                )
        dqkv = jnp.concatenate(grads[0] + grads[1] + grads[2], axis=-1)
        g_s[...] += nn(m1.T, dqkv)
        sums = jnp.sum(dqkv.astype(F32), axis=0, keepdims=True)
        gb_s[0:1, 0:width] += sums[:, 0:width]
        gb_s[0:1, width : 2 * width] += sums[:, 2 * width : 3 * width]
        dm1 = nt(dqkv, wq_s[...])
        small_s[row, 0:width] = jnp.sum(dm1, axis=0, keepdims=True)
        small_s[row, width : 2 * width] = jnp.sum(dm1 * n1, axis=0, keepdims=True)
        gtok_o[l] = dx1_i[l] + norm_back(n1, rstd1, dm1 * (1.0 + scale))

    @pl.when(step == pl.num_programs(0) - 1)
    def _():
        late = small_s[...].astype(BF16)
        late_o[0:8, :] = late
        late_o[8:16, :] = gb_s[...].astype(BF16)
        dada = jnp.concatenate([late, early[0:8, 0 : 4 * width]], axis=-1)
        gcs = nt(dada, wa_s[...])
        c = cond[...].astype(F32)
        sig = 1.0 / (1.0 + jnp.exp(-c))
        gcond_o[...] = gcs * (sig * (1.0 + c * (1.0 - sig)))
        core = jnp.bitwise_and(info[0], 1)
        rows = width // 4
        for y in range(2):
            for which, ref in enumerate((keep_o, send_o)):
                shard = 2 * y + jnp.bitwise_xor(core, which)
                take = pl.ds(pl.multiple_of(shard * rows, 8), rows)
                ref[y] = g_s[take, :].astype(BF16)


def add_split(info, *refs):
    count = len(refs) // 6
    for n in range(count):
        keep, got = refs[n], refs[count + n]
        half = keep.shape[1] // 2
        for k in range(4):
            out = refs[2 * count + 4 * n + k]
            y = jnp.bitwise_xor(info[1], k >> 1)
            x = jnp.bitwise_xor(info[2], k & 1)
            take = pl.ds(pl.multiple_of(x * half, 16), half)
            out[...] = (keep[y, take, :].astype(F32) + got[y, take, :].astype(F32)).astype(BF16)


def tree_sum(values):
    while len(values) > 1:
        values = [values[2 * i] + values[2 * i + 1] for i in range(len(values) // 2)]
    return values[0]


def full(shape):
    return pl.BlockSpec(shape, lambda *_: (0,) * len(shape))


def call(body, info, operands, specs, outs, out_specs, scratch, grid, flops, traffic, exps=0):
    return pl.pallas_call(
        body,
        out_shape=outs,
        grid_spec=pltpu.PrefetchScalarGridSpec(
            num_scalar_prefetch=1,
            grid=grid,
            in_specs=specs,
            out_specs=out_specs,
            scratch_shapes=scratch,
        ),
        compiler_params=pltpu.CompilerParams(
            dimension_semantics=("arbitrary",) * len(grid), vmem_limit_bytes=VMEM_LIMIT
        ),
        cost_estimate=pl.CostEstimate(flops=flops, bytes_accessed=traffic, transcendentals=exps),
    )(info, *operands)


def on_device(
    latent_tokens, cond, w_ada, b_ada, w_qkv, b_qv, w_o, b_o, w_1, b_1, w_2, b_2, grad_out
):
    count, length, width = latent_tokens.shape
    hidden = w_1.shape[1]
    reps = lax.axis_size("rep")
    shards = lax.axis_size("shard")
    s = lax.axis_index("shard")
    r = lax.axis_index("rep")
    info = jnp.stack([s, s >> 1, r & 1, r >> 1]).astype(jnp.int32)

    def swap(v, shard_bits=0, rep_bits=0):
        pairs = [
            (i * shards + j, (i ^ rep_bits) * shards + (j ^ shard_bits))
            for i in range(reps)
            for j in range(shards)
        ]
        return lax.ppermute(v, ("rep", "shard"), pairs)

    def gather(v):
        far = swap(v, 2)
        return (v, swap(v, 1), far, swap(far, 1))

    def gather_row(v):
        a = gather(v.astype(BF16))
        core = (s & 1) == 0
        near = jnp.where(core, jnp.stack([a[0], a[1]]), jnp.stack([a[1], a[0]]))
        far = jnp.where(core, jnp.stack([a[2], a[3]]), jnp.stack([a[3], a[2]]))
        low = (s >> 1) == 0
        both = jnp.where(low, jnp.stack([near, far]), jnp.stack([far, near]))
        return both.reshape(1, -1).astype(F32)

    biases = gather_row(jnp.concatenate([b_ada, b_qv, b_o, b_1, b_2]))
    cuts, bias_rows, at = [b_ada, b_qv, b_o, b_1, b_2], [], 0
    table = biases.reshape(shards, -1)
    for b in cuts:
        bias_rows.append(table[:, at : at + b.shape[0]].reshape(1, -1))
        at += b.shape[0]
    f_bada, f_bqv, f_bo, f_b1, f_b2 = bias_rows
    b_qkv = jnp.concatenate(
        [f_bqv[:, :width], jnp.zeros((1, width), F32), f_bqv[:, width:]], axis=-1
    )
    p_ada, p_qkv = gather(w_ada), gather(w_qkv)
    w_o, w_1, w_2, _ = lax.optimization_barrier((w_o, w_1, w_2, p_qkv[2]))
    p_o, p_1, p_2 = gather(w_o), gather(w_1), gather(w_2)

    anyspec = pl.BlockSpec(memory_space=pl.ANY)
    dma4 = pltpu.SemaphoreType.DMA((4,))
    tokens = count * length

    per = 1
    lat = lambda *tail: pl.BlockSpec((per,) + tail, lambda i, _: (i,) + (0,) * len(tail))
    ada, m1, qkv, probs, att = call(
        functools.partial(attn_fwd, per=per),
        info,
        (latent_tokens, cond, f_bada, b_qkv) + p_ada + p_qkv,
        [lat(length, width), full(cond.shape), full(f_bada.shape), full(b_qkv.shape)]
        + [anyspec] * 8,
        [
            jax.ShapeDtypeStruct((count, 6 * width), F32),
            jax.ShapeDtypeStruct((count, length, width), BF16),
            jax.ShapeDtypeStruct((count, length, 3 * width), BF16),
            jax.ShapeDtypeStruct((count, HEADS, length, length), BF16),
            jax.ShapeDtypeStruct((count, length, width), BF16),
        ],
        [
            full((count, 6 * width)),
            lat(length, width),
            lat(length, 3 * width),
            lat(HEADS, length, length),
            lat(length, width),
        ],
        [
            pltpu.VMEM((width, 6 * width), BF16),
            pltpu.VMEM((width, 3 * width), BF16),
            dma4,
            dma4,
        ],
        (count // per,),
        8 * tokens * width * width + 8 * tokens * length * width,
        20 * tokens * width,
        tokens * length * HEADS,
    )

    per2 = 2 if count % 2 == 0 else 1
    lat2 = lambda *tail: pl.BlockSpec((per2,) + tail, lambda i, _: (i,) + (0,) * len(tail))
    quarter = width // 4
    block_out, dx1, datt, early, keep_a, send_a, keep_b, send_b = call(
        functools.partial(ffn_both, per=per2, chunk=512),
        info,
        (latent_tokens, att, grad_out, ada, cond, f_bo, f_b1, f_b2) + p_o + p_1 + p_2,
        [lat2(length, width)] * 3
        + [full(ada.shape), full(cond.shape), full(f_bo.shape), full(f_b1.shape), full(f_b2.shape)]
        + [anyspec] * 12,
        [
            jax.ShapeDtypeStruct((count, length, width), BF16),
            jax.ShapeDtypeStruct((count, length, width), F32),
            jax.ShapeDtypeStruct((count, length, width), BF16),
            jax.ShapeDtypeStruct((16, 5 * width), BF16),
        ]
        + [jax.ShapeDtypeStruct((2, quarter, width + hidden), BF16)] * 2
        + [jax.ShapeDtypeStruct((2, width, hidden // 4), BF16)] * 2,
        [lat2(length, width)] * 3
        + [full((16, 5 * width))]
        + [full((2, quarter, width + hidden))] * 2
        + [full((2, width, hidden // 4))] * 2,
        [
            pltpu.VMEM((width, width), BF16),
            pltpu.VMEM((width, hidden), BF16),
            pltpu.VMEM((hidden, width), BF16),
            pltpu.VMEM((width, width), F32),
            pltpu.VMEM((width, hidden), F32),
            pltpu.VMEM((width, hidden), F32),
            pltpu.VMEM((8, 5 * width), F32),
            pltpu.VMEM((8, 5 * width), F32),
            dma4,
            dma4,
            dma4,
        ],
        (count // per2,),
        12 * tokens * width * hidden + 6 * tokens * width * width,
        14 * tokens * width,
        tokens * hidden,
    )

    grad_tokens, grad_cond, late, keep_q, send_q = call(
        functools.partial(attn_bwd, per=per),
        info,
        (latent_tokens, m1, qkv, probs, datt, dx1, ada, cond, early) + p_ada + p_qkv,
        [
            lat(length, width),
            lat(length, width),
            lat(length, 3 * width),
            lat(HEADS, length, length),
            lat(length, width),
            lat(length, width),
            full(ada.shape),
            full(cond.shape),
            full(early.shape),
        ]
        + [anyspec] * 8,
        [
            jax.ShapeDtypeStruct((count, length, width), F32),
            jax.ShapeDtypeStruct((count, width), F32),
            jax.ShapeDtypeStruct((16, 2 * width), BF16),
        ]
        + [jax.ShapeDtypeStruct((2, quarter, 3 * width), BF16)] * 2,
        [lat(length, width), full((count, width)), full((16, 2 * width))]
        + [full((2, quarter, 3 * width))] * 2,
        [
            pltpu.VMEM((width, 6 * width), BF16),
            pltpu.VMEM((width, 3 * width), BF16),
            pltpu.VMEM((width, 3 * width), F32),
            pltpu.VMEM((8, 2 * width), F32),
            pltpu.VMEM((8, 2 * width), F32),
            dma4,
            dma4,
        ],
        (count // per,),
        12 * tokens * width * width + 16 * tokens * length * width,
        30 * tokens * width,
        0,
    )

    def reduce(keeps, sends):
        got = [swap(v, 1) for v in sends]
        outs = []
        for v in keeps:
            outs += [jax.ShapeDtypeStruct((v.shape[1] // 2, v.shape[2]), BF16)] * 4
        parts = call(
            add_split,
            info,
            tuple(keeps) + tuple(got),
            [full(v.shape) for v in list(keeps) + got],
            outs,
            [full(o.shape) for o in outs],
            [],
            (1,),
            0,
            sum(4 * v.size for v in keeps),
        )
        done = []
        for n in range(len(keeps)):
            own, to_x, to_y, to_d = parts[4 * n : 4 * n + 4]
            got4 = [own, swap(to_x, 0, 1), swap(to_y, 2, 0), swap(to_d, 2, 1)]
            total = tree_sum([v.astype(F32) for v in got4]).astype(BF16)
            ring = [total] + [swap(total, 0, 2 * k) for k in range(1, reps // 2)]
            total = tree_sum([v.astype(F32) for v in ring]).astype(BF16)
            other = swap(total, 0, 1)
            first = (r & 1) == 0
            whole = jnp.where(
                first, jnp.stack([total, other]), jnp.stack([other, total])
            ).astype(F32)
            done.append(whole.reshape(-1, total.shape[1]))
        return done

    def gather_all(v):
        zs = jnp.stack([v] + [swap(v, 0, 2 * k) for k in range(1, reps // 2)])
        four = jnp.stack([zs, swap(zs, 0, 1), swap(zs, 2, 0), swap(zs, 2, 1)])
        return four, swap(four, 1)

    def ada_grads(early4, late4):
        n_z = reps // 2
        n_dev = reps * shards

        def body(info, e0, e1, l0, l1, gw_o, gb_o, bias_o, e_s, l_s):
            for kc in range(2):
                e_ref, l_ref = ((e0, l0), (e1, l1))[kc]
                for kp in range(4):
                    for kz in range(n_z):
                        rep_at = jnp.bitwise_xor(info[3], kz) * 2 + jnp.bitwise_xor(
                            info[2], kp & 1
                        )
                        at = rep_at * 4 + jnp.bitwise_xor(info[0], 2 * (kp >> 1) + kc)
                        e_s[at] = e_ref[kp, kz].astype(F32)
                        l_s[at] = l_ref[kp, kz].astype(F32)
            cs = e_s[:, 0:8, 4 * width : 5 * width].reshape(8 * n_dev, width)
            cs_t = cs.T.astype(BF16)
            early_d = e_s[:, 0:8, 0 : 4 * width].reshape(8 * n_dev, 4 * width)
            late_d = l_s[:, 0:8, :].reshape(8 * n_dev, 2 * width)
            first = nn(cs_t, late_d.astype(BF16))
            second = nn(cs_t, early_d.astype(BF16))
            rows = width // 4
            for j in range(4):

                @pl.when(info[0] == j)
                def _():
                    gw_o[:, 0 : 2 * width] = first[j * rows : (j + 1) * rows]
                    gw_o[:, 2 * width : 6 * width] = second[j * rows : (j + 1) * rows]

            gb_o[:, 0 : 2 * width] = jnp.sum(late_d, axis=0, keepdims=True)
            gb_o[:, 2 * width : 6 * width] = jnp.sum(early_d, axis=0, keepdims=True)
            e_b = jnp.sum(e_s[:, 8:16, :], axis=0)
            l_b = jnp.sum(l_s[:, 8:16, :], axis=0)
            bias_o[:, 0 : 2 * width] = l_b[0:1]
            bias_o[:, 2 * width : 4 * width] = e_b[1:2, 0 : 2 * width]
            bias_o[:, 4 * width : 4 * width + hidden] = e_b[0:1, 0:hidden]

        ins = early4 + late4
        outs = [
            jax.ShapeDtypeStruct((quarter, 6 * width), F32),
            jax.ShapeDtypeStruct((1, 6 * width), F32),
            jax.ShapeDtypeStruct((1, 4 * width + hidden), F32),
        ]
        return call(
            body,
            info,
            ins,
            [full(v.shape) for v in ins],
            outs,
            [full(o.shape) for o in outs],
            [
                pltpu.VMEM((n_dev, 16, 5 * width), F32),
                pltpu.VMEM((n_dev, 16, 2 * width), F32),
            ],
            (1,),
            2 * 8 * n_dev * width * 6 * width,
            4 * n_dev * 16 * 7 * width,
        )

    gw_o1, gw_2t = reduce([keep_a, keep_b], [send_a, send_b])
    early4 = gather_all(early)
    (gw_qkv,) = reduce([keep_q], [send_q])
    late4 = gather_all(late)
    gw_ada, gb_ada, gb_rest = ada_grads(early4, late4)

    def mine(row, total):
        part = total // shards
        return lax.dynamic_slice(row.reshape(-1), (s * part,), (part,))

    return (
        block_out,
        grad_tokens,
        grad_cond,
        gw_ada,
        mine(gb_ada, 6 * width),
        gw_qkv,
        mine(gb_rest[:, 0 : 2 * width], 2 * width),
        gw_o1[:, 0:width],
        mine(gb_rest[:, 2 * width : 3 * width], width),
        gw_o1[:, width:],
        mine(gb_rest[:, 4 * width :], hidden),
        gw_2t.T,
        mine(gb_rest[:, 3 * width : 4 * width], width),
    )


def solution(mesh):
    lead = P(("rep", "shard"))
    part = P("shard")
    return jax.shard_map(
        on_device,
        mesh=mesh,
        in_specs=(lead, lead) + (part,) * 10 + (lead,),
        out_specs=(lead,) * 3 + (part,) * 10,
        check_vma=False,
    )
```

```python
import functools
import math

import jax
import jax.numpy as jnp
from jax import lax
from jax.experimental import pallas as pl
from jax.experimental.pallas import tpu as pltpu
from jax.sharding import PartitionSpec as P

HEADS = 6
F32 = jnp.float32
BF16 = jnp.bfloat16
EPS = 1e-06
GELU_C = math.sqrt(2.0 / math.pi)
GELU_A = 0.044715


def nn(a, b):
    return lax.dot_general(a, b, (((1,), (0,)), ((), ())), preferred_element_type=F32)


def nt(a, b):
    return lax.dot_general(a, b, (((1,), (1,)), ((), ())), preferred_element_type=F32)


def tn(a, b):
    return lax.dot_general(a, b, (((0,), (0,)), ((), ())), preferred_element_type=F32)


def norm_parts(x):
    centred = x - jnp.mean(x, axis=-1, keepdims=True)
    rstd = lax.rsqrt(jnp.mean(centred * centred, axis=-1, keepdims=True) + EPS)
    return centred * rstd, rstd


def norm_back(normed, rstd, grad):
    inner = jnp.mean(grad, axis=-1, keepdims=True)
    along = jnp.mean(grad * normed, axis=-1, keepdims=True)
    return rstd * (grad - inner - normed * along)


def piece_copies(mine, pieces, whole, sems):
    rows = pieces[0].shape[0]
    return [
        pltpu.make_async_copy(
            piece,
            whole.at[pl.ds(pl.multiple_of(jnp.bitwise_xor(mine, k) * rows, 32), rows)],
            sems.at[k],
        )
        for k, piece in enumerate(pieces)
    ]


def half_mask(shape, half):
    lane = lax.broadcasted_iota(jnp.int32, shape, len(shape) - 1)
    return (lane < shape[-1] // 2) if half == 0 else (lane >= shape[-1] // 2)


def condition(info, cond, b_ada, b_qv, b_o, b_1, b_2, *refs):
    cuts, share, packed = refs[0:4], refs[4], refs[5]
    c = cond[...].astype(F32)
    cs = c / (1.0 + jnp.exp(-c))
    cut = cs.shape[1] // 4
    for k, ref in enumerate(cuts):
        mine = jnp.bitwise_xor(info[0], k)
        ref[...] = sum(
            jnp.where(mine == j, cs[:, j * cut : (j + 1) * cut], 0.0) for j in range(4)
        ).astype(BF16)
    share[...] = jnp.zeros_like(share)
    n = b_ada.shape[0]
    row = b_ada[...].astype(F32).reshape(1, n)
    for j in range(4):

        @pl.when(info[0] == j)
        def _():
            share[:, j * n : (j + 1) * n] = row

    packed[...] = jnp.zeros_like(packed)
    for i, b in enumerate((b_qv, b_o, b_1, b_2)):
        packed[i : i + 1, 0 : b.shape[0]] = b[...].astype(F32).reshape(1, b.shape[0])


def ada_parts(info, c0, c1, c2, c3, w_ada, share, packed, *outs):
    for cut, out in zip((c0, c1, c2, c3), outs):
        n = w_ada.shape[1]
        out[:, 0:n] = nn(cut[...], w_ada[...]) + share[...]
        out[:, n:] = packed[...]


def bias_row(table, at, n):
    return jnp.concatenate([table[i, at : at + 1, 0:n] for i in range(4)], axis=1)


def attn_fwd(info, tok, *refs, per):
    parts, wq = refs[0:4], refs[4:8]
    m1_o, qkv_o, p_o, att_o, ada, table = refs[8:14]
    wq_s, bias_s, sem_q = refs[14:]
    step = pl.program_id(0)
    width = tok.shape[-1]

    @pl.when(step == 0)
    def _():
        cq = piece_copies(info[0], wq, wq_s, sem_q)
        for copy in cq:
            copy.start()
        ada[...] = sum(v[:, 0 : 6 * width] for v in parts)
        for k in range(4):
            table[jnp.bitwise_xor(info[0], k)] = parts[k][:, 6 * width :]
        row_qv = bias_row(table, 0, width // 2)
        bias_s[:, 0:width] = row_qv[:, 0:width]
        bias_s[:, width : 2 * width] = jnp.zeros((1, width), F32)
        bias_s[:, 2 * width : 3 * width] = row_qv[:, width : 2 * width]
        for copy in cq:
            copy.wait()

    qkvs, ss, ps, atts = {}, {}, {}, {}
    part = lambda l, at, j: qkvs[l][:, at + 128 * j : at + 128 * j + 128]

    def stage_q(l):
        row = pl.ds(step * per + l, 1)
        shift = ada[row, 0:width]
        scale = ada[row, width : 2 * width]
        n1, _ = norm_parts(tok[l].astype(F32))
        m1 = (n1 * (1.0 + scale) + shift).astype(BF16)
        m1_o[l] = m1
        qkvs[l] = (nn(m1, wq_s[...]) + bias_s[...]).astype(BF16)
        qkv_o[l] = qkvs[l]

    def stage_a(u):
        l, t = divmod(u, HEADS)
        j, h = t // 2, t % 2
        k = part(l, width, j)
        ss[u] = nt(jnp.where(half_mask(k.shape, h), k, jnp.zeros_like(k)), part(l, 0, j))

    def stage_b(u):
        l, t = divmod(u, HEADS)
        s = ss[u]
        top = jnp.max(s, axis=0, keepdims=True)
        e = jnp.exp((s - top) * 0.125)
        total = jnp.sum(e, axis=0, keepdims=True)
        ps[u] = (e * (1.0 / total)).astype(BF16)
        p_o[l, t] = ps[u]

    def stage_c(u):
        l, t = divmod(u, HEADS)
        j = t // 2
        atts[u] = tn(ps[u], part(l, 2 * width, j))
        if t % 2:
            att = jnp.where(half_mask(atts[u].shape, 0), atts[u - 1], atts[u])
            att_o[l, :, 128 * j : 128 * j + 128] = att.astype(BF16)

    n = HEADS * per
    stage_q(0)
    for u in range(n + 2):
        if u < n:
            stage_a(u)
        if u % HEADS == 1 and u // HEADS + 1 < per:
            stage_q(u // HEADS + 1)
        if 0 <= u - 1 < n:
            stage_b(u - 1)
        if 0 <= u - 2 < n:
            stage_c(u - 2)


def ffn_both(info, tok, att_i, dy_i, ada, cond, table, *refs, per, chunk):
    wo, w1, w2 = refs[0:4], refs[4:8], refs[8:12]
    out_o, dx1_o, datt_o, early_o, keep_o, send_o = refs[12:18]
    wo_s, w1_s, w2_s, go_s, g1_s, g2_s, small_s, gb_s, bo_s, b1_s, b2_s, sem_o, sem_1, sem_2 = refs[18:]
    step = pl.program_id(0)
    length, width = tok.shape[1:]
    hidden = w1_s.shape[1]

    @pl.when(step == 0)
    def _():
        copies = (
            piece_copies(info[0], wo, wo_s, sem_o)
            + piece_copies(info[0], w1, w1_s, sem_1)
            + piece_copies(info[0], w2, w2_s, sem_2)
        )
        for copy in copies:
            copy.start()
        go_s[...] = jnp.zeros_like(go_s)
        g1_s[...] = jnp.zeros_like(g1_s)
        g2_s[...] = jnp.zeros_like(g2_s)
        gb_s[...] = jnp.zeros_like(gb_s)
        bo_s[...] = bias_row(table, 1, width // 4)
        b1_s[...] = bias_row(table, 2, hidden // 4)
        b2_s[...] = bias_row(table, 3, width // 4)
        c = cond[...].astype(F32)
        small_s[:, 4 * width : 5 * width] = c / (1.0 + jnp.exp(-c))
        for copy in copies:
            copy.wait()

    def rows_of(at):
        return jnp.stack(
            [ada[pl.ds(step * per + l, 1), at * width : (at + 1) * width] for l in range(per)]
        )

    def flat(v):
        return v.reshape(per * length, v.shape[-1])

    def deep(v):
        return v.reshape(per, length, v.shape[-1])

    gate1, shift2, scale2, gate2 = rows_of(2), rows_of(3), rows_of(4), rows_of(5)
    att = flat(att_i[...])
    branch = deep(nn(att, wo_s[...]) + bo_s[...])
    x1 = tok[...].astype(F32) + gate1 * branch
    n2, rstd2 = norm_parts(x1)
    m2 = flat((n2 * (1.0 + scale2) + shift2).astype(BF16))
    dy = dy_i[...].astype(F32)
    df = flat((dy * gate2).astype(BF16))
    df_t = df.T
    m2_t = m2.T
    ffn = None
    dm2 = None
    for j in range(hidden // chunk):
        cols = slice(j * chunk, (j + 1) * chunk)
        h = nn(m2, w1_s[:, cols]) + b1_s[:, cols]
        hh = h * h
        t = jnp.tanh(h * (GELU_C + (GELU_C * GELU_A) * hh))
        half_t = 0.5 + 0.5 * t
        g = (h * half_t).astype(BF16)
        slope = half_t + (0.5 * h) * (1.0 - t * t) * (GELU_C + (3.0 * GELU_C * GELU_A) * hh)
        part = nn(g, w2_s[cols, :])
        ffn = part if ffn is None else ffn + part
        g2_s[:, cols] += nn(df_t, g)
        dh32 = nt(df, w2_s[cols, :]) * slope
        dh = dh32.astype(BF16)
        gb_s[0:1, cols] += jnp.sum(dh.astype(F32), axis=0, keepdims=True)
        g1_s[:, cols] += nn(m2_t, dh)
        part = nt(dh, w1_s[:, cols])
        dm2 = part if dm2 is None else dm2 + part
    ffn = deep(ffn + b2_s[...])
    dm2 = deep(dm2)
    out_o[...] = (x1 + gate2 * ffn).astype(BF16)
    gb_s[1:2, width : 2 * width] += jnp.sum(df.astype(F32), axis=0, keepdims=True)
    d_gate2 = jnp.sum(dy * ffn, axis=1)
    d_scale2 = jnp.sum(dm2 * n2, axis=1)
    d_shift2 = jnp.sum(dm2, axis=1)
    dx1 = dy + norm_back(n2, rstd2, dm2 * (1.0 + scale2))
    dx1_o[...] = dx1
    do = flat((dx1 * gate1).astype(BF16))
    d_gate1 = jnp.sum(dx1 * branch, axis=1)
    for l in range(per):
        row = pl.ds(step * per + l, 1)
        small_s[row, 0:width] = d_gate1[l : l + 1]
        small_s[row, width : 2 * width] = d_shift2[l : l + 1]
        small_s[row, 2 * width : 3 * width] = d_scale2[l : l + 1]
        small_s[row, 3 * width : 4 * width] = d_gate2[l : l + 1]
    gb_s[1:2, 0:width] += jnp.sum(do.astype(F32), axis=0, keepdims=True)
    go_s[...] += tn(att, do)
    datt_o[...] = deep(nt(do, wo_s[...]).astype(BF16))

    @pl.when(step == pl.num_programs(0) - 1)
    def _():
        for i in range(5):
            early_o[8 * i : 8 * i + 8, :] = small_s[:, i * width : (i + 1) * width].astype(BF16)
        pack = [gb_s[0:1, i * width : (i + 1) * width] for i in range(hidden // width)]
        pack += [gb_s[1:2, 0:width], gb_s[1:2, width : 2 * width]]
        pack += [jnp.zeros((1, width), F32)] * (8 - len(pack))
        early_o[40:48, :] = jnp.concatenate(pack, axis=0).astype(BF16)
        core = jnp.bitwise_and(info[0], 1)
        half = width // 8
        for y in range(2):
            for which, ref in enumerate((keep_o, send_o)):
                shard = 2 * y + jnp.bitwise_xor(core, which)
                for x in range(2):
                    take = pl.ds(pl.multiple_of(shard * 2 * half + x * half, 8), half)
                    wide = pl.ds(pl.multiple_of(shard * width, 128), width)
                    for z in range(4):
                        at = 2 * half * z
                        ref[y, x, at : at + half, :] = g1_s[
                            take, z * width : (z + 1) * width
                        ].astype(BF16)
                        rows = slice((4 * x + z) * half, (4 * x + z + 1) * half)
                        ref[y, x, at + half : at + 2 * half, :] = g2_s[rows, wide].astype(BF16)
                    ref[y, x, 8 * half : 9 * half, :] = go_s[take, :].astype(BF16)


def attn_bwd(info, tok, m1_i, qkv_i, p_i, datt_i, dx1_i, ada, *refs, per, base, last):
    wq, refs = refs[0:4], refs[4:]
    step = pl.program_id(0)
    length, width = tok.shape[1:]
    if last:
        _, g_i, small_i, gb_i = refs[0:4]
        gtok_o, late_o, keep_o, send_o = refs[4:8]
        wq_s, sem_q, g_s, small_s, gb_s = refs[8:]
    else:
        gtok_o, g_s, small_s, gb_s, wq_s, sem_q = refs

    @pl.when(step == 0)
    def _():
        copies = piece_copies(info[0], wq, wq_s, sem_q)
        for copy in copies:
            copy.start()
        if last:
            g_s[...] = g_i[...]
            small_s[...] = small_i[...]
            gb_s[...] = gb_i[...]
        else:
            g_s[...] = jnp.zeros_like(g_s)
            small_s[...] = jnp.zeros_like(small_s)
            gb_s[...] = jnp.zeros_like(gb_s)
        for copy in copies:
            copy.wait()

    part = lambda ref, l, at, j: ref[l, :, at + 128 * j : at + 128 * j + 128]
    dvs, dps, dss, dks, dqs, dqkvs, dm1s = {}, {}, {}, {}, {}, {}, {}

    def stage_a(u):
        l, t = divmod(u, HEADS)
        j, h = t // 2, t % 2
        v, datt = part(qkv_i, l, 2 * width, j), part(datt_i, l, 0, j)
        vm = jnp.where(half_mask(v.shape, h), v, jnp.zeros_like(v))
        dps[u] = nt(vm, datt)
        dvs[u] = nn(p_i[l, t], datt)

    def stage_b(u):
        l, t = divmod(u, HEADS)
        p32 = p_i[l, t].astype(F32)
        pd = p32 * dps[u]
        dss[u] = (pd - p32 * jnp.sum(pd, axis=0, keepdims=True)).astype(BF16)

    def stage_c(u):
        l, t = divmod(u, HEADS)
        j = t // 2
        dks[u] = nn(dss[u], part(qkv_i, l, 0, j)) * 0.125
        dqs[u] = tn(dss[u], part(qkv_i, l, width, j)) * 0.125

    def stage_f(l):
        grads = [
            jnp.where(half_mask(d[u].shape, 0), d[u], d[u + 1]).astype(BF16)
            for d in (dqs, dks, dvs)
            for u in range(l * HEADS, (l + 1) * HEADS, 2)
        ]
        dqkvs[l] = jnp.concatenate(grads, axis=-1)
        dm1s[l] = nt(dqkvs[l], wq_s[...])
        g_s[...] += nn(m1_i[l].T, dqkvs[l])

    def stage_g(l):
        dqkv, dm1 = dqkvs[l], dm1s[l]
        row = pl.ds(base + step * per + l, 1)
        scale = ada[row, width : 2 * width]
        n1, rstd1 = norm_parts(tok[l].astype(F32))
        sums = jnp.sum(dqkv.astype(F32), axis=0, keepdims=True)
        gb_s[0:1, :] += sums[:, 0:width]
        gb_s[1:2, :] += sums[:, 2 * width : 3 * width]
        small_s[row, 0:width] = jnp.sum(dm1, axis=0, keepdims=True)
        small_s[row, width : 2 * width] = jnp.sum(dm1 * n1, axis=0, keepdims=True)
        gtok_o[l] = dx1_i[l] + norm_back(n1, rstd1, dm1 * (1.0 + scale))

    n = HEADS * per
    for u in range(n + 2 + 0 + 0):
        if u < n:
            stage_a(u)
        if 0 <= u - 1 < n:
            stage_b(u - 1)
        if 0 <= u - 2 < n:
            stage_c(u - 2)
        f = u - 2 - 0
        if 0 <= f < n and f % HEADS == HEADS - 1:
            stage_f(f // HEADS)
        g = f - 0
        if 0 <= g < n and g % HEADS == HEADS - 1:
            stage_g(g // HEADS)

    if last:

        @pl.when(step == pl.num_programs(0) - 1)
        def _():
            for i in range(2):
                late_o[8 * i : 8 * i + 8, :] = small_s[:, i * width : (i + 1) * width].astype(BF16)
            late_o[16:24, :] = gb_s[...].astype(BF16)
            core = jnp.bitwise_and(info[0], 1)
            half = width // 8
            for y in range(2):
                for which, ref in enumerate((keep_o, send_o)):
                    shard = 2 * y + jnp.bitwise_xor(core, which)
                    for x in range(2):
                        take = pl.ds(pl.multiple_of(shard * 2 * half + x * half, 8), half)
                        ref[y, x] = g_s[take, :].astype(BF16)


def tree_sum(values):
    values = [v.astype(F32) for v in values]
    while len(values) > 1:
        values = [values[2 * i] + values[2 * i + 1] for i in range(len(values) // 2)]
    return values[0]


def ordered(values, me):
    bit = 1
    while bit < len(values):
        flip = (me & bit) != 0
        values = [jnp.where(flip, values[i ^ bit], values[i]) for i in range(len(values))]
        bit *= 2
    return values


def after(values, *deps):
    flat, tree = jax.tree.flatten(values)
    out = lax.optimization_barrier(tuple(flat) + tuple(deps))
    return jax.tree.unflatten(tree, out[: len(flat)])


def full(shape):
    return pl.BlockSpec(shape, lambda *_: (0,) * len(shape))


def call(body, info, operands, specs, outs, out_specs, scratch, grid, vmem, flops, traffic, exps=0, alias=None):
    return pl.pallas_call(
        body,
        out_shape=outs,
        input_output_aliases=alias or {},
        grid_spec=pltpu.PrefetchScalarGridSpec(
            num_scalar_prefetch=1,
            grid=grid,
            in_specs=specs,
            out_specs=out_specs,
            scratch_shapes=scratch,
        ),
        compiler_params=pltpu.CompilerParams(
            dimension_semantics=("arbitrary",) * len(grid), vmem_limit_bytes=vmem << 20
        ),
        cost_estimate=pl.CostEstimate(flops=flops, bytes_accessed=traffic, transcendentals=exps),
    )(info, *operands)


def on_device(
    latent_tokens, cond, w_ada, b_ada, w_qkv, b_qv, w_o, b_o, w_1, b_1, w_2, b_2, grad_out
):
    count, length, width = latent_tokens.shape
    hidden = w_1.shape[1]
    quarter, half = width // 4, width // 8
    reps = lax.axis_size("rep")
    shards = lax.axis_size("shard")
    s = lax.axis_index("shard")
    r = lax.axis_index("rep")
    y_at, x_at, z_at = s >> 1, r & 1, r >> 1
    n_z = reps // 2
    info = jnp.stack([s, y_at, x_at, z_at]).astype(jnp.int32)

    def swap(v, shard_bits=0, rep_bits=0):
        pairs = [
            (i * shards + j, (i ^ rep_bits) * shards + (j ^ shard_bits))
            for i in range(reps)
            for j in range(shards)
        ]
        return lax.ppermute(v, ("rep", "shard"), pairs)

    whole = lambda vs: [full(v.shape) for v in vs]
    ins = (cond, b_ada, b_qv, b_o, b_1, b_2)
    outs = [jax.ShapeDtypeStruct((count, quarter), BF16)] * 4 + [
        jax.ShapeDtypeStruct((1, 6 * width), F32),
        jax.ShapeDtypeStruct((8, width), F32),
    ]
    *cuts, share, packed = call(
        condition, info, ins, whole(ins), outs, whole(outs), [], (1,), 60, 0, 1 << 17
    )
    near_qkv, far_qkv = after((w_qkv, w_qkv), cuts[0])
    cuts = [cuts[0]] + [swap(cuts[k], k) for k in range(1, 4)]
    near_qkv, far_qkv = swap(near_qkv, 1), swap(far_qkv, 2)
    ffn_w = (w_o, w_1, w_2)
    near_w = [swap(v, 1) for v in after(ffn_w, cuts[1])]
    ins = tuple(cuts) + (w_ada, share, packed)
    outs = [jax.ShapeDtypeStruct((count, 7 * width), F32)] * 4
    parts = call(ada_parts, info, ins, whole(ins), outs, whole(outs), [], (1,), 60, 1 << 24, 1 << 20)
    sent = parts[0]
    p_qkv = (w_qkv, near_qkv, far_qkv, swap(far_qkv, 1))
    parts = [parts[0]] + [swap(parts[k], k) for k in range(1, 4)]
    far_w = [swap(v, 2) for v in after(ffn_w, sent)]

    anyspec = pl.BlockSpec(memory_space=pl.ANY)
    dma4 = pltpu.SemaphoreType.DMA((4,))
    tokens = count * length

    per = 2
    per3 = 1
    lat = lambda *tail: pl.BlockSpec((per,) + tail, lambda i, _: (i,) + (0,) * len(tail))
    m1, qkv, probs, att, ada, table = call(
        functools.partial(attn_fwd, per=per),
        info,
        (latent_tokens,) + tuple(parts) + p_qkv,
        [lat(length, width)] + [full(v.shape) for v in parts] + [anyspec] * 4,
        [
            jax.ShapeDtypeStruct((count, length, width), BF16),
            jax.ShapeDtypeStruct((count, length, 3 * width), BF16),
            jax.ShapeDtypeStruct((count, HEADS, length, length), BF16),
            jax.ShapeDtypeStruct((count, length, width), BF16),
            jax.ShapeDtypeStruct((count, 6 * width), F32),
            jax.ShapeDtypeStruct((4, 8, width), F32),
        ],
        [
            lat(length, width),
            lat(length, 3 * width),
            lat(HEADS, length, length),
            lat(length, width),
            full((count, 6 * width)),
            full((4, 8, width)),
        ],
        [pltpu.VMEM((width, 3 * width), BF16), pltpu.VMEM((1, 3 * width), F32), dma4],
        (count // per,),
        60,
        8 * tokens * width * width + 8 * tokens * length * width,
        20 * tokens * width,
        tokens * length * HEADS,
    )

    far_w = after(far_w, table)
    p_o, p_1, p_2 = ((v, near, far, swap(far, 1)) for v, near, far in zip(ffn_w, near_w, far_w))

    per2 = 2 if count % 2 == 0 else 1
    lat2 = lambda *tail: pl.BlockSpec((per2,) + tail, lambda i, _: (i,) + (0,) * len(tail))
    grads = (2, 2, 9 * half, width)
    block_out, dx1, datt, early, keep_f, send_f = call(
        functools.partial(ffn_both, per=per2, chunk=hidden),
        info,
        (latent_tokens, att, grad_out, ada, cond, table) + p_o + p_1 + p_2,
        [lat2(length, width)] * 3
        + [full(ada.shape), full(cond.shape), full(table.shape)]
        + [anyspec] * 12,
        [
            jax.ShapeDtypeStruct((count, length, width), BF16),
            jax.ShapeDtypeStruct((count, length, width), F32),
            jax.ShapeDtypeStruct((count, length, width), BF16),
            jax.ShapeDtypeStruct((48, width), BF16),
        ]
        + [jax.ShapeDtypeStruct(grads, BF16)] * 2,
        [lat2(length, width)] * 3 + [full((48, width))] + [full(grads)] * 2,
        [
            pltpu.VMEM((width, width), BF16),
            pltpu.VMEM((width, hidden), BF16),
            pltpu.VMEM((hidden, width), BF16),
            pltpu.VMEM((width, width), F32),
            pltpu.VMEM((width, hidden), F32),
            pltpu.VMEM((width, hidden), F32),
            pltpu.VMEM((8, 5 * width), F32),
            pltpu.VMEM((8, 5 * width), F32),
            pltpu.VMEM((1, width), F32),
            pltpu.VMEM((1, hidden), F32),
            pltpu.VMEM((1, width), F32),
            dma4,
            dma4,
            dma4,
        ],
        (count // per2,),
        60,
        12 * tokens * width * hidden + 6 * tokens * width * width,
        14 * tokens * width,
        tokens * hidden,
    )

    def chip_sum(keep, send):
        got = swap(send, 1)

        def part(y, x):
            both = [
                lax.dynamic_index_in_dim(
                    lax.dynamic_index_in_dim(v, y, 0, keepdims=False), x, 0, keepdims=False
                ).astype(F32)
                for v in (keep, got)
            ]
            return (both[0] + both[1]).astype(BF16)

        return [part(y_at ^ (k >> 1), x_at ^ (k & 1)) for k in range(4)]

    def backward(base, last, info, extra, extra_specs, outs, out_specs, scratch, alias):
        half_n = count // 2
        at = lambda *tail: pl.BlockSpec(
            (per3,) + tail, lambda i, _: (i + base // per3,) + (0,) * len(tail)
        )
        return call(
            functools.partial(attn_bwd, per=per3, base=base, last=last),
            info,
            (latent_tokens, m1, qkv, probs, datt, dx1, ada) + p_qkv + extra,
            [
                at(length, width),
                at(length, width),
                at(length, 3 * width),
                at(HEADS, length, length),
                at(length, width),
                at(length, width),
                full(ada.shape),
            ]
            + [anyspec] * 4
            + extra_specs,
            [jax.ShapeDtypeStruct((count, length, width), F32)] + outs,
            [at(length, width)] + out_specs,
            [pltpu.VMEM((width, 3 * width), BF16), dma4] + scratch,
            (half_n // per3,),
            60,
            6 * tokens * width * width + 5 * tokens * length * width,
            15 * tokens * width,
            0,
            alias,
        )

    acc = [(width, 3 * width), (8, 2 * width), (8, width)]
    acc_shapes = [jax.ShapeDtypeStruct(v, F32) for v in acc]
    acc_specs = [full(v) for v in acc]

    def over_plane(own, sends):
        return [own] + [swap(sends[k - 1], 2 * (k >> 1), k & 1) for k in range(1, 4)]

    def over_z(own, sends):
        return [own] + [swap(sends[k - 1], 0, 2 * k) for k in range(1, n_z)]

    first = x_at == 0

    def by_x(mine, yours):
        return jnp.where(first, mine, yours), jnp.where(first, yours, mine)

    def pair(v, shard_bits, rep_bits, second):
        other = swap(v, shard_bits, rep_bits)
        return jnp.concatenate(
            [jnp.where(second, other, v), jnp.where(second, v, other)], axis=0
        )

    def z_pair(v, bit):
        return pair(v, 0, 2 * bit, (z_at & bit) != 0)

    n_f = 9 * half
    n_e = early.shape[0]
    parts_f = chip_sum(keep_f, send_f)
    gtok, g_half, small_half, gb_half = backward(
        0, False, after(info, *parts_f), (), [], acc_shapes, acc_specs, [], None
    )
    got = over_plane(parts_f[0], parts_f[1:])
    early_g = z_pair(after(early, *parts_f), 2)
    bit = 4
    while bit < n_z:
        early_g = z_pair(early_g, bit)
        bit *= 2
    *got, early_g = after(got + [early_g], gb_half)
    total_f = tree_sum(got).astype(BF16)
    z_low = z_at & 3
    loads = [
        jnp.concatenate(
            [
                lax.dynamic_slice_in_dim(total_f, (z_low ^ (k & 3)) * 2 * half, 2 * half, 0),
                total_f[8 * half :],
            ],
            axis=0,
        )
        for k in range(n_z)
    ]
    early_g = pair(early_g, 0, 1, x_at == 1)
    send_shape = (2, 2, half, 3 * width)
    grad_tokens, late, keep_a, send_a = backward(
        count // 2,
        True,
        after(info, *loads),
        (gtok, g_half, small_half, gb_half),
        [anyspec] + acc_specs,
        [
            jax.ShapeDtypeStruct((24, width), BF16),
            jax.ShapeDtypeStruct(send_shape, BF16),
            jax.ShapeDtypeStruct(send_shape, BF16),
        ],
        [full((24, width)), full(send_shape), full(send_shape)],
        [pltpu.VMEM(v, F32) for v in acc],
        {12: 0},
    )
    *got, early_g = after(over_z(loads[0], loads[1:]) + [early_g], late)
    piece_f = tree_sum([v[: 2 * half] for v in got]).astype(BF16)
    out_f = tree_sum([v[2 * half : 3 * half] for v in got]).astype(BF16)

    parts_a = chip_sum(keep_a, send_a)
    n_l = late.shape[0]
    load = z_pair(jnp.concatenate([piece_f, late], axis=0), 1)
    early_g = z_pair(early_g, 1)
    got_a = over_plane(parts_a[0], parts_a[1:])
    load, early_g = after((load, early_g), *parts_a)
    bit = 2
    while bit < n_z:
        load = z_pair(load, bit)
        bit *= 2
    total_a, load, early_g = after((tree_sum(got_a).astype(BF16), load, early_g))
    ring_a = over_z(total_a, [total_a] * (n_z - 1))
    n_p = 2 * half + n_l
    blocks = [load[i * n_p : i * n_p + 2 * half] for i in range(4)]
    late_g = jnp.concatenate([load[i * n_p + 2 * half : (i + 1) * n_p] for i in range(n_z)], axis=0)
    mine_f = jnp.concatenate(blocks + [out_f], axis=0)
    yours_f = swap(mine_f, 0, 1)
    late_g = pair(late_g, 2, 0, y_at == 1)
    early_g = pair(early_g, 2, 0, y_at == 1)
    late_g = pair(late_g, 0, 1, x_at == 1)
    early_g = pair(early_g, 1, 0, (s & 1) == 1)
    late_g = pair(late_g, 1, 0, (s & 1) == 1)

    sides = by_x(mine_f, yours_f)
    deep = [side[: 8 * half].reshape(4, 2 * half, width) for side in sides]
    gw_1 = jnp.concatenate(
        [side[:, :half].transpose(1, 0, 2).reshape(half, hidden) for side in deep], axis=0
    ).astype(F32)
    gw_2 = jnp.concatenate(
        [side[:, half:].reshape(4 * half, width) for side in deep], axis=0
    ).T.astype(F32)
    gw_o = jnp.concatenate([side[8 * half :] for side in sides], axis=0).astype(F32)

    n_h = n_z // 2
    early_r = early_g.reshape(2, 2, 2, 2, n_h, n_e // 8, 8, width)
    early_r = early_r.transpose(0, 3, 1, 4, 2, 5, 6, 7).reshape(2, 2, 2, n_z, n_e // 8, 8, width)
    late_r = late_g.reshape(2, 2, 2, n_z, n_l // 8, 8, width)
    to_rows = lambda v, i: v[:, :, :, :, i].reshape(-1, width)
    cs_all = lax.dynamic_slice_in_dim(to_rows(early_r, 4), s * quarter, quarter, 1)
    d_late = jnp.concatenate([to_rows(late_r, i) for i in range(2)], axis=1)
    d_early = jnp.concatenate([to_rows(early_r, i) for i in range(4)], axis=1)
    contract = lambda v: lax.dot_general(
        cs_all, v, (((0,), (0,)), ((), ())), preferred_element_type=F32
    )
    gw_ada = jnp.concatenate([contract(d_late), contract(d_early)], axis=1)
    gb_ada = jnp.concatenate(
        [jnp.sum(d_late.astype(F32), axis=0), jnp.sum(d_early.astype(F32), axis=0)]
    )
    gb_early = jnp.sum(early_r[:, :, :, :, 5].astype(F32), axis=(0, 1, 2, 3))
    gb_late = jnp.sum(late_r[:, :, :, :, 2, :2].astype(F32), axis=(0, 1, 2, 3)).reshape(-1)

    def group(v, parts):
        v = lax.dynamic_index_in_dim(v, z_at, 3, keepdims=False)
        v = lax.dynamic_index_in_dim(v, x_at, 1, keepdims=False)
        return [v[:, :, i].transpose(1, 0, 2, 3).reshape(4 * 8, width) for i in range(parts)]

    dada = jnp.concatenate(group(late_r, 2) + group(early_r, 4), axis=1)
    dcs = lax.dot_general(dada, w_ada, (((1,), (1,)), ((), ())), preferred_element_type=F32)
    dcs = ordered([dcs[k * 8 : (k + 1) * 8] for k in range(4)], s)
    dcs = ordered([dcs[0]] + [swap(dcs[k], k) for k in range(1, 4)], s)
    c32 = cond.astype(F32)
    sig = 1.0 / (1.0 + jnp.exp(-c32))
    grad_cond = jnp.concatenate(dcs, axis=1) * (sig * (1.0 + c32 * (1.0 - sig)))

    def mine(row):
        part = row.shape[0] // shards
        return lax.dynamic_slice(row, (s * part,), (part,))

    *ring_a, gw_1, gw_2, gw_o = after(ring_a + [gw_1, gw_2, gw_o])
    mine_a = tree_sum(ring_a).astype(BF16)
    gw_qkv = jnp.concatenate(by_x(mine_a, swap(mine_a, 0, 1)), axis=0).astype(F32)

    return (
        block_out,
        grad_tokens,
        grad_cond,
        gw_ada,
        mine(gb_ada),
        gw_qkv,
        mine(gb_late),
        gw_o,
        mine(gb_early[hidden // width]),
        gw_1,
        mine(gb_early[: hidden // width].reshape(-1)),
        gw_2,
        mine(gb_early[hidden // width + 1]),
    )


def solution(mesh):
    lead = P(("rep", "shard"))
    part = P("shard")
    return jax.shard_map(
        on_device,
        mesh=mesh,
        in_specs=(lead, lead) + (part,) * 10 + (lead,),
        out_specs=(lead,) * 3 + (part,) * 10,
        check_vma=False,
    )
```

```python
import functools
import math

import jax
import jax.numpy as jnp
from jax import lax
from jax.experimental import pallas as pl
from jax.experimental.pallas import tpu as pltpu
from jax.sharding import PartitionSpec as P

HEADS = 6
F32 = jnp.float32
BF16 = jnp.bfloat16
EPS = 1e-06
GELU_C = math.sqrt(2.0 / math.pi)
GELU_A = 0.044715


def nn(a, b):
    return lax.dot_general(a, b, (((1,), (0,)), ((), ())), preferred_element_type=F32)


def nt(a, b):
    return lax.dot_general(a, b, (((1,), (1,)), ((), ())), preferred_element_type=F32)


def tn(a, b):
    return lax.dot_general(a, b, (((0,), (0,)), ((), ())), preferred_element_type=F32)


def norm_parts(x):
    centred = x - jnp.mean(x, axis=-1, keepdims=True)
    rstd = lax.rsqrt(jnp.mean(centred * centred, axis=-1, keepdims=True) + EPS)
    return centred * rstd, rstd


def norm_back(normed, rstd, grad):
    inner = jnp.mean(grad, axis=-1, keepdims=True)
    along = jnp.mean(grad * normed, axis=-1, keepdims=True)
    return rstd * (grad - inner - normed * along)


def piece_copies(mine, pieces, whole, sems):
    rows = pieces[0].shape[0]
    return [
        pltpu.make_async_copy(
            piece,
            whole.at[pl.ds(pl.multiple_of(jnp.bitwise_xor(mine, k) * rows, 32), rows)],
            sems.at[k],
        )
        for k, piece in enumerate(pieces)
    ]


def half_mask(shape, half):
    lane = lax.broadcasted_iota(jnp.int32, shape, len(shape) - 1)
    return (lane < shape[-1] // 2) if half == 0 else (lane >= shape[-1] // 2)


def condition(info, cond, b_ada, b_qv, b_o, b_1, b_2, w_o, w_1, w_2, *refs):
    cuts, share, packed, tall = refs[0:4], refs[4], refs[5], refs[6]
    c = cond[...].astype(F32)
    cs = c / (1.0 + jnp.exp(-c))
    cut = cs.shape[1] // 4
    for k, ref in enumerate(cuts):
        mine = jnp.bitwise_xor(info[0], k)
        ref[...] = sum(
            jnp.where(mine == j, cs[:, j * cut : (j + 1) * cut], 0.0) for j in range(4)
        ).astype(BF16)
    share[...] = jnp.zeros_like(share)
    n = b_ada.shape[0]
    row = b_ada[...].astype(F32).reshape(1, n)
    for j in range(4):

        @pl.when(info[0] == j)
        def _():
            share[:, j * n : (j + 1) * n] = row

    packed[...] = jnp.zeros_like(packed)
    for i, b in enumerate((b_qv, b_o, b_1, b_2)):
        packed[i : i + 1, 0 : b.shape[0]] = b[...].astype(F32).reshape(1, b.shape[0])
    rows, width = w_o.shape
    tall[0:rows] = w_o[...]
    many = w_1.shape[1] // width
    for i in range(many):
        tall[(1 + i) * rows : (2 + i) * rows] = w_1[:, i * width : (i + 1) * width]
    tall[(1 + many) * rows :] = w_2[...]


def ada_parts(info, c0, c1, c2, c3, w_ada, share, packed, *outs):
    for cut, out in zip((c0, c1, c2, c3), outs):
        n = w_ada.shape[1]
        out[:, 0:n] = nn(cut[...], w_ada[...]) + share[...]
        out[:, n:] = packed[...]


def bias_row(table, at, n):
    return jnp.concatenate([table[i, at : at + 1, 0:n] for i in range(4)], axis=1)


def attn_fwd(info, tok, *refs, per):
    parts, wq = refs[0:4], refs[4:8]
    m1_o, qkv_o, p_o, att_o, ada, table = refs[8:14]
    wq_s, bias_s, sem_q = refs[14:]
    step = pl.program_id(0)
    width = tok.shape[-1]

    @pl.when(step == 0)
    def _():
        cq = piece_copies(info[0], wq, wq_s, sem_q)
        for copy in cq:
            copy.start()
        ada[...] = sum(v[:, 0 : 6 * width] for v in parts)
        for k in range(4):
            table[jnp.bitwise_xor(info[0], k)] = parts[k][:, 6 * width :]
        row_qv = bias_row(table, 0, width // 2)
        bias_s[:, 0:width] = row_qv[:, 0:width]
        bias_s[:, width : 2 * width] = jnp.zeros((1, width), F32)
        bias_s[:, 2 * width : 3 * width] = row_qv[:, width : 2 * width]
        for copy in cq:
            copy.wait()

    qkvs, ss, ps, atts = {}, {}, {}, {}
    part = lambda l, at, j: qkvs[l][:, at + 128 * j : at + 128 * j + 128]

    def stage_q(l):
        row = pl.ds(step * per + l, 1)
        shift = ada[row, 0:width]
        scale = ada[row, width : 2 * width]
        n1, _ = norm_parts(tok[l].astype(F32))
        m1 = (n1 * (1.0 + scale) + shift).astype(BF16)
        m1_o[l] = m1
        qkvs[l] = (nn(m1, wq_s[...]) + bias_s[...]).astype(BF16)
        qkv_o[l] = qkvs[l]

    def stage_a(u):
        l, t = divmod(u, HEADS)
        j, h = t // 2, t % 2
        k = part(l, width, j)
        ss[u] = nt(jnp.where(half_mask(k.shape, h), k, jnp.zeros_like(k)), part(l, 0, j))

    def stage_b(u):
        l, t = divmod(u, HEADS)
        s = ss[u]
        top = jnp.max(s, axis=0, keepdims=True)
        e = jnp.exp((s - top) * 0.125)
        total = jnp.sum(e, axis=0, keepdims=True)
        ps[u] = (e * (1.0 / total)).astype(BF16)
        p_o[l, t] = ps[u]

    def stage_c(u):
        l, t = divmod(u, HEADS)
        j = t // 2
        atts[u] = tn(ps[u], part(l, 2 * width, j))
        if t % 2:
            att = jnp.where(half_mask(atts[u].shape, 0), atts[u - 1], atts[u])
            att_o[l, :, 128 * j : 128 * j + 128] = att.astype(BF16)

    n = HEADS * per
    stage_q(0)
    for u in range(n + 2):
        if u < n:
            stage_a(u)
        if u % HEADS == 1 and u // HEADS + 1 < per:
            stage_q(u // HEADS + 1)
        if 0 <= u - 1 < n:
            stage_b(u - 1)
        if 0 <= u - 2 < n:
            stage_c(u - 2)


def ffn_both(info, tok, att_i, dy_i, ada, cond, table, *refs, per, chunk):
    pieces = refs[0:4]
    out_o, dx1_o, datt_o, early_o, keep_o, send_o = refs[4:10]
    wo_s, w1_s, w2_s, go_s, g1_s, g2_s, small_s, gb_s, bo_s, b1_s, b2_s, sems = refs[10:]
    step = pl.program_id(0)
    length, width = tok.shape[1:]
    hidden = w1_s.shape[1]

    @pl.when(step == 0)
    def _():
        copies, n, rows = [], hidden // width + 2, width // 4
        for k, piece in enumerate(pieces):
            at = pl.multiple_of(jnp.bitwise_xor(info[0], k) * rows, 32)
            at2 = pl.multiple_of(jnp.bitwise_xor(info[0], k) * (hidden // 4), 32)
            places = [wo_s.at[pl.ds(at, rows)]]
            places += [
                w1_s.at[pl.ds(at, rows), i * width : (i + 1) * width] for i in range(n - 2)
            ]
            places += [w2_s.at[pl.ds(at2, hidden // 4)]]
            start = 0
            for i, place in enumerate(places):
                source = piece.at[start : start + place.shape[0]]
                copies.append(pltpu.make_async_copy(source, place, sems.at[n * k + i]))
                start += place.shape[0]
        for copy in copies:
            copy.start()
        go_s[...] = jnp.zeros_like(go_s)
        g1_s[...] = jnp.zeros_like(g1_s)
        g2_s[...] = jnp.zeros_like(g2_s)
        gb_s[...] = jnp.zeros_like(gb_s)
        bo_s[...] = bias_row(table, 1, width // 4)
        b1_s[...] = bias_row(table, 2, hidden // 4)
        b2_s[...] = bias_row(table, 3, width // 4)
        c = cond[...].astype(F32)
        small_s[:, 4 * width : 5 * width] = c / (1.0 + jnp.exp(-c))
        for copy in copies:
            copy.wait()

    def rows_of(at):
        return jnp.stack(
            [ada[pl.ds(step * per + l, 1), at * width : (at + 1) * width] for l in range(per)]
        )

    def flat(v):
        return v.reshape(per * length, v.shape[-1])

    def deep(v):
        return v.reshape(per, length, v.shape[-1])

    gate1, shift2, scale2, gate2 = rows_of(2), rows_of(3), rows_of(4), rows_of(5)
    att = flat(att_i[...])
    branch = deep(nn(att, wo_s[...]) + bo_s[...])
    x1 = tok[...].astype(F32) + gate1 * branch
    n2, rstd2 = norm_parts(x1)
    m2 = flat((n2 * (1.0 + scale2) + shift2).astype(BF16))
    dy = dy_i[...].astype(F32)
    df = flat((dy * gate2).astype(BF16))
    df_t = df.T
    m2_t = m2.T
    ffn = None
    dm2 = None
    for j in range(hidden // chunk):
        cols = slice(j * chunk, (j + 1) * chunk)
        h = nn(m2, w1_s[:, cols]) + b1_s[:, cols]
        hh = h * h
        t = jnp.tanh(h * (GELU_C + (GELU_C * GELU_A) * hh))
        half_t = 0.5 + 0.5 * t
        g = (h * half_t).astype(BF16)
        slope = half_t + (0.5 * h) * (1.0 - t * t) * (GELU_C + (3.0 * GELU_C * GELU_A) * hh)
        part = nn(g, w2_s[cols, :])
        ffn = part if ffn is None else ffn + part
        g2_s[:, cols] += nn(df_t, g)
        dh32 = nt(df, w2_s[cols, :]) * slope
        dh = dh32.astype(BF16)
        gb_s[0:1, cols] += jnp.sum(dh.astype(F32), axis=0, keepdims=True)
        g1_s[:, cols] += nn(m2_t, dh)
        part = nt(dh, w1_s[:, cols])
        dm2 = part if dm2 is None else dm2 + part
    ffn = deep(ffn + b2_s[...])
    dm2 = deep(dm2)
    out_o[...] = (x1 + gate2 * ffn).astype(BF16)
    gb_s[1:2, width : 2 * width] += jnp.sum(df.astype(F32), axis=0, keepdims=True)
    d_gate2 = jnp.sum(dy * ffn, axis=1)
    d_scale2 = jnp.sum(dm2 * n2, axis=1)
    d_shift2 = jnp.sum(dm2, axis=1)
    dx1 = dy + norm_back(n2, rstd2, dm2 * (1.0 + scale2))
    dx1_o[...] = dx1
    do = flat((dx1 * gate1).astype(BF16))
    d_gate1 = jnp.sum(dx1 * branch, axis=1)
    for l in range(per):
        row = pl.ds(step * per + l, 1)
        small_s[row, 0:width] = d_gate1[l : l + 1]
        small_s[row, width : 2 * width] = d_shift2[l : l + 1]
        small_s[row, 2 * width : 3 * width] = d_scale2[l : l + 1]
        small_s[row, 3 * width : 4 * width] = d_gate2[l : l + 1]
    gb_s[1:2, 0:width] += jnp.sum(do.astype(F32), axis=0, keepdims=True)
    go_s[...] += tn(att, do)
    datt_o[...] = deep(nt(do, wo_s[...]).astype(BF16))

    @pl.when(step == pl.num_programs(0) - 1)
    def _():
        for i in range(5):
            early_o[8 * i : 8 * i + 8, :] = small_s[:, i * width : (i + 1) * width].astype(BF16)
        pack = [gb_s[0:1, i * width : (i + 1) * width] for i in range(hidden // width)]
        pack += [gb_s[1:2, 0:width], gb_s[1:2, width : 2 * width]]
        pack += [jnp.zeros((1, width), F32)] * (8 - len(pack))
        early_o[40:48, :] = jnp.concatenate(pack, axis=0).astype(BF16)
        core = jnp.bitwise_and(info[0], 1)
        half = width // 8
        for y in range(2):
            for which, ref in enumerate((keep_o, send_o)):
                shard = 2 * y + jnp.bitwise_xor(core, which)
                for x in range(2):
                    take = pl.ds(pl.multiple_of(shard * 2 * half + x * half, 8), half)
                    wide = pl.ds(pl.multiple_of(shard * width, 128), width)
                    for z in range(4):
                        at = 2 * half * z
                        ref[y, x, at : at + half, :] = g1_s[
                            take, z * width : (z + 1) * width
                        ].astype(BF16)
                        rows = slice((4 * x + z) * half, (4 * x + z + 1) * half)
                        ref[y, x, at + half : at + 2 * half, :] = g2_s[rows, wide].astype(BF16)
                    ref[y, x, 8 * half : 9 * half, :] = go_s[take, :].astype(BF16)


def attn_bwd(info, tok, m1_i, qkv_i, p_i, datt_i, dx1_i, ada, *refs, per, base, last):
    wq, refs = refs[0:4], refs[4:]
    step = pl.program_id(0)
    length, width = tok.shape[1:]
    if last:
        _, g_i, small_i, gb_i = refs[0:4]
        gtok_o, late_o, keep_o, send_o = refs[4:8]
        wq_s, sem_q, g_s, small_s, gb_s = refs[8:]
    else:
        gtok_o, g_s, small_s, gb_s, wq_s, sem_q = refs

    @pl.when(step == 0)
    def _():
        copies = piece_copies(info[0], wq, wq_s, sem_q)
        for copy in copies:
            copy.start()
        if last:
            g_s[...] = g_i[...]
            small_s[...] = small_i[...]
            gb_s[...] = gb_i[...]
        else:
            g_s[...] = jnp.zeros_like(g_s)
            small_s[...] = jnp.zeros_like(small_s)
            gb_s[...] = jnp.zeros_like(gb_s)
        for copy in copies:
            copy.wait()

    part = lambda ref, l, at, j: ref[l, :, at + 128 * j : at + 128 * j + 128]
    dvs, dps, dss, dks, dqs, dqkvs, dm1s = {}, {}, {}, {}, {}, {}, {}

    def stage_a(u):
        l, t = divmod(u, HEADS)
        j, h = t // 2, t % 2
        v, datt = part(qkv_i, l, 2 * width, j), part(datt_i, l, 0, j)
        vm = jnp.where(half_mask(v.shape, h), v, jnp.zeros_like(v))
        dps[u] = nt(vm, datt)
        dvs[u] = nn(p_i[l, t], datt)

    def stage_b(u):
        l, t = divmod(u, HEADS)
        p32 = p_i[l, t].astype(F32)
        pd = p32 * dps[u]
        dss[u] = (pd - p32 * jnp.sum(pd, axis=0, keepdims=True)).astype(BF16)

    def stage_c(u):
        l, t = divmod(u, HEADS)
        j = t // 2
        dks[u] = nn(dss[u], part(qkv_i, l, 0, j)) * 0.125
        dqs[u] = tn(dss[u], part(qkv_i, l, width, j)) * 0.125

    def stage_f(l):
        grads = [
            jnp.where(half_mask(d[u].shape, 0), d[u], d[u + 1]).astype(BF16)
            for d in (dqs, dks, dvs)
            for u in range(l * HEADS, (l + 1) * HEADS, 2)
        ]
        dqkvs[l] = jnp.concatenate(grads, axis=-1)
        dm1s[l] = nt(dqkvs[l], wq_s[...])
        g_s[...] += nn(m1_i[l].T, dqkvs[l])

    def stage_g(l):
        dqkv, dm1 = dqkvs[l], dm1s[l]
        row = pl.ds(base + step * per + l, 1)
        scale = ada[row, width : 2 * width]
        n1, rstd1 = norm_parts(tok[l].astype(F32))
        sums = jnp.sum(dqkv.astype(F32), axis=0, keepdims=True)
        gb_s[0:1, :] += sums[:, 0:width]
        gb_s[1:2, :] += sums[:, 2 * width : 3 * width]
        small_s[row, 0:width] = jnp.sum(dm1, axis=0, keepdims=True)
        small_s[row, width : 2 * width] = jnp.sum(dm1 * n1, axis=0, keepdims=True)
        gtok_o[l] = dx1_i[l] + norm_back(n1, rstd1, dm1 * (1.0 + scale))

    n = HEADS * per
    for u in range(n + 2 + 0 + 0):
        if u < n:
            stage_a(u)
        if 0 <= u - 1 < n:
            stage_b(u - 1)
        if 0 <= u - 2 < n:
            stage_c(u - 2)
        f = u - 2 - 0
        if 0 <= f < n and f % HEADS == HEADS - 1:
            stage_f(f // HEADS)
        g = f - 0
        if 0 <= g < n and g % HEADS == HEADS - 1:
            stage_g(g // HEADS)

    if last:

        @pl.when(step == pl.num_programs(0) - 1)
        def _():
            for i in range(2):
                late_o[8 * i : 8 * i + 8, :] = small_s[:, i * width : (i + 1) * width].astype(BF16)
            late_o[16:24, :] = gb_s[...].astype(BF16)
            core = jnp.bitwise_and(info[0], 1)
            half = width // 8
            for y in range(2):
                for which, ref in enumerate((keep_o, send_o)):
                    shard = 2 * y + jnp.bitwise_xor(core, which)
                    for x in range(2):
                        take = pl.ds(pl.multiple_of(shard * 2 * half + x * half, 8), half)
                        ref[y, x] = g_s[take, :].astype(BF16)


def tree_sum(values):
    values = [v.astype(F32) for v in values]
    while len(values) > 1:
        values = [values[2 * i] + values[2 * i + 1] for i in range(len(values) // 2)]
    return values[0]


def ordered(values, me):
    bit = 1
    while bit < len(values):
        flip = (me & bit) != 0
        values = [jnp.where(flip, values[i ^ bit], values[i]) for i in range(len(values))]
        bit *= 2
    return values


def after(values, *deps):
    flat, tree = jax.tree.flatten(values)
    out = lax.optimization_barrier(tuple(flat) + tuple(deps))
    return jax.tree.unflatten(tree, out[: len(flat)])


def full(shape):
    return pl.BlockSpec(shape, lambda *_: (0,) * len(shape))


def call(body, info, operands, specs, outs, out_specs, scratch, grid, vmem, flops, traffic, exps=0, alias=None):
    return pl.pallas_call(
        body,
        out_shape=outs,
        input_output_aliases=alias or {},
        grid_spec=pltpu.PrefetchScalarGridSpec(
            num_scalar_prefetch=1,
            grid=grid,
            in_specs=specs,
            out_specs=out_specs,
            scratch_shapes=scratch,
        ),
        compiler_params=pltpu.CompilerParams(
            dimension_semantics=("arbitrary",) * len(grid), vmem_limit_bytes=vmem << 20
        ),
        cost_estimate=pl.CostEstimate(flops=flops, bytes_accessed=traffic, transcendentals=exps),
    )(info, *operands)


def on_device(
    latent_tokens, cond, w_ada, b_ada, w_qkv, b_qv, w_o, b_o, w_1, b_1, w_2, b_2, grad_out
):
    count, length, width = latent_tokens.shape
    hidden = w_1.shape[1]
    quarter, half = width // 4, width // 8
    reps = lax.axis_size("rep")
    shards = lax.axis_size("shard")
    s = lax.axis_index("shard")
    r = lax.axis_index("rep")
    y_at, x_at, z_at = s >> 1, r & 1, r >> 1
    n_z = reps // 2
    info = jnp.stack([s, y_at, x_at, z_at]).astype(jnp.int32)

    def swap(v, shard_bits=0, rep_bits=0):
        pairs = [
            (i * shards + j, (i ^ rep_bits) * shards + (j ^ shard_bits))
            for i in range(reps)
            for j in range(shards)
        ]
        return lax.ppermute(v, ("rep", "shard"), pairs)

    whole = lambda vs: [full(v.shape) for v in vs]
    ins = (cond, b_ada, b_qv, b_o, b_1, b_2, w_o, w_1, w_2)
    outs = [jax.ShapeDtypeStruct((count, quarter), BF16)] * 4 + [
        jax.ShapeDtypeStruct((1, 6 * width), F32),
        jax.ShapeDtypeStruct((8, width), F32),
        jax.ShapeDtypeStruct((quarter + quarter * hidden // width + hidden // 4, width), BF16),
    ]
    *cuts, share, packed, ffn_w = call(
        condition, info, ins, whole(ins), outs, whole(outs), [], (1,), 60, 0, 1 << 17
    )
    cuts = [cuts[0]] + [swap(cuts[k], k) for k in range(1, 4)]
    near_qkv, far_qkv = after((w_qkv, w_qkv), *cuts)
    near_qkv, far_qkv = swap(near_qkv, 1), swap(far_qkv, 2)
    ins = tuple(cuts) + (w_ada, share, packed)
    outs = [jax.ShapeDtypeStruct((count, 7 * width), F32)] * 4
    parts = call(ada_parts, info, ins, whole(ins), outs, whole(outs), [], (1,), 60, 1 << 24, 1 << 20)
    sent = parts[0]
    p_qkv = (w_qkv, near_qkv, far_qkv, swap(far_qkv, 1))
    parts = [parts[0]] + [swap(parts[k], k) for k in range(1, 4)]
    near_w = swap(after(ffn_w, sent), 1)
    far_w = swap(after(ffn_w, *parts), 2)

    anyspec = pl.BlockSpec(memory_space=pl.ANY)
    dma4 = pltpu.SemaphoreType.DMA((4,))
    tokens = count * length

    per = 2
    per3 = 1
    lat = lambda *tail: pl.BlockSpec((per,) + tail, lambda i, _: (i,) + (0,) * len(tail))
    m1, qkv, probs, att, ada, table = call(
        functools.partial(attn_fwd, per=per),
        info,
        (latent_tokens,) + tuple(parts) + p_qkv,
        [lat(length, width)] + [full(v.shape) for v in parts] + [anyspec] * 4,
        [
            jax.ShapeDtypeStruct((count, length, width), BF16),
            jax.ShapeDtypeStruct((count, length, 3 * width), BF16),
            jax.ShapeDtypeStruct((count, HEADS, length, length), BF16),
            jax.ShapeDtypeStruct((count, length, width), BF16),
            jax.ShapeDtypeStruct((count, 6 * width), F32),
            jax.ShapeDtypeStruct((4, 8, width), F32),
        ],
        [
            lat(length, width),
            lat(length, 3 * width),
            lat(HEADS, length, length),
            lat(length, width),
            full((count, 6 * width)),
            full((4, 8, width)),
        ],
        [pltpu.VMEM((width, 3 * width), BF16), pltpu.VMEM((1, 3 * width), F32), dma4],
        (count // per,),
        60,
        8 * tokens * width * width + 8 * tokens * length * width,
        20 * tokens * width,
        tokens * length * HEADS,
    )

    far_w = after(far_w, table)
    p_ffn = (ffn_w, near_w, far_w, swap(far_w, 1))

    per2 = 2 if count % 2 == 0 else 1
    lat2 = lambda *tail: pl.BlockSpec((per2,) + tail, lambda i, _: (i,) + (0,) * len(tail))
    grads = (2, 2, 9 * half, width)
    block_out, dx1, datt, early, keep_f, send_f = call(
        functools.partial(ffn_both, per=per2, chunk=hidden),
        info,
        (latent_tokens, att, grad_out, ada, cond, table) + p_ffn,
        [lat2(length, width)] * 3
        + [full(ada.shape), full(cond.shape), full(table.shape)]
        + [anyspec] * 4,
        [
            jax.ShapeDtypeStruct((count, length, width), BF16),
            jax.ShapeDtypeStruct((count, length, width), F32),
            jax.ShapeDtypeStruct((count, length, width), BF16),
            jax.ShapeDtypeStruct((48, width), BF16),
        ]
        + [jax.ShapeDtypeStruct(grads, BF16)] * 2,
        [lat2(length, width)] * 3 + [full((48, width))] + [full(grads)] * 2,
        [
            pltpu.VMEM((width, width), BF16),
            pltpu.VMEM((width, hidden), BF16),
            pltpu.VMEM((hidden, width), BF16),
            pltpu.VMEM((width, width), F32),
            pltpu.VMEM((width, hidden), F32),
            pltpu.VMEM((width, hidden), F32),
            pltpu.VMEM((8, 5 * width), F32),
            pltpu.VMEM((8, 5 * width), F32),
            pltpu.VMEM((1, width), F32),
            pltpu.VMEM((1, hidden), F32),
            pltpu.VMEM((1, width), F32),
            pltpu.SemaphoreType.DMA((4 * (hidden // width + 2),)),
        ],
        (count // per2,),
        60,
        12 * tokens * width * hidden + 6 * tokens * width * width,
        14 * tokens * width,
        tokens * hidden,
    )

    def chip_sum(keep, send):
        got = swap(send, 1)

        def part(y, x):
            both = [
                lax.dynamic_index_in_dim(
                    lax.dynamic_index_in_dim(v, y, 0, keepdims=False), x, 0, keepdims=False
                ).astype(F32)
                for v in (keep, got)
            ]
            return (both[0] + both[1]).astype(BF16)

        return [part(y_at ^ (k >> 1), x_at ^ (k & 1)) for k in range(4)]

    def backward(base, last, info, extra, extra_specs, outs, out_specs, scratch, alias):
        half_n = count // 2
        at = lambda *tail: pl.BlockSpec(
            (per3,) + tail, lambda i, _: (i + base // per3,) + (0,) * len(tail)
        )
        return call(
            functools.partial(attn_bwd, per=per3, base=base, last=last),
            info,
            (latent_tokens, m1, qkv, probs, datt, dx1, ada) + p_qkv + extra,
            [
                at(length, width),
                at(length, width),
                at(length, 3 * width),
                at(HEADS, length, length),
                at(length, width),
                at(length, width),
                full(ada.shape),
            ]
            + [anyspec] * 4
            + extra_specs,
            [jax.ShapeDtypeStruct((count, length, width), F32)] + outs,
            [at(length, width)] + out_specs,
            [pltpu.VMEM((width, 3 * width), BF16), dma4] + scratch,
            (half_n // per3,),
            60,
            6 * tokens * width * width + 5 * tokens * length * width,
            15 * tokens * width,
            0,
            alias,
        )

    acc = [(width, 3 * width), (8, 2 * width), (8, width)]
    acc_shapes = [jax.ShapeDtypeStruct(v, F32) for v in acc]
    acc_specs = [full(v) for v in acc]

    def over_plane(own, sends):
        return [own] + [swap(sends[k - 1], 2 * (k >> 1), k & 1) for k in range(1, 4)]

    def over_z(own, sends):
        return [own] + [swap(sends[k - 1], 0, 2 * k) for k in range(1, n_z)]

    first = x_at == 0

    def by_x(mine, yours):
        return jnp.where(first, mine, yours), jnp.where(first, yours, mine)

    def pair(v, shard_bits, rep_bits, second):
        other = swap(v, shard_bits, rep_bits)
        return jnp.concatenate(
            [jnp.where(second, other, v), jnp.where(second, v, other)], axis=0
        )

    def z_pair(v, bit):
        return pair(v, 0, 2 * bit, (z_at & bit) != 0)

    n_f, n_e = 9 * half, early.shape[0]
    early_z = over_z(early, [early] * (n_z - 1))
    parts_f = chip_sum(keep_f, send_f)
    *early_z, first_part = after(early_z + parts_f[:1])
    parts_f = [first_part] + parts_f[1:]
    early_g = jnp.concatenate(ordered(early_z, z_at), axis=0)

    got = over_plane(parts_f[0], parts_f[1:])
    early_x = pair(early_g, 2, 0, y_at == 1)
    gtok, g_half, small_half, gb_half = backward(
        0, False, after(info, *parts_f), (), [], acc_shapes, acc_specs, [], None
    )
    *got, early_g = after(got + [early_x], gb_half)
    total_f = tree_sum(got).astype(BF16)
    z_low = z_at & 3
    loads = [
        jnp.concatenate(
            [
                lax.dynamic_slice_in_dim(total_f, (z_low ^ (k & 3)) * 2 * half, 2 * half, 0),
                total_f[8 * half :],
            ],
            axis=0,
        )
        for k in range(n_z)
    ]

    got = over_z(loads[0], loads[1:])
    early_y = pair(early_g, 0, 1, x_at == 1)
    send_shape = (2, 2, half, 3 * width)
    grad_tokens, late, keep_a, send_a = backward(
        count // 2,
        True,
        after(info, *loads),
        (gtok, g_half, small_half, gb_half),
        [anyspec] + acc_specs,
        [
            jax.ShapeDtypeStruct((24, width), BF16),
            jax.ShapeDtypeStruct(send_shape, BF16),
            jax.ShapeDtypeStruct(send_shape, BF16),
        ],
        [full((24, width)), full(send_shape), full(send_shape)],
        [pltpu.VMEM(v, F32) for v in acc],
        {12: 0},
    )
    *got, early_g, keep_a, send_a, late = after(got + [early_y, keep_a, send_a, late])
    piece_f = tree_sum([v[: 2 * half] for v in got]).astype(BF16)
    out_f = tree_sum([v[2 * half : 3 * half] for v in got]).astype(BF16)

    n_l = late.shape[0]
    parts_a = chip_sum(keep_a, send_a)
    late_z = over_z(late, [late] * (n_z - 1))
    first_f = swap(piece_f, 0, 2)
    *phase, early_g, first_f = after(parts_a + late_z + [early_g, first_f])
    parts_a, late_z = phase[:4], phase[4:]

    late_g = jnp.concatenate(ordered(late_z, z_at), axis=0)
    wide_rows = lambda v: jnp.concatenate(
        [v[:, i * width : (i + 1) * width] for i in range(3)], axis=0
    )
    loads = [jnp.concatenate([wide_rows(v), late_g], axis=0) for v in parts_a]
    got = over_plane(loads[0], loads[1:])
    two_f = jnp.concatenate([piece_f, first_f], axis=0)
    rest_f = swap(two_f, 0, 4)
    early_c = pair(early_g, 1, 0, (s & 1) == 1)
    *got, two_f, rest_f, early_g = after(got + [two_f, rest_f, early_c])

    total_a = tree_sum([v[: 3 * half] for v in got]).astype(BF16)
    late_g = jnp.concatenate(ordered([v[3 * half :] for v in got], 2 * y_at + x_at), axis=0)
    ring_a = over_z(total_a, [total_a] * (n_z - 1))
    blocks = [two_f[: 2 * half], two_f[2 * half :], rest_f[: 2 * half], rest_f[2 * half :]]
    mine_f = jnp.concatenate(ordered(blocks, z_low) + [out_f], axis=0)
    yours_f = swap(mine_f, 0, 1)
    late_g = pair(late_g, 1, 0, (s & 1) == 1)

    sides = by_x(mine_f, yours_f)
    deep = [side[: 8 * half].reshape(4, 2 * half, width) for side in sides]
    gw_1 = jnp.concatenate(
        [side[:, :half].transpose(1, 0, 2).reshape(half, hidden) for side in deep], axis=0
    ).astype(F32)
    gw_2 = jnp.concatenate(
        [side[:, half:].reshape(4 * half, width) for side in deep], axis=0
    ).T.astype(F32)
    gw_o = jnp.concatenate([side[8 * half :] for side in sides], axis=0).astype(F32)

    early_r = early_g.reshape(2, 2, 2, n_z, n_e // 8, 8, width).transpose(0, 2, 1, 3, 4, 5, 6)
    late_r = late_g.reshape(2, 2, 2, n_z, n_l // 8, 8, width)
    to_rows = lambda v, i: v[:, :, :, :, i].reshape(-1, width)
    cs_all = lax.dynamic_slice_in_dim(to_rows(early_r, 4), s * quarter, quarter, 1)
    d_late = jnp.concatenate([to_rows(late_r, i) for i in range(2)], axis=1)
    d_early = jnp.concatenate([to_rows(early_r, i) for i in range(4)], axis=1)
    contract = lambda v: lax.dot_general(
        cs_all, v, (((0,), (0,)), ((), ())), preferred_element_type=F32
    )
    gw_ada = jnp.concatenate([contract(d_late), contract(d_early)], axis=1)
    gb_ada = jnp.concatenate(
        [jnp.sum(d_late.astype(F32), axis=0), jnp.sum(d_early.astype(F32), axis=0)]
    )
    gb_early = jnp.sum(early_r[:, :, :, :, 5].astype(F32), axis=(0, 1, 2, 3))
    gb_late = jnp.sum(late_r[:, :, :, :, 2, :2].astype(F32), axis=(0, 1, 2, 3)).reshape(-1)

    def group(v, parts):
        v = lax.dynamic_index_in_dim(v, z_at, 3, keepdims=False)
        v = lax.dynamic_index_in_dim(v, x_at, 2, keepdims=False)
        return [v[:, :, i].transpose(1, 0, 2, 3).reshape(4 * 8, width) for i in range(parts)]

    dada = jnp.concatenate(group(late_r, 2) + group(early_r, 4), axis=1)
    dcs = lax.dot_general(dada, w_ada, (((1,), (1,)), ((), ())), preferred_element_type=F32)
    *ring_a, gw_1, gw_2, gw_o, gw_ada, dcs = after(ring_a + [gw_1, gw_2, gw_o, gw_ada, dcs])
    mine_a = tree_sum(ring_a).astype(BF16)
    yours_a = swap(mine_a, 0, 1)
    dcs = ordered([dcs[k * 8 : (k + 1) * 8] for k in range(4)], s)
    dcs = ordered([dcs[0]] + [swap(dcs[k], k) for k in range(1, 4)], s)
    c32 = cond.astype(F32)
    sig = 1.0 / (1.0 + jnp.exp(-c32))
    grad_cond = jnp.concatenate(dcs, axis=1) * (sig * (1.0 + c32 * (1.0 - sig)))

    def mine(row):
        part = row.shape[0] // shards
        return lax.dynamic_slice(row, (s * part,), (part,))

    tall = jnp.concatenate(
        [v.reshape(3, half, width).transpose(1, 0, 2).reshape(half, 3 * width) for v in by_x(mine_a, yours_a)],
        axis=0,
    )
    gw_qkv = tall.astype(F32)

    return (
        block_out,
        grad_tokens,
        grad_cond,
        gw_ada,
        mine(gb_ada),
        gw_qkv,
        mine(gb_late),
        gw_o,
        mine(gb_early[hidden // width]),
        gw_1,
        mine(gb_early[: hidden // width].reshape(-1)),
        gw_2,
        mine(gb_early[hidden // width + 1]),
    )


def solution(mesh):
    lead = P(("rep", "shard"))
    part = P("shard")
    return jax.shard_map(
        on_device,
        mesh=mesh,
        in_specs=(lead, lead) + (part,) * 10 + (lead,),
        out_specs=(lead,) * 3 + (part,) * 10,
        check_vma=False,
    )
```

```python
import functools
import math

import jax
import jax.numpy as jnp
from jax import lax
from jax.experimental import pallas as pl
from jax.experimental.pallas import tpu as pltpu
from jax.sharding import PartitionSpec as P

HEADS = 6
F32 = jnp.float32
BF16 = jnp.bfloat16
EPS = 1e-06
GELU_C = math.sqrt(2.0 / math.pi)
GELU_A = 0.044715


def nn(a, b):
    return lax.dot_general(a, b, (((1,), (0,)), ((), ())), preferred_element_type=F32)


def nt(a, b):
    return lax.dot_general(a, b, (((1,), (1,)), ((), ())), preferred_element_type=F32)


def tn(a, b):
    return lax.dot_general(a, b, (((0,), (0,)), ((), ())), preferred_element_type=F32)


def norm_parts(x):
    centred = x - jnp.mean(x, axis=-1, keepdims=True)
    rstd = lax.rsqrt(jnp.mean(centred * centred, axis=-1, keepdims=True) + EPS)
    return centred * rstd, rstd


def norm_back(normed, rstd, grad):
    inner = jnp.mean(grad, axis=-1, keepdims=True)
    along = jnp.mean(grad * normed, axis=-1, keepdims=True)
    return rstd * (grad - inner - normed * along)


def piece_copies(mine, pieces, whole, sems):
    rows = pieces[0].shape[0]
    return [
        pltpu.make_async_copy(
            piece,
            whole.at[pl.ds(pl.multiple_of(jnp.bitwise_xor(mine, k) * rows, 32), rows)],
            sems.at[k],
        )
        for k, piece in enumerate(pieces)
    ]


def half_mask(shape, half):
    lane = lax.broadcasted_iota(jnp.int32, shape, len(shape) - 1)
    return (lane < shape[-1] // 2) if half == 0 else (lane >= shape[-1] // 2)


def pack(info, w_o, w_1, w_2, tall):
    rows, width = w_o.shape
    tall[0:rows] = w_o[...]
    many = w_1.shape[1] // width
    for i in range(many):
        tall[(1 + i) * rows : (2 + i) * rows] = w_1[:, i * width : (i + 1) * width]
    tall[(1 + many) * rows :] = w_2[...]


def ada_parts(info, c0, c1, c2, c3, w_ada, b_ada, b_qv, b_o, b_1, b_2, *refs):
    outs, share, packed = refs[0:8], refs[8], refs[9]
    share[...] = jnp.zeros_like(share)
    packed[...] = jnp.zeros_like(packed)
    n = b_ada.shape[0]
    row = b_ada[...].astype(F32).reshape(1, n)
    for j in range(4):

        @pl.when(info[0] == j)
        def _():
            share[:, j * n : (j + 1) * n] = row

    for i, b in enumerate((b_qv, b_o, b_1, b_2)):
        packed[i : i + 1, 0 : b.shape[0]] = b[...].astype(F32).reshape(1, b.shape[0])
    m = w_ada.shape[1] // 3
    for cond, first, rest in zip((c0, c1, c2, c3), outs[0:4], outs[4:8]):
        c = cond[...].astype(F32)
        cs = c / (1.0 + jnp.exp(-c))
        cut = cs.shape[1] // 4
        mine = sum(
            jnp.where(info[0] == j, cs[:, j * cut : (j + 1) * cut], 0.0) for j in range(4)
        ).astype(BF16)
        part = nn(mine, w_ada[...]) + share[...]
        first[:, 0:m] = part[:, 0:m]
        first[:, m:] = packed[...]
        rest[...] = part[:, m:]


def bias_row(table, at, n):
    return jnp.concatenate([table[i, at : at + 1, 0:n] for i in range(4)], axis=1)


def attn_fwd(info, tok, *refs, per):
    parts, wq = refs[0:4], refs[4:8]
    m1_o, qkv_o, p_o, att_o, ada, table, wq_o = refs[8:15]
    wq_s, bias_s, sem_q = refs[15:]
    step = pl.program_id(0)
    width = tok.shape[-1]

    @pl.when(step == 0)
    def _():
        cq = piece_copies(info[0], wq, wq_s, sem_q)
        for copy in cq:
            copy.start()
        ada[...] = sum(v[:, 0 : 2 * width] for v in parts)
        for k in range(4):
            table[jnp.bitwise_xor(info[0], k)] = parts[k][:, 2 * width :]
        row_qv = bias_row(table, 0, width // 2)
        bias_s[:, 0:width] = row_qv[:, 0:width]
        bias_s[:, width : 2 * width] = jnp.zeros((1, width), F32)
        bias_s[:, 2 * width : 3 * width] = row_qv[:, width : 2 * width]
        for copy in cq:
            copy.wait()
        wq_o[...] = wq_s[...]

    qkvs, ss, ps, atts = {}, {}, {}, {}
    part = lambda l, at, j: qkvs[l][:, at + 128 * j : at + 128 * j + 128]

    def stage_q(l):
        row = pl.ds(step * per + l, 1)
        shift = ada[row, 0:width]
        scale = ada[row, width : 2 * width]
        n1, _ = norm_parts(tok[l].astype(F32))
        m1 = (n1 * (1.0 + scale) + shift).astype(BF16)
        m1_o[l] = m1
        qkvs[l] = (nn(m1, wq_s[...]) + bias_s[...]).astype(BF16)
        qkv_o[l] = qkvs[l]

    def stage_a(u):
        l, t = divmod(u, HEADS)
        j, h = t // 2, t % 2
        k = part(l, width, j)
        ss[u] = nt(jnp.where(half_mask(k.shape, h), k, jnp.zeros_like(k)), part(l, 0, j))

    def stage_b(u):
        l, t = divmod(u, HEADS)
        s = ss[u]
        top = jnp.max(s, axis=0, keepdims=True)
        e = jnp.exp((s - top) * 0.125)
        total = jnp.sum(e, axis=0, keepdims=True)
        ps[u] = (e * (1.0 / total)).astype(BF16)
        p_o[l, t] = ps[u]

    def stage_c(u):
        l, t = divmod(u, HEADS)
        j = t // 2
        atts[u] = tn(ps[u], part(l, 2 * width, j))
        if t % 2:
            att = jnp.where(half_mask(atts[u].shape, 0), atts[u - 1], atts[u])
            att_o[l, :, 128 * j : 128 * j + 128] = att.astype(BF16)

    n = HEADS * per
    stage_q(0)
    for u in range(n + 2):
        if u < n:
            stage_a(u)
        if u % HEADS == 1 and u // HEADS + 1 < per:
            stage_q(u // HEADS + 1)
        if 0 <= u - 1 < n:
            stage_b(u - 1)
        if 0 <= u - 2 < n:
            stage_c(u - 2)


def ffn_both(info, tok, att_i, dy_i, cond, table, *refs, per, chunk):
    ada_parts, pieces = refs[0:4], refs[4:8]
    out_o, dx1_o, datt_o, early_o, keep_o, send_o = refs[8:14]
    wo_s, w1_s, w2_s, go_s, g1_s, g2_s, small_s, gb_s, bo_s, b1_s, b2_s, ada, sems = refs[14:]
    step = pl.program_id(0)
    length, width = tok.shape[1:]
    hidden = w1_s.shape[1]

    @pl.when(step == 0)
    def _():
        copies, n, rows = [], hidden // width + 2, width // 4
        for k, piece in enumerate(pieces):
            at = pl.multiple_of(jnp.bitwise_xor(info[0], k) * rows, 32)
            at2 = pl.multiple_of(jnp.bitwise_xor(info[0], k) * (hidden // 4), 32)
            places = [wo_s.at[pl.ds(at, rows)]]
            places += [
                w1_s.at[pl.ds(at, rows), i * width : (i + 1) * width] for i in range(n - 2)
            ]
            places += [w2_s.at[pl.ds(at2, hidden // 4)]]
            start = 0
            for i, place in enumerate(places):
                source = piece.at[start : start + place.shape[0]]
                copies.append(pltpu.make_async_copy(source, place, sems.at[n * k + i]))
                start += place.shape[0]
        for copy in copies:
            copy.start()
        go_s[...] = jnp.zeros_like(go_s)
        g1_s[...] = jnp.zeros_like(g1_s)
        g2_s[...] = jnp.zeros_like(g2_s)
        gb_s[...] = jnp.zeros_like(gb_s)
        ada[...] = sum(v[...] for v in ada_parts)
        bo_s[...] = bias_row(table, 1, width // 4)
        b1_s[...] = bias_row(table, 2, hidden // 4)
        b2_s[...] = bias_row(table, 3, width // 4)
        c = cond[...].astype(F32)
        small_s[:, 4 * width : 5 * width] = c / (1.0 + jnp.exp(-c))
        for copy in copies:
            copy.wait()

    def rows_of(at):
        return jnp.stack(
            [ada[pl.ds(step * per + l, 1), at * width : (at + 1) * width] for l in range(per)]
        )

    def flat(v):
        return v.reshape(per * length, v.shape[-1])

    def deep(v):
        return v.reshape(per, length, v.shape[-1])

    gate1, shift2, scale2, gate2 = rows_of(0), rows_of(1), rows_of(2), rows_of(3)
    att = flat(att_i[...])
    branch = deep(nn(att, wo_s[...]) + bo_s[...])
    x1 = tok[...].astype(F32) + gate1 * branch
    n2, rstd2 = norm_parts(x1)
    m2 = flat((n2 * (1.0 + scale2) + shift2).astype(BF16))
    dy = dy_i[...].astype(F32)
    df = flat((dy * gate2).astype(BF16))
    df_t = df.T
    m2_t = m2.T
    ffn = None
    dm2 = None
    for j in range(hidden // chunk):
        cols = slice(j * chunk, (j + 1) * chunk)
        h = nn(m2, w1_s[:, cols]) + b1_s[:, cols]
        hh = h * h
        u = h * (GELU_C + (GELU_C * GELU_A) * hh)
        half_t = 0.5 + 0.5 * jnp.tanh(u)
        g = (h * half_t).astype(BF16)
        slope = half_t * (1.0 + (1.0 - half_t) * (6.0 * u - (4.0 * GELU_C) * h))
        part = nn(g, w2_s[cols, :])
        ffn = part if ffn is None else ffn + part
        g2_s[:, cols] += nn(df_t, g)
        dh32 = nt(df, w2_s[cols, :]) * slope
        dh = dh32.astype(BF16)
        gb_s[0:1, cols] += jnp.sum(dh.astype(F32), axis=0, keepdims=True)
        g1_s[:, cols] += nn(m2_t, dh)
        part = nt(dh, w1_s[:, cols])
        dm2 = part if dm2 is None else dm2 + part
    ffn = deep(ffn + b2_s[...])
    dm2 = deep(dm2)
    out_o[...] = (x1 + gate2 * ffn).astype(BF16)
    gb_s[1:2, width : 2 * width] += jnp.sum(df.astype(F32), axis=0, keepdims=True)
    d_gate2 = jnp.sum(dy * ffn, axis=1)
    d_scale2 = jnp.sum(dm2 * n2, axis=1)
    d_shift2 = jnp.sum(dm2, axis=1)
    dx1 = dy + norm_back(n2, rstd2, dm2 * (1.0 + scale2))
    dx1_o[...] = dx1
    do = flat((dx1 * gate1).astype(BF16))
    d_gate1 = jnp.sum(dx1 * branch, axis=1)
    for l in range(per):
        row = pl.ds(step * per + l, 1)
        small_s[row, 0:width] = d_gate1[l : l + 1]
        small_s[row, width : 2 * width] = d_shift2[l : l + 1]
        small_s[row, 2 * width : 3 * width] = d_scale2[l : l + 1]
        small_s[row, 3 * width : 4 * width] = d_gate2[l : l + 1]
    gb_s[1:2, 0:width] += jnp.sum(do.astype(F32), axis=0, keepdims=True)
    go_s[...] += tn(att, do)
    datt_o[...] = deep(nt(do, wo_s[...]).astype(BF16))

    @pl.when(step == pl.num_programs(0) - 1)
    def _():
        for i in range(5):
            early_o[8 * i : 8 * i + 8, :] = small_s[:, i * width : (i + 1) * width].astype(BF16)
        pack = [gb_s[0:1, i * width : (i + 1) * width] for i in range(hidden // width)]
        pack += [gb_s[1:2, 0:width], gb_s[1:2, width : 2 * width]]
        pack += [jnp.zeros((1, width), F32)] * (8 - len(pack))
        early_o[40:48, :] = jnp.concatenate(pack, axis=0).astype(BF16)
        core = jnp.bitwise_and(info[0], 1)
        half = width // 8
        for y in range(2):
            for which, ref in enumerate((keep_o, send_o)):
                shard = 2 * y + jnp.bitwise_xor(core, which)
                for x in range(2):
                    take = pl.ds(pl.multiple_of(shard * 2 * half + x * half, 8), half)
                    wide = pl.ds(pl.multiple_of(shard * width, 128), width)
                    for z in range(4):
                        at = 2 * half * z
                        ref[y, x, at : at + half, :] = g1_s[
                            take, z * width : (z + 1) * width
                        ].astype(BF16)
                        rows = slice((4 * x + z) * half, (4 * x + z + 1) * half)
                        ref[y, x, at + half : at + 2 * half, :] = g2_s[rows, wide].astype(BF16)
                    ref[y, x, 8 * half : 9 * half, :] = go_s[take, :].astype(BF16)


def attn_bwd(info, tok, m1_i, qkv_i, p_i, datt_i, dx1_i, ada, wq_s, *refs, per, base, last):
    step = pl.program_id(0)
    length, width = tok.shape[1:]
    if last:
        _, g_i, small_i, gb_i, early = refs[0:5]
        gtok_o, late_o, keep_o, send_o = refs[5:9]
        g_s, small_s, gb_s = refs[9:]
    else:
        gtok_o, g_s, small_s, gb_s = refs

    @pl.when(step == 0)
    def _():
        if last:
            g_s[...] = g_i[...]
            small_s[...] = small_i[...]
            gb_s[...] = gb_i[...]
        else:
            g_s[...] = jnp.zeros_like(g_s)
            small_s[...] = jnp.zeros_like(small_s)
            gb_s[...] = jnp.zeros_like(gb_s)

    part = lambda ref, l, at, j: ref[l, :, at + 128 * j : at + 128 * j + 128]
    dvs, dps, dss, dks, dqs, dqkvs, dm1s = {}, {}, {}, {}, {}, {}, {}

    def stage_a(u):
        l, t = divmod(u, HEADS)
        j, h = t // 2, t % 2
        v, datt = part(qkv_i, l, 2 * width, j), part(datt_i, l, 0, j)
        vm = jnp.where(half_mask(v.shape, h), v, jnp.zeros_like(v))
        dps[u] = nt(vm, datt)
        dvs[u] = nn(p_i[l, t], datt)

    def stage_b(u):
        l, t = divmod(u, HEADS)
        p32 = p_i[l, t].astype(F32)
        pd = p32 * dps[u]
        dss[u] = (pd - p32 * jnp.sum(pd, axis=0, keepdims=True)).astype(BF16)

    def stage_c(u):
        l, t = divmod(u, HEADS)
        j = t // 2
        dks[u] = nn(dss[u], part(qkv_i, l, 0, j)) * 0.125
        dqs[u] = tn(dss[u], part(qkv_i, l, width, j)) * 0.125

    def stage_f(l):
        grads = [
            jnp.where(half_mask(d[u].shape, 0), d[u], d[u + 1]).astype(BF16)
            for d in (dqs, dks, dvs)
            for u in range(l * HEADS, (l + 1) * HEADS, 2)
        ]
        dqkvs[l] = jnp.concatenate(grads, axis=-1)
        dm1s[l] = nt(dqkvs[l], wq_s[...])
        g_s[...] += nn(m1_i[l].T, dqkvs[l])

    def stage_g(l):
        dqkv, dm1 = dqkvs[l], dm1s[l]
        row = pl.ds(base + step * per + l, 1)
        scale = ada[row, width : 2 * width]
        n1, rstd1 = norm_parts(tok[l].astype(F32))
        sums = jnp.sum(dqkv.astype(F32), axis=0, keepdims=True)
        gb_s[0:1, :] += sums[:, 0:width]
        gb_s[1:2, :] += sums[:, 2 * width : 3 * width]
        small_s[row, 0:width] = jnp.sum(dm1, axis=0, keepdims=True)
        small_s[row, width : 2 * width] = jnp.sum(dm1 * n1, axis=0, keepdims=True)
        gtok_o[l] = dx1_i[l] + norm_back(n1, rstd1, dm1 * (1.0 + scale))

    n = HEADS * per
    for u in range(n + 2 + 0 + 0):
        if u < n:
            stage_a(u)
        if 0 <= u - 1 < n:
            stage_b(u - 1)
        if 0 <= u - 2 < n:
            stage_c(u - 2)
        f = u - 2 - 0
        if 0 <= f < n and f % HEADS == HEADS - 1:
            stage_f(f // HEADS)
        g = f - 0
        if 0 <= g < n and g % HEADS == HEADS - 1:
            stage_g(g // HEADS)

    if last:

        @pl.when(step == pl.num_programs(0) - 1)
        def _():
            for i in range(2):
                late_o[8 * i : 8 * i + 8, :] = small_s[:, i * width : (i + 1) * width].astype(BF16)
            late_o[16:24, :] = gb_s[...].astype(BF16)
            late_o[24:32, :] = early[32:40, :]
            core = jnp.bitwise_and(info[0], 1)
            half = width // 8
            for y in range(2):
                for which, ref in enumerate((keep_o, send_o)):
                    shard = 2 * y + jnp.bitwise_xor(core, which)
                    for x in range(2):
                        take = pl.ds(pl.multiple_of(shard * 2 * half + x * half, 8), half)
                        ref[y, x] = g_s[take, :].astype(BF16)


def join(info, keep, got, *refs):
    late, outs = refs[:-4], refs[-4:]
    half, width = keep.shape[2], late[0].shape[1]
    n = late[0].shape[0]
    for k, out in enumerate(outs):
        y, x = jnp.bitwise_xor(info[1], k >> 1), jnp.bitwise_xor(info[2], k & 1)
        total = (keep[y, x].astype(F32) + got[y, x].astype(F32)).astype(BF16)
        for i in range(3):
            out[i * half : (i + 1) * half] = total[:, i * width : (i + 1) * width]
        for z, piece in enumerate(late):
            at = pl.multiple_of(3 * half + n * jnp.bitwise_xor(info[3], z), 16)
            out[pl.ds(at, n)] = piece[0:n]


def finish(info, w_late, sum_late, w_early, sum_early, few, gw, gb_ada, gb_o, gb_1, gb_2, row):
    cols, width = w_late.shape[1], few.shape[1]
    gw[:, 0:cols] = w_late[...]
    gw[:, cols:] = w_early[...]
    row[0:1, 0:cols] = sum_late[...]
    row[0:1, cols:] = sum_early[...]
    n_a, n_o, n_1 = gb_ada.shape[0], gb_o.shape[0], gb_1.shape[0]
    rest = 4 * n_1 // width
    for i in range(rest):
        row[1:2, i * width : (i + 1) * width] = few[i : i + 1]
    row[2:3, 0:width] = few[rest : rest + 1]
    row[3:4, 0:width] = few[rest + 1 : rest + 2]
    for j in range(4):

        @pl.when(info[0] == j)
        def _():
            gb_ada[...] = row[0, j * n_a : (j + 1) * n_a]
            gb_1[...] = row[1, j * n_1 : (j + 1) * n_1]
            gb_o[...] = row[2, j * n_o : (j + 1) * n_o]
            gb_2[...] = row[3, j * n_o : (j + 1) * n_o]


def tree_sum(values):
    values = [v.astype(F32) for v in values]
    while len(values) > 1:
        values = [values[2 * i] + values[2 * i + 1] for i in range(len(values) // 2)]
    return values[0]


def ordered(values, me):
    bit = 1
    while bit < len(values):
        flip = (me & bit) != 0
        values = [jnp.where(flip, values[i ^ bit], values[i]) for i in range(len(values))]
        bit *= 2
    return values


def after(values, *deps):
    flat, tree = jax.tree.flatten(values)
    out = lax.optimization_barrier(tuple(flat) + tuple(deps))
    return jax.tree.unflatten(tree, out[: len(flat)])


def full(shape):
    return pl.BlockSpec(shape, lambda *_: (0,) * len(shape))


def call(body, info, operands, specs, outs, out_specs, scratch, grid, vmem, flops, traffic, exps=0, alias=None):
    return pl.pallas_call(
        body,
        out_shape=outs,
        input_output_aliases=alias or {},
        grid_spec=pltpu.PrefetchScalarGridSpec(
            num_scalar_prefetch=1,
            grid=grid,
            in_specs=specs,
            out_specs=out_specs,
            scratch_shapes=scratch,
        ),
        compiler_params=pltpu.CompilerParams(
            dimension_semantics=("arbitrary",) * len(grid), vmem_limit_bytes=vmem << 20
        ),
        cost_estimate=pl.CostEstimate(flops=flops, bytes_accessed=traffic, transcendentals=exps),
    )(info, *operands)


def on_device(
    latent_tokens, cond, w_ada, b_ada, w_qkv, b_qv, w_o, b_o, w_1, b_1, w_2, b_2, grad_out
):
    count, length, width = latent_tokens.shape
    hidden = w_1.shape[1]
    quarter, half = width // 4, width // 8
    reps = lax.axis_size("rep")
    shards = lax.axis_size("shard")
    s = lax.axis_index("shard")
    r = lax.axis_index("rep")
    y_at, x_at, z_at = s >> 1, r & 1, r >> 1
    n_z = reps // 2
    info = jnp.stack([s, y_at, x_at, z_at]).astype(jnp.int32)

    def swap(v, shard_bits=0, rep_bits=0):
        pairs = [
            (i * shards + j, (i ^ rep_bits) * shards + (j ^ shard_bits))
            for i in range(reps)
            for j in range(shards)
        ]
        return lax.ppermute(v, ("rep", "shard"), pairs)

    whole = lambda vs: [full(v.shape) for v in vs]
    conds = [cond] + [swap(cond, k) for k in range(1, 4)]
    outs = [
        jax.ShapeDtypeStruct((quarter + quarter * hidden // width + hidden // 4, width), BF16),
    ]
    ins = (w_o, w_1, w_2)
    (ffn_w,) = call(pack, info, ins, whole(ins), outs, whole(outs), [], (1,), 60, 0, 1 << 20)
    *conds, ffn_w = after(conds + [ffn_w])
    near_qkv, far_qkv = after((w_qkv, w_qkv), *conds)
    near_qkv, far_qkv = swap(near_qkv, 1), swap(far_qkv, 2)
    near_w = swap(ffn_w, 1)
    ins = tuple(conds) + (w_ada, b_ada, b_qv, b_o, b_1, b_2)
    outs = [jax.ShapeDtypeStruct((count, 3 * width), F32)] * 4
    outs += [jax.ShapeDtypeStruct((count, 4 * width), F32)] * 4
    scratch = [pltpu.VMEM((1, 6 * width), F32), pltpu.VMEM((8, width), F32)]
    parts = call(
        ada_parts, info, ins, whole(ins), outs, whole(outs), scratch, (1,), 60, 1 << 24, 1 << 20
    )
    p_qkv = (w_qkv, near_qkv, far_qkv, swap(far_qkv, 1))
    parts, later = parts[:4], parts[4:]
    parts = [parts[0]] + [swap(parts[k], k) for k in range(1, 4)]
    *later, ffn_far = after(list(later) + [ffn_w], *parts)
    later = [later[0]] + [swap(later[k], k) for k in range(1, 4)]
    far_w = swap(ffn_far, 2)

    anyspec = pl.BlockSpec(memory_space=pl.ANY)
    dma4 = pltpu.SemaphoreType.DMA((4,))
    tokens = count * length

    per = 2
    per3 = 1
    lat = lambda *tail: pl.BlockSpec((per,) + tail, lambda i, _: (i,) + (0,) * len(tail))
    m1, qkv, probs, att, ada, table, wq_all = call(
        functools.partial(attn_fwd, per=per),
        info,
        (latent_tokens,) + tuple(parts) + p_qkv,
        [lat(length, width)] + [full(v.shape) for v in parts] + [anyspec] * 4,
        [
            jax.ShapeDtypeStruct((count, length, width), BF16),
            jax.ShapeDtypeStruct((count, length, 3 * width), BF16),
            jax.ShapeDtypeStruct((count, HEADS, length, length), BF16),
            jax.ShapeDtypeStruct((count, length, width), BF16),
            jax.ShapeDtypeStruct((count, 2 * width), F32),
            jax.ShapeDtypeStruct((4, 8, width), F32),
            jax.ShapeDtypeStruct((width, 3 * width), BF16),
        ],
        [
            lat(length, width),
            lat(length, 3 * width),
            lat(HEADS, length, length),
            lat(length, width),
            full((count, 2 * width)),
            full((4, 8, width)),
            full((width, 3 * width)),
        ],
        [pltpu.VMEM((width, 3 * width), BF16), pltpu.VMEM((1, 3 * width), F32), dma4],
        (count // per,),
        60,
        8 * tokens * width * width + 8 * tokens * length * width,
        20 * tokens * width,
        tokens * length * HEADS,
    )

    far_w, *later = after([far_w] + later, table)
    p_ffn = (ffn_w, near_w, far_w, swap(far_w, 1))

    per2 = 2 if count % 2 == 0 else 1
    lat2 = lambda *tail: pl.BlockSpec((per2,) + tail, lambda i, _: (i,) + (0,) * len(tail))
    grads = (2, 2, 9 * half, width)
    block_out, dx1, datt, early, keep_f, send_f = call(
        functools.partial(ffn_both, per=per2, chunk=hidden),
        info,
        (latent_tokens, att, grad_out, cond, table) + tuple(later) + p_ffn,
        [lat2(length, width)] * 3
        + [full(cond.shape), full(table.shape)]
        + [full(v.shape) for v in later]
        + [anyspec] * 4,
        [
            jax.ShapeDtypeStruct((count, length, width), BF16),
            jax.ShapeDtypeStruct((count, length, width), F32),
            jax.ShapeDtypeStruct((count, length, width), BF16),
            jax.ShapeDtypeStruct((48, width), BF16),
        ]
        + [jax.ShapeDtypeStruct(grads, BF16)] * 2,
        [lat2(length, width)] * 3 + [full((48, width))] + [full(grads)] * 2,
        [
            pltpu.VMEM((width, width), BF16),
            pltpu.VMEM((width, hidden), BF16),
            pltpu.VMEM((hidden, width), BF16),
            pltpu.VMEM((width, width), F32),
            pltpu.VMEM((width, hidden), F32),
            pltpu.VMEM((width, hidden), F32),
            pltpu.VMEM((8, 5 * width), F32),
            pltpu.VMEM((8, 5 * width), F32),
            pltpu.VMEM((1, width), F32),
            pltpu.VMEM((1, hidden), F32),
            pltpu.VMEM((1, width), F32),
            pltpu.VMEM((count, 4 * width), F32),
            pltpu.SemaphoreType.DMA((4 * (hidden // width + 2),)),
        ],
        (count // per2,),
        60,
        12 * tokens * width * hidden + 6 * tokens * width * width,
        14 * tokens * width,
        tokens * hidden,
    )

    def chip_sum(keep, send):
        got = swap(send, 1)

        def part(y, x):
            both = [
                lax.dynamic_index_in_dim(
                    lax.dynamic_index_in_dim(v, y, 0, keepdims=False), x, 0, keepdims=False
                ).astype(F32)
                for v in (keep, got)
            ]
            return (both[0] + both[1]).astype(BF16)

        return [part(y_at ^ (k >> 1), x_at ^ (k & 1)) for k in range(4)]

    def backward(base, last, info, extra, extra_specs, outs, out_specs, scratch, alias):
        half_n = count // 2
        at = lambda *tail: pl.BlockSpec(
            (per3,) + tail, lambda i, _: (i + base // per3,) + (0,) * len(tail)
        )
        return call(
            functools.partial(attn_bwd, per=per3, base=base, last=last),
            info,
            (latent_tokens, m1, qkv, probs, datt, dx1, ada, wq_all) + extra,
            [
                at(length, width),
                at(length, width),
                at(length, 3 * width),
                at(HEADS, length, length),
                at(length, width),
                at(length, width),
                full(ada.shape),
                full(wq_all.shape),
            ]
            + extra_specs,
            [jax.ShapeDtypeStruct((count, length, width), F32)] + outs,
            [at(length, width)] + out_specs,
            scratch,
            (half_n // per3,),
            60,
            6 * tokens * width * width + 5 * tokens * length * width,
            15 * tokens * width,
            0,
            alias,
        )

    acc = [(width, 3 * width), (8, 2 * width), (8, width)]
    acc_shapes = [jax.ShapeDtypeStruct(v, F32) for v in acc]
    acc_specs = [full(v) for v in acc]

    def over_plane(own, sends):
        return [own] + [swap(sends[k - 1], 2 * (k >> 1), k & 1) for k in range(1, 4)]

    def over_z(own, sends):
        return [own] + [swap(sends[k - 1], 0, 2 * k) for k in range(1, n_z)]

    first = x_at == 0

    def by_x(mine, yours):
        return jnp.where(first, mine, yours), jnp.where(first, yours, mine)

    def pair(v, shard_bits, rep_bits, second):
        other = swap(v, shard_bits, rep_bits)
        return jnp.concatenate(
            [jnp.where(second, other, v), jnp.where(second, v, other)], axis=0
        )

    def z_pair(v, bit):
        return pair(v, 0, 2 * bit, (z_at & bit) != 0)

    n_f, n_e = 9 * half, early.shape[0]
    parts_f = chip_sum(keep_f, send_f)

    got = over_plane(parts_f[0], parts_f[1:])
    early_y = pair(early, 2, 0, y_at == 1)
    gtok, g_half, small_half, gb_half = backward(
        0, False, after(info, *parts_f), (), [], acc_shapes, acc_specs, [], None
    )
    *got, early_y = after(got + [early_y], gb_half)
    total_f = tree_sum(got).astype(BF16)
    z_low = z_at & 3
    loads = [
        jnp.concatenate(
            [
                lax.dynamic_slice_in_dim(total_f, (z_low ^ (k & 3)) * 2 * half, 2 * half, 0),
                total_f[8 * half :],
                early_y,
            ],
            axis=0,
        )
        for k in range(n_z)
    ]

    got = over_z(loads[0], loads[1:])
    send_shape = (2, 2, half, 3 * width)
    grad_tokens, late, keep_a, send_a = backward(
        count // 2,
        True,
        after(info, *loads),
        (gtok, g_half, small_half, gb_half, early),
        [anyspec] + acc_specs + [full(early.shape)],
        [
            jax.ShapeDtypeStruct((32, width), BF16),
            jax.ShapeDtypeStruct(send_shape, BF16),
            jax.ShapeDtypeStruct(send_shape, BF16),
        ],
        [full((32, width)), full(send_shape), full(send_shape)],
        [pltpu.VMEM(v, F32) for v in acc],
        {9: 0},
    )
    *got, keep_a, send_a, late = after(got + [keep_a, send_a, late])
    early_g = jnp.concatenate(ordered([v[3 * half :] for v in got], z_at), axis=0)
    piece_f = tree_sum([v[: 2 * half] for v in got]).astype(BF16)
    out_f = tree_sum([v[2 * half : 3 * half] for v in got]).astype(BF16)

    n_l, n_e = late.shape[0], early.shape[0]
    got_a = swap(send_a, 1)
    both = jnp.concatenate([late, piece_f], axis=0)
    late_z = [late, swap(both, 0, 2)] + [swap(late, 0, 2 * k) for k in range(2, n_z)]
    early_x = pair(early_g, 0, 1, x_at == 1)
    got_a, *late_z, early_g = after([got_a] + late_z + [early_x])
    first_f = late_z[1][n_l:]

    ins = (keep_a, got_a) + tuple(late_z)
    outs = [jax.ShapeDtypeStruct((3 * half + n_z * n_l, width), BF16)] * 4
    loads = call(join, info, ins, whole(ins), outs, whole(outs), [], (1,), 16, 0, 1 << 20)
    got = over_plane(loads[0], loads[1:])
    two_f = jnp.concatenate([piece_f, first_f], axis=0)
    rest_f = swap(two_f, 0, 4)
    early_g = pair(early_g, 1, 0, (s & 1) == 1)

    contract = lambda a, b: lax.dot_general(
        a, b, (((0,), (0,)), ((), ())), preferred_element_type=F32
    )
    early_r = early_g.reshape(2, 2, n_z, 2, n_e // 8, 8, width)
    to_rows = lambda v, i: v[..., i, :, :].reshape(-1, width)
    cs_all = lax.dynamic_slice_in_dim(to_rows(early_r, 4), s * quarter, quarter, 1)
    d_early = jnp.concatenate([to_rows(early_r, i) for i in range(4)], axis=1)
    few = jnp.sum(early_r[..., 5, :, :].astype(F32), axis=(0, 1, 2, 3))
    w_early, sum_early = contract(cs_all, d_early), jnp.sum(d_early.astype(F32), axis=0)
    group_r = lax.dynamic_index_in_dim(early_r, z_at, 2, keepdims=False)
    group_r = lax.dynamic_index_in_dim(group_r, x_at, 1, keepdims=False)
    near_d = [
        group_r[:, :, i].transpose(1, 0, 2, 3).reshape(4 * count, width) for i in range(4)
    ]
    *got, two_f, rest_f, w_early, sum_early, few = after(
        got + [two_f, rest_f, w_early, sum_early, few]
    )

    total_a = tree_sum([v[: 3 * half] for v in got]).astype(BF16)
    late_g = jnp.concatenate(ordered([v[3 * half :] for v in got], 2 * y_at + x_at), axis=0)
    ring_a = over_z(total_a, [total_a] * (n_z - 1))
    blocks = [two_f[: 2 * half], two_f[2 * half :], rest_f[: 2 * half], rest_f[2 * half :]]
    mine_f = jnp.concatenate(ordered(blocks, z_low) + [out_f], axis=0)
    yours_f = swap(mine_f, 0, 1)
    late_g = pair(late_g, 1, 0, (s & 1) == 1)

    def mine(row):
        part = row.shape[0] // shards
        return lax.dynamic_slice(row, (s * part,), (part,))

    late_r = late_g.reshape(2, 2, 2, n_z, n_l // 8, 8, width)
    d_late = jnp.concatenate([to_rows(late_r, i) for i in range(2)], axis=1)
    cs_all = lax.dynamic_slice_in_dim(to_rows(late_r, 3), s * quarter, quarter, 1)
    w_late, sum_late = contract(cs_all, d_late), jnp.sum(d_late.astype(F32), axis=0)
    gb_late = mine(jnp.sum(late_r[..., 2, :2, :].astype(F32), axis=(0, 1, 2, 3)).reshape(-1))
    side_r = lax.dynamic_index_in_dim(late_r, x_at, 2, keepdims=False)
    side_r = lax.dynamic_index_in_dim(side_r, z_at, 2, keepdims=False)
    late_d = [side_r[:, :, i].transpose(1, 0, 2, 3).reshape(4 * 8, width) for i in range(2)]
    ins = (w_late, sum_late.reshape(1, -1), w_early, sum_early.reshape(1, -1), few)
    outs = [
        jax.ShapeDtypeStruct(shape, F32)
        for shape in (
            (quarter, 6 * width),
            (6 * width // 4,),
            (quarter,),
            (hidden // 4,),
            (quarter,),
        )
    ]
    gw_ada, gb_ada, gb_o, gb_1, gb_2 = call(
        finish,
        info,
        ins,
        whole(ins),
        outs,
        whole(outs),
        [pltpu.VMEM((8, 6 * width), F32)],
        (1,),
        16,
        0,
        1 << 20,
    )
    grads_b = [gb_ada, gb_late, gb_o, gb_1, gb_2]
    dada = jnp.concatenate(late_d + near_d, axis=1)
    dcs = lax.dot_general(dada, w_ada, (((1,), (1,)), ((), ())), preferred_element_type=F32)
    yours_f, gw_ada, gb_late, dcs = after((yours_f, gw_ada, gb_late, dcs))
    sides = by_x(mine_f, yours_f)
    deep = [side[: 8 * half].reshape(4, 2 * half, width) for side in sides]
    gw_1 = jnp.concatenate(
        [side[:, :half].transpose(1, 0, 2).reshape(half, hidden) for side in deep], axis=0
    ).astype(F32)
    gw_2 = jnp.concatenate(
        [side[:, half:].reshape(4 * half, width) for side in deep], axis=0
    ).T.astype(F32)
    gw_o = jnp.concatenate([side[8 * half :] for side in sides], axis=0).astype(F32)
    *ring_a, gw_1, gw_2, gw_o = after(ring_a + [gw_1, gw_2, gw_o])
    mine_a = tree_sum(ring_a).astype(BF16)
    yours_a = swap(mine_a, 0, 1)
    dcs = after(dcs, mine_a)
    dcs = ordered([dcs[k * 8 : (k + 1) * 8] for k in range(4)], s)
    dcs = ordered([dcs[0]] + [swap(dcs[k], k) for k in range(1, 4)], s)
    c32 = cond.astype(F32)
    sig = 1.0 / (1.0 + jnp.exp(-c32))
    grad_cond = jnp.concatenate(dcs, axis=1) * (sig * (1.0 + c32 * (1.0 - sig)))

    tall = jnp.concatenate(
        [v.reshape(3, half, width).transpose(1, 0, 2).reshape(half, 3 * width) for v in by_x(mine_a, yours_a)],
        axis=0,
    )
    gw_qkv = tall.astype(F32)

    return (
        block_out,
        grad_tokens,
        grad_cond,
        gw_ada,
        grads_b[0],
        gw_qkv,
        grads_b[1],
        gw_o,
        grads_b[2],
        gw_1,
        grads_b[3],
        gw_2,
        grads_b[4],
    )


def solution(mesh):
    lead = P(("rep", "shard"))
    part = P("shard")
    return jax.shard_map(
        on_device,
        mesh=mesh,
        in_specs=(lead, lead) + (part,) * 10 + (lead,),
        out_specs=(lead,) * 3 + (part,) * 10,
        check_vma=False,
    )
```

```python
import functools
import math

import jax
import jax.numpy as jnp
from jax import lax
from jax.experimental import pallas as pl
from jax.experimental.pallas import tpu as pltpu
from jax.sharding import PartitionSpec as P

HEADS = 6
F32 = jnp.float32
BF16 = jnp.bfloat16
EPS = 1e-06
GELU_C = math.sqrt(2.0 / math.pi)
GELU_A = 0.044715


def nn(a, b):
    return lax.dot_general(a, b, (((1,), (0,)), ((), ())), preferred_element_type=F32)


def nt(a, b):
    return lax.dot_general(a, b, (((1,), (1,)), ((), ())), preferred_element_type=F32)


def tn(a, b):
    return lax.dot_general(a, b, (((0,), (0,)), ((), ())), preferred_element_type=F32)


def norm_parts(x):
    centred = x - jnp.mean(x, axis=-1, keepdims=True)
    rstd = lax.rsqrt(jnp.mean(centred * centred, axis=-1, keepdims=True) + EPS)
    return centred * rstd, rstd


def norm_back(normed, rstd, grad):
    inner = jnp.mean(grad, axis=-1, keepdims=True)
    along = jnp.mean(grad * normed, axis=-1, keepdims=True)
    return rstd * (grad - inner - normed * along)


def piece_copies(mine, pieces, whole, sems):
    rows = pieces[0].shape[0]
    return [
        pltpu.make_async_copy(
            piece,
            whole.at[pl.ds(pl.multiple_of(jnp.bitwise_xor(mine, k) * rows, 32), rows)],
            sems.at[k],
        )
        for k, piece in enumerate(pieces)
    ]


def half_mask(shape, half):
    lane = lax.broadcasted_iota(jnp.int32, shape, len(shape) - 1)
    return (lane < shape[-1] // 2) if half == 0 else (lane >= shape[-1] // 2)


def pack(info, w_o, w_1, w_2, tall):
    rows, width = w_o.shape
    tall[0:rows] = w_o[...]
    many = w_1.shape[1] // width
    for i in range(many):
        tall[(1 + i) * rows : (2 + i) * rows] = w_1[:, i * width : (i + 1) * width]
    tall[(1 + many) * rows :] = w_2[...]


def ada_parts(info, c0, c1, c2, c3, w_ada, b_ada, b_qv, b_o, b_1, b_2, *refs):
    outs, share, packed = refs[0:8], refs[8], refs[9]
    share[...] = jnp.zeros_like(share)
    packed[...] = jnp.zeros_like(packed)
    n = b_ada.shape[0]
    row = b_ada[...].astype(F32).reshape(1, n)
    for j in range(4):

        @pl.when(info[0] == j)
        def _():
            share[:, j * n : (j + 1) * n] = row

    for i, b in enumerate((b_qv, b_o, b_1, b_2)):
        packed[i : i + 1, 0 : b.shape[0]] = b[...].astype(F32).reshape(1, b.shape[0])
    m = w_ada.shape[1] // 3
    for cond, first, rest in zip((c0, c1, c2, c3), outs[0:4], outs[4:8]):
        c = cond[...].astype(F32)
        cs = c / (1.0 + jnp.exp(-c))
        cut = cs.shape[1] // 4
        mine = sum(
            jnp.where(info[0] == j, cs[:, j * cut : (j + 1) * cut], 0.0) for j in range(4)
        ).astype(BF16)
        part = nn(mine, w_ada[...]) + share[...]
        first[:, 0:m] = part[:, 0:m]
        first[:, m:] = packed[...]
        rest[...] = part[:, m:]


def bias_row(table, at, n):
    return jnp.concatenate([table[i, at : at + 1, 0:n] for i in range(4)], axis=1)


def attn_fwd(info, tok, *refs, per):
    parts, wq = refs[0:4], refs[4:8]
    m1_o, qkv_o, p_o, att_o, ada, table, wq_o = refs[8:15]
    wq_s, bias_s, sem_q = refs[15:]
    step = pl.program_id(0)
    width = tok.shape[-1]

    @pl.when(step == 0)
    def _():
        cq = piece_copies(info[0], wq, wq_s, sem_q)
        for copy in cq:
            copy.start()
        ada[...] = sum(v[:, 0 : 2 * width] for v in parts)
        for k in range(4):
            table[jnp.bitwise_xor(info[0], k)] = parts[k][:, 2 * width :]
        row_qv = bias_row(table, 0, width // 2)
        bias_s[:, 0:width] = row_qv[:, 0:width]
        bias_s[:, width : 2 * width] = jnp.zeros((1, width), F32)
        bias_s[:, 2 * width : 3 * width] = row_qv[:, width : 2 * width]
        for copy in cq:
            copy.wait()
        wq_o[...] = wq_s[...]

    qkvs, ss, ps, atts = {}, {}, {}, {}
    part = lambda l, at, j: qkvs[l][:, at + 128 * j : at + 128 * j + 128]

    def stage_q(l):
        row = pl.ds(step * per + l, 1)
        shift = ada[row, 0:width]
        scale = ada[row, width : 2 * width]
        n1, _ = norm_parts(tok[l].astype(F32))
        m1 = (n1 * (1.0 + scale) + shift).astype(BF16)
        m1_o[l] = m1
        qkvs[l] = (nn(m1, wq_s[...]) + bias_s[...]).astype(BF16)
        qkv_o[l] = qkvs[l]

    def stage_a(u):
        l, t = divmod(u, HEADS)
        j, h = t // 2, t % 2
        k = part(l, width, j)
        ss[u] = nt(jnp.where(half_mask(k.shape, h), k, jnp.zeros_like(k)), part(l, 0, j))

    def stage_b(u):
        l, t = divmod(u, HEADS)
        s = ss[u]
        top = jnp.max(s, axis=0, keepdims=True)
        e = jnp.exp((s - top) * 0.125)
        total = jnp.sum(e, axis=0, keepdims=True)
        ps[u] = (e * (1.0 / total)).astype(BF16)
        p_o[l, t] = ps[u]

    def stage_c(u):
        l, t = divmod(u, HEADS)
        j = t // 2
        atts[u] = tn(ps[u], part(l, 2 * width, j))
        if t % 2:
            att = jnp.where(half_mask(atts[u].shape, 0), atts[u - 1], atts[u])
            att_o[l, :, 128 * j : 128 * j + 128] = att.astype(BF16)

    n = HEADS * per
    stage_q(0)
    for u in range(n + 2):
        if u < n:
            stage_a(u)
        if u % HEADS == 1 and u // HEADS + 1 < per:
            stage_q(u // HEADS + 1)
        if 0 <= u - 1 < n:
            stage_b(u - 1)
        if 0 <= u - 2 < n:
            stage_c(u - 2)


def ffn_both(info, tok, att_i, dy_i, cond, table, *refs, per, chunk):
    ada_parts, pieces = refs[0:4], refs[4:8]
    out_o, dx1_o, datt_o, early_o, cs_o, keep_o, send_o = refs[8:15]
    wo_s, w1_s, w2_s, go_s, g1_s, g2_s, small_s, gb_s, bo_s, b1_s, b2_s, ada, sems = refs[15:]
    step = pl.program_id(0)
    length, width = tok.shape[1:]
    hidden = w1_s.shape[1]

    @pl.when(step == 0)
    def _():
        copies, n, rows = [], hidden // width + 2, width // 4
        for k, piece in enumerate(pieces):
            at = pl.multiple_of(jnp.bitwise_xor(info[0], k) * rows, 32)
            at2 = pl.multiple_of(jnp.bitwise_xor(info[0], k) * (hidden // 4), 32)
            places = [wo_s.at[pl.ds(at, rows)]]
            places += [
                w1_s.at[pl.ds(at, rows), i * width : (i + 1) * width] for i in range(n - 2)
            ]
            places += [w2_s.at[pl.ds(at2, hidden // 4)]]
            start = 0
            for i, place in enumerate(places):
                source = piece.at[start : start + place.shape[0]]
                copies.append(pltpu.make_async_copy(source, place, sems.at[n * k + i]))
                start += place.shape[0]
        for copy in copies:
            copy.start()
        go_s[...] = jnp.zeros_like(go_s)
        g1_s[...] = jnp.zeros_like(g1_s)
        g2_s[...] = jnp.zeros_like(g2_s)
        gb_s[...] = jnp.zeros_like(gb_s)
        ada[...] = sum(v[...] for v in ada_parts)
        bo_s[...] = bias_row(table, 1, width // 4)
        b1_s[...] = bias_row(table, 2, hidden // 4)
        b2_s[...] = bias_row(table, 3, width // 4)
        c = cond[...].astype(F32)
        cs_o[...] = (c / (1.0 + jnp.exp(-c))).astype(BF16)
        for copy in copies:
            copy.wait()

    def rows_of(at):
        return jnp.stack(
            [ada[pl.ds(step * per + l, 1), at * width : (at + 1) * width] for l in range(per)]
        )

    def flat(v):
        return v.reshape(per * length, v.shape[-1])

    def deep(v):
        return v.reshape(per, length, v.shape[-1])

    gate1, shift2, scale2, gate2 = rows_of(0), rows_of(1), rows_of(2), rows_of(3)
    att = flat(att_i[...])
    branch = deep(nn(att, wo_s[...]) + bo_s[...])
    x1 = tok[...].astype(F32) + gate1 * branch
    n2, rstd2 = norm_parts(x1)
    m2 = flat((n2 * (1.0 + scale2) + shift2).astype(BF16))
    dy = dy_i[...].astype(F32)
    df = flat((dy * gate2).astype(BF16))
    df_t = df.T
    m2_t = m2.T
    ffn = None
    dm2 = None
    for j in range(hidden // chunk):
        cols = slice(j * chunk, (j + 1) * chunk)
        h = nn(m2, w1_s[:, cols]) + b1_s[:, cols]
        hh = h * h
        u = h * (GELU_C + (GELU_C * GELU_A) * hh)
        half_t = 0.5 + 0.5 * jnp.tanh(u)
        g = (h * half_t).astype(BF16)
        slope = half_t * (1.0 + (1.0 - half_t) * (6.0 * u - (4.0 * GELU_C) * h))
        part = nn(g, w2_s[cols, :])
        ffn = part if ffn is None else ffn + part
        g2_s[:, cols] += nn(df_t, g)
        dh32 = nt(df, w2_s[cols, :]) * slope
        dh = dh32.astype(BF16)
        gb_s[0:1, cols] += jnp.sum(dh.astype(F32), axis=0, keepdims=True)
        g1_s[:, cols] += nn(m2_t, dh)
        part = nt(dh, w1_s[:, cols])
        dm2 = part if dm2 is None else dm2 + part
    ffn = deep(ffn + b2_s[...])
    dm2 = deep(dm2)
    out_o[...] = (x1 + gate2 * ffn).astype(BF16)
    gb_s[1:2, width : 2 * width] += jnp.sum(df.astype(F32), axis=0, keepdims=True)
    d_gate2 = jnp.sum(dy * ffn, axis=1)
    d_scale2 = jnp.sum(dm2 * n2, axis=1)
    d_shift2 = jnp.sum(dm2, axis=1)
    dx1 = dy + norm_back(n2, rstd2, dm2 * (1.0 + scale2))
    dx1_o[...] = dx1
    do = flat((dx1 * gate1).astype(BF16))
    d_gate1 = jnp.sum(dx1 * branch, axis=1)
    for l in range(per):
        row = pl.ds(step * per + l, 1)
        small_s[row, 0:width] = d_gate1[l : l + 1]
        small_s[row, width : 2 * width] = d_shift2[l : l + 1]
        small_s[row, 2 * width : 3 * width] = d_scale2[l : l + 1]
        small_s[row, 3 * width : 4 * width] = d_gate2[l : l + 1]
    gb_s[1:2, 0:width] += jnp.sum(do.astype(F32), axis=0, keepdims=True)
    go_s[...] += tn(att, do)
    datt_o[...] = deep(nt(do, wo_s[...]).astype(BF16))

    @pl.when(step == pl.num_programs(0) - 1)
    def _():
        for i in range(4):
            early_o[8 * i : 8 * i + 8, :] = small_s[:, i * width : (i + 1) * width].astype(BF16)
        pack = [gb_s[0:1, i * width : (i + 1) * width] for i in range(hidden // width)]
        pack += [gb_s[1:2, 0:width], gb_s[1:2, width : 2 * width]]
        pack += [jnp.zeros((1, width), F32)] * (8 - len(pack))
        early_o[32:40, :] = jnp.concatenate(pack, axis=0).astype(BF16)
        core = jnp.bitwise_and(info[0], 1)
        half = width // 8
        for y in range(2):
            for which, ref in enumerate((keep_o, send_o)):
                shard = 2 * y + jnp.bitwise_xor(core, which)
                for x in range(2):
                    take = pl.ds(pl.multiple_of(shard * 2 * half + x * half, 8), half)
                    wide = pl.ds(pl.multiple_of(shard * width, 128), width)
                    for z in range(4):
                        at = 2 * half * z
                        ref[y, x, at : at + half, :] = g1_s[
                            take, z * width : (z + 1) * width
                        ].astype(BF16)
                        rows = slice((4 * x + z) * half, (4 * x + z + 1) * half)
                        ref[y, x, at + half : at + 2 * half, :] = g2_s[rows, wide].astype(BF16)
                    ref[y, x, 8 * half : 9 * half, :] = go_s[take, :].astype(BF16)


def attn_bwd(info, tok, m1_i, qkv_i, p_i, datt_i, dx1_i, ada, wq_s, *refs, per, base, last):
    step = pl.program_id(0)
    length, width = tok.shape[1:]
    if last:
        _, g_i, small_i, gb_i, cs = refs[0:5]
        gtok_o, late_o, keep_o, send_o = refs[5:9]
        g_s, small_s, gb_s = refs[9:]
    else:
        gtok_o, g_s, small_s, gb_s = refs

    @pl.when(step == 0)
    def _():
        if last:
            g_s[...] = g_i[...]
            small_s[...] = small_i[...]
            gb_s[...] = gb_i[...]
        else:
            g_s[...] = jnp.zeros_like(g_s)
            small_s[...] = jnp.zeros_like(small_s)
            gb_s[...] = jnp.zeros_like(gb_s)

    part = lambda ref, l, at, j: ref[l, :, at + 128 * j : at + 128 * j + 128]
    dvs, dps, dss, dks, dqs, dqkvs, dm1s = {}, {}, {}, {}, {}, {}, {}

    def stage_a(u):
        l, t = divmod(u, HEADS)
        j, h = t // 2, t % 2
        v, datt = part(qkv_i, l, 2 * width, j), part(datt_i, l, 0, j)
        vm = jnp.where(half_mask(v.shape, h), v, jnp.zeros_like(v))
        dps[u] = nt(vm, datt)
        dvs[u] = nn(p_i[l, t], datt)

    def stage_b(u):
        l, t = divmod(u, HEADS)
        p32 = p_i[l, t].astype(F32)
        pd = p32 * dps[u]
        dss[u] = (pd - p32 * jnp.sum(pd, axis=0, keepdims=True)).astype(BF16)

    def stage_c(u):
        l, t = divmod(u, HEADS)
        j = t // 2
        dks[u] = nn(dss[u], part(qkv_i, l, 0, j)) * 0.125
        dqs[u] = tn(dss[u], part(qkv_i, l, width, j)) * 0.125

    def stage_f(l):
        grads = [
            jnp.where(half_mask(d[u].shape, 0), d[u], d[u + 1]).astype(BF16)
            for d in (dqs, dks, dvs)
            for u in range(l * HEADS, (l + 1) * HEADS, 2)
        ]
        dqkvs[l] = jnp.concatenate(grads, axis=-1)
        dm1s[l] = nt(dqkvs[l], wq_s[...])
        g_s[...] += nn(m1_i[l].T, dqkvs[l])

    def stage_g(l):
        dqkv, dm1 = dqkvs[l], dm1s[l]
        row = pl.ds(base + step * per + l, 1)
        scale = ada[row, width : 2 * width]
        n1, rstd1 = norm_parts(tok[l].astype(F32))
        sums = jnp.sum(dqkv.astype(F32), axis=0, keepdims=True)
        gb_s[0:1, :] += sums[:, 0:width]
        gb_s[1:2, :] += sums[:, 2 * width : 3 * width]
        small_s[row, 0:width] = jnp.sum(dm1, axis=0, keepdims=True)
        small_s[row, width : 2 * width] = jnp.sum(dm1 * n1, axis=0, keepdims=True)
        gtok_o[l] = dx1_i[l] + norm_back(n1, rstd1, dm1 * (1.0 + scale))

    n = HEADS * per
    for u in range(n + 2 + 0 + 0):
        if u < n:
            stage_a(u)
        if 0 <= u - 1 < n:
            stage_b(u - 1)
        if 0 <= u - 2 < n:
            stage_c(u - 2)
        f = u - 2 - 0
        if 0 <= f < n and f % HEADS == HEADS - 1:
            stage_f(f // HEADS)
        g = f - 0
        if 0 <= g < n and g % HEADS == HEADS - 1:
            stage_g(g // HEADS)

    if last:

        @pl.when(step == pl.num_programs(0) - 1)
        def _():
            for i in range(2):
                late_o[8 * i : 8 * i + 8, :] = small_s[:, i * width : (i + 1) * width].astype(BF16)
            late_o[16:24, :] = gb_s[...].astype(BF16)
            late_o[24:32, :] = cs[...]
            core = jnp.bitwise_and(info[0], 1)
            half = width // 8
            for y in range(2):
                for which, ref in enumerate((keep_o, send_o)):
                    shard = 2 * y + jnp.bitwise_xor(core, which)
                    for x in range(2):
                        take = pl.ds(pl.multiple_of(shard * 2 * half + x * half, 8), half)
                        ref[y, x] = g_s[take, :].astype(BF16)


def join(info, keep, got, *refs):
    late, outs = refs[:-4], refs[-4:]
    half, width = keep.shape[2], late[0].shape[1]
    n = late[0].shape[0]
    for k, out in enumerate(outs):
        y, x = jnp.bitwise_xor(info[1], k >> 1), jnp.bitwise_xor(info[2], k & 1)
        total = (keep[y, x].astype(F32) + got[y, x].astype(F32)).astype(BF16)
        for i in range(3):
            out[i * half : (i + 1) * half] = total[:, i * width : (i + 1) * width]
        for z, piece in enumerate(late):
            at = pl.multiple_of(3 * half + n * jnp.bitwise_xor(info[3], z), 16)
            out[pl.ds(at, n)] = piece[0:n]


def finish(info, w_late, sum_late, w_early, sum_early, few, gw, gb_ada, gb_o, gb_1, gb_2, row):
    cols, width = w_late.shape[1], few.shape[1]
    gw[:, 0:cols] = w_late[...]
    gw[:, cols:] = w_early[...]
    row[0:1, 0:cols] = sum_late[...]
    row[0:1, cols:] = sum_early[...]
    n_a, n_o, n_1 = gb_ada.shape[0], gb_o.shape[0], gb_1.shape[0]
    rest = 4 * n_1 // width
    for i in range(rest):
        row[1:2, i * width : (i + 1) * width] = few[i : i + 1]
    row[2:3, 0:width] = few[rest : rest + 1]
    row[3:4, 0:width] = few[rest + 1 : rest + 2]
    for j in range(4):

        @pl.when(info[0] == j)
        def _():
            gb_ada[...] = row[0, j * n_a : (j + 1) * n_a]
            gb_1[...] = row[1, j * n_1 : (j + 1) * n_1]
            gb_o[...] = row[2, j * n_o : (j + 1) * n_o]
            gb_2[...] = row[3, j * n_o : (j + 1) * n_o]


def tree_sum(values):
    values = [v.astype(F32) for v in values]
    while len(values) > 1:
        values = [values[2 * i] + values[2 * i + 1] for i in range(len(values) // 2)]
    return values[0]


def ordered(values, me):
    bit = 1
    while bit < len(values):
        flip = (me & bit) != 0
        values = [jnp.where(flip, values[i ^ bit], values[i]) for i in range(len(values))]
        bit *= 2
    return values


def after(values, *deps):
    flat, tree = jax.tree.flatten(values)
    out = lax.optimization_barrier(tuple(flat) + tuple(deps))
    return jax.tree.unflatten(tree, out[: len(flat)])


def full(shape):
    return pl.BlockSpec(shape, lambda *_: (0,) * len(shape))


def call(body, info, operands, specs, outs, out_specs, scratch, grid, vmem, flops, traffic, exps=0, alias=None):
    return pl.pallas_call(
        body,
        out_shape=outs,
        input_output_aliases=alias or {},
        grid_spec=pltpu.PrefetchScalarGridSpec(
            num_scalar_prefetch=1,
            grid=grid,
            in_specs=specs,
            out_specs=out_specs,
            scratch_shapes=scratch,
        ),
        compiler_params=pltpu.CompilerParams(
            dimension_semantics=("arbitrary",) * len(grid), vmem_limit_bytes=vmem << 20
        ),
        cost_estimate=pl.CostEstimate(flops=flops, bytes_accessed=traffic, transcendentals=exps),
    )(info, *operands)


def on_device(
    latent_tokens, cond, w_ada, b_ada, w_qkv, b_qv, w_o, b_o, w_1, b_1, w_2, b_2, grad_out
):
    count, length, width = latent_tokens.shape
    hidden = w_1.shape[1]
    quarter, half = width // 4, width // 8
    reps = lax.axis_size("rep")
    shards = lax.axis_size("shard")
    s = lax.axis_index("shard")
    r = lax.axis_index("rep")
    y_at, x_at, z_at = s >> 1, r & 1, r >> 1
    n_z = reps // 2
    info = jnp.stack([s, y_at, x_at, z_at]).astype(jnp.int32)

    def swap(v, shard_bits=0, rep_bits=0):
        pairs = [
            (i * shards + j, (i ^ rep_bits) * shards + (j ^ shard_bits))
            for i in range(reps)
            for j in range(shards)
        ]
        return lax.ppermute(v, ("rep", "shard"), pairs)

    whole = lambda vs: [full(v.shape) for v in vs]
    conds = [cond] + [swap(cond, k) for k in range(1, 4)]
    ins = tuple(conds) + (w_ada, b_ada, b_qv, b_o, b_1, b_2)
    outs = [jax.ShapeDtypeStruct((count, 3 * width), F32)] * 4
    outs += [jax.ShapeDtypeStruct((count, 4 * width), F32)] * 4
    scratch = [pltpu.VMEM((1, 6 * width), F32), pltpu.VMEM((8, width), F32)]
    parts = call(
        ada_parts, info, ins, whole(ins), outs, whole(outs), scratch, (1,), 60, 1 << 24, 1 << 20
    )
    near_qkv, far_qkv = after((w_qkv, w_qkv), *conds)
    near_qkv, far_qkv = swap(near_qkv, 1), swap(far_qkv, 2)
    p_qkv = (w_qkv, near_qkv, far_qkv, swap(far_qkv, 1))
    tall = quarter + quarter * hidden // width + hidden // 4
    ins = after((w_o, w_1, w_2), parts[0])
    outs = [jax.ShapeDtypeStruct((tall, width), BF16)]
    (ffn_w,) = call(pack, info, ins, whole(ins), outs, whole(outs), [], (1,), 60, 0, 1 << 20)
    near_w = swap(ffn_w, 1)
    parts, later = parts[:4], parts[4:]
    parts = [parts[0]] + [swap(parts[k], k) for k in range(1, 4)]
    *later, ffn_far = after(list(later) + [ffn_w], *parts)
    later = [later[0]] + [swap(later[k], k) for k in range(1, 4)]
    far_w = swap(ffn_far, 2)

    anyspec = pl.BlockSpec(memory_space=pl.ANY)
    dma4 = pltpu.SemaphoreType.DMA((4,))
    tokens = count * length

    per = 2
    per3 = 1
    lat = lambda *tail: pl.BlockSpec((per,) + tail, lambda i, _: (i,) + (0,) * len(tail))
    m1, qkv, probs, att, ada, table, wq_all = call(
        functools.partial(attn_fwd, per=per),
        info,
        (latent_tokens,) + tuple(parts) + p_qkv,
        [lat(length, width)] + [full(v.shape) for v in parts] + [anyspec] * 4,
        [
            jax.ShapeDtypeStruct((count, length, width), BF16),
            jax.ShapeDtypeStruct((count, length, 3 * width), BF16),
            jax.ShapeDtypeStruct((count, HEADS, length, length), BF16),
            jax.ShapeDtypeStruct((count, length, width), BF16),
            jax.ShapeDtypeStruct((count, 2 * width), F32),
            jax.ShapeDtypeStruct((4, 8, width), F32),
            jax.ShapeDtypeStruct((width, 3 * width), BF16),
        ],
        [
            lat(length, width),
            lat(length, 3 * width),
            lat(HEADS, length, length),
            lat(length, width),
            full((count, 2 * width)),
            full((4, 8, width)),
            full((width, 3 * width)),
        ],
        [pltpu.VMEM((width, 3 * width), BF16), pltpu.VMEM((1, 3 * width), F32), dma4],
        (count // per,),
        60,
        8 * tokens * width * width + 8 * tokens * length * width,
        20 * tokens * width,
        tokens * length * HEADS,
    )

    far_w, *later = after([far_w] + later, table)
    p_ffn = (ffn_w, near_w, far_w, swap(far_w, 1))

    per2 = 2 if count % 2 == 0 else 1
    lat2 = lambda *tail: pl.BlockSpec((per2,) + tail, lambda i, _: (i,) + (0,) * len(tail))
    grads = (2, 2, 9 * half, width)
    block_out, dx1, datt, early, cs_own, keep_f, send_f = call(
        functools.partial(ffn_both, per=per2, chunk=hidden),
        info,
        (latent_tokens, att, grad_out, cond, table) + tuple(later) + p_ffn,
        [lat2(length, width)] * 3
        + [full(cond.shape), full(table.shape)]
        + [full(v.shape) for v in later]
        + [anyspec] * 4,
        [
            jax.ShapeDtypeStruct((count, length, width), BF16),
            jax.ShapeDtypeStruct((count, length, width), F32),
            jax.ShapeDtypeStruct((count, length, width), BF16),
            jax.ShapeDtypeStruct((40, width), BF16),
            jax.ShapeDtypeStruct((count, width), BF16),
        ]
        + [jax.ShapeDtypeStruct(grads, BF16)] * 2,
        [lat2(length, width)] * 3 + [full((40, width)), full((count, width))] + [full(grads)] * 2,
        [
            pltpu.VMEM((width, width), BF16),
            pltpu.VMEM((width, hidden), BF16),
            pltpu.VMEM((hidden, width), BF16),
            pltpu.VMEM((width, width), F32),
            pltpu.VMEM((width, hidden), F32),
            pltpu.VMEM((width, hidden), F32),
            pltpu.VMEM((8, 4 * width), F32),
            pltpu.VMEM((8, 5 * width), F32),
            pltpu.VMEM((1, width), F32),
            pltpu.VMEM((1, hidden), F32),
            pltpu.VMEM((1, width), F32),
            pltpu.VMEM((count, 4 * width), F32),
            pltpu.SemaphoreType.DMA((4 * (hidden // width + 2),)),
        ],
        (count // per2,),
        60,
        12 * tokens * width * hidden + 6 * tokens * width * width,
        14 * tokens * width,
        tokens * hidden,
    )

    def chip_sum(keep, send):
        got = swap(send, 1)

        def part(y, x):
            both = [
                lax.dynamic_index_in_dim(
                    lax.dynamic_index_in_dim(v, y, 0, keepdims=False), x, 0, keepdims=False
                ).astype(F32)
                for v in (keep, got)
            ]
            return (both[0] + both[1]).astype(BF16)

        return [part(y_at ^ (k >> 1), x_at ^ (k & 1)) for k in range(4)]

    def backward(base, last, info, extra, extra_specs, outs, out_specs, scratch, alias):
        half_n = count // 2
        at = lambda *tail: pl.BlockSpec(
            (per3,) + tail, lambda i, _: (i + base // per3,) + (0,) * len(tail)
        )
        return call(
            functools.partial(attn_bwd, per=per3, base=base, last=last),
            info,
            (latent_tokens, m1, qkv, probs, datt, dx1, ada, wq_all) + extra,
            [
                at(length, width),
                at(length, width),
                at(length, 3 * width),
                at(HEADS, length, length),
                at(length, width),
                at(length, width),
                full(ada.shape),
                full(wq_all.shape),
            ]
            + extra_specs,
            [jax.ShapeDtypeStruct((count, length, width), F32)] + outs,
            [at(length, width)] + out_specs,
            scratch,
            (half_n // per3,),
            60,
            6 * tokens * width * width + 5 * tokens * length * width,
            15 * tokens * width,
            0,
            alias,
        )

    acc = [(width, 3 * width), (8, 2 * width), (8, width)]
    acc_shapes = [jax.ShapeDtypeStruct(v, F32) for v in acc]
    acc_specs = [full(v) for v in acc]

    def over_plane(own, sends):
        return [own] + [swap(sends[k - 1], 2 * (k >> 1), k & 1) for k in range(1, 4)]

    z_order = sorted(range(1, n_z), key=lambda k: (k & 3) % 3 if k & 3 else 4)

    def over_z(own, sends):
        got = {k: swap(sends[k - 1], 0, 2 * k) for k in z_order}
        return [own] + [got[k] for k in range(1, n_z)]

    first = x_at == 0

    def by_x(mine, yours):
        return jnp.where(first, mine, yours), jnp.where(first, yours, mine)

    def pair(v, shard_bits, rep_bits, second):
        other = swap(v, shard_bits, rep_bits)
        return jnp.concatenate(
            [jnp.where(second, other, v), jnp.where(second, v, other)], axis=0
        )

    def z_pair(v, bit):
        return pair(v, 0, 2 * bit, (z_at & bit) != 0)

    n_f, n_e = 9 * half, early.shape[0]
    parts_f = chip_sum(keep_f, send_f)

    got = over_plane(parts_f[0], parts_f[1:])
    early_y = pair(early, 2, 0, y_at == 1)
    gtok, g_half, small_half, gb_half = backward(
        0, False, after(info, *parts_f), (), [], acc_shapes, acc_specs, [], None
    )
    *got, early_y = after(got + [early_y], gb_half)
    total_f = tree_sum(got).astype(BF16)
    z_low = z_at & 3
    loads = [
        jnp.concatenate(
            [
                lax.dynamic_slice_in_dim(total_f, (z_low ^ (k & 3)) * 2 * half, 2 * half, 0),
                total_f[8 * half :],
                early_y,
            ],
            axis=0,
        )
        for k in range(n_z)
    ]

    got = over_z(loads[0], loads[1:])
    send_shape = (2, 2, half, 3 * width)
    grad_tokens, late, keep_a, send_a = backward(
        count // 2,
        True,
        after(info, *loads),
        (gtok, g_half, small_half, gb_half, cs_own),
        [anyspec] + acc_specs + [full(cs_own.shape)],
        [
            jax.ShapeDtypeStruct((32, width), BF16),
            jax.ShapeDtypeStruct(send_shape, BF16),
            jax.ShapeDtypeStruct(send_shape, BF16),
        ],
        [full((32, width)), full(send_shape), full(send_shape)],
        [pltpu.VMEM(v, F32) for v in acc],
        {9: 0},
    )
    *got, keep_a, send_a, late = after(got + [keep_a, send_a, late])
    early_g = jnp.concatenate(ordered([v[3 * half :] for v in got], z_at), axis=0)
    piece_f = tree_sum([v[: 2 * half] for v in got]).astype(BF16)
    out_f = tree_sum([v[2 * half : 3 * half] for v in got]).astype(BF16)

    n_l, n_e = late.shape[0], early.shape[0]
    got_a = swap(send_a, 1)
    both = jnp.concatenate([late, piece_f], axis=0)
    late_z = over_z(late, [both] + [late] * (n_z - 2))
    got_a, *late_z, early_g = after([got_a] + late_z + [early_g])
    first_f = late_z[1][n_l:]

    ins = (keep_a, got_a) + tuple(late_z)
    outs = [jax.ShapeDtypeStruct((3 * half + n_z * n_l, width), BF16)] * 4
    loads = call(join, info, ins, whole(ins), outs, whole(outs), [], (1,), 16, 0, 1 << 20)
    got = over_plane(loads[0], loads[1:])
    two_f = jnp.concatenate([piece_f, first_f], axis=0)
    rest_f = swap(two_f, 0, 4)
    early_g = pair(early_g, 0, 1, x_at == 1)
    *got, two_f, rest_f, early_g = after(got + [two_f, rest_f, early_g])

    total_a = tree_sum([v[: 3 * half] for v in got]).astype(BF16)
    late_g = jnp.concatenate(ordered([v[3 * half :] for v in got], 2 * y_at + x_at), axis=0)
    ring_a = over_z(total_a, [total_a] * (n_z - 1))
    blocks = [two_f[: 2 * half], two_f[2 * half :], rest_f[: 2 * half], rest_f[2 * half :]]
    mine_f = jnp.concatenate(ordered(blocks, z_low) + [out_f], axis=0)
    yours_f = swap(mine_f, 0, 1)
    n_rows = late_g.shape[0]
    both_g = pair(jnp.concatenate([late_g, early_g], axis=0), 1, 0, (s & 1) == 1)
    both_g = both_g.reshape(2, -1, width)
    late_g, early_g = both_g[:, :n_rows], both_g[:, n_rows:]

    def mine(row):
        part = row.shape[0] // shards
        return lax.dynamic_slice(row, (s * part,), (part,))

    contract = lambda a, b: lax.dot_general(
        a, b, (((0,), (0,)), ((), ())), preferred_element_type=F32
    )
    early_r = early_g.reshape(2, 2, n_z, 2, n_e // 8, 8, width)
    to_rows = lambda v, i: v[..., i, :, :].reshape(-1, width)
    late_r = late_g.reshape(2, 2, 2, n_z, n_l // 8, 8, width)
    cs_all = lax.dynamic_slice_in_dim(to_rows(late_r, 3), s * quarter, quarter, 1)
    cs_turned = cs_all.reshape(2, 2, 2, n_z, 8, quarter).transpose(0, 2, 3, 1, 4, 5)
    d_early = jnp.concatenate([to_rows(early_r, i) for i in range(4)], axis=1)
    few = jnp.sum(early_r[..., 4, :, :].astype(F32), axis=(0, 1, 2, 3))
    w_early, sum_early = contract(cs_turned.reshape(-1, quarter), d_early), jnp.sum(d_early.astype(F32), axis=0)
    group_r = lax.dynamic_index_in_dim(early_r, z_at, 2, keepdims=False)
    group_r = lax.dynamic_index_in_dim(group_r, x_at, 1, keepdims=False)
    near_d = [
        group_r[:, :, i].transpose(1, 0, 2, 3).reshape(4 * count, width) for i in range(4)
    ]
    d_late = jnp.concatenate([to_rows(late_r, i) for i in range(2)], axis=1)
    w_late, sum_late = contract(cs_all, d_late), jnp.sum(d_late.astype(F32), axis=0)
    gb_late = mine(jnp.sum(late_r[..., 2, :2, :].astype(F32), axis=(0, 1, 2, 3)).reshape(-1))
    side_r = lax.dynamic_index_in_dim(late_r, x_at, 2, keepdims=False)
    side_r = lax.dynamic_index_in_dim(side_r, z_at, 2, keepdims=False)
    late_d = [side_r[:, :, i].transpose(1, 0, 2, 3).reshape(4 * 8, width) for i in range(2)]
    ins = (w_late, sum_late.reshape(1, -1), w_early, sum_early.reshape(1, -1), few)
    outs = [
        jax.ShapeDtypeStruct(shape, F32)
        for shape in (
            (quarter, 6 * width),
            (6 * width // 4,),
            (quarter,),
            (hidden // 4,),
            (quarter,),
        )
    ]
    gw_ada, gb_ada, gb_o, gb_1, gb_2 = call(
        finish,
        info,
        ins,
        whole(ins),
        outs,
        whole(outs),
        [pltpu.VMEM((8, 6 * width), F32)],
        (1,),
        16,
        0,
        1 << 20,
    )
    grads_b = [gb_ada, gb_late, gb_o, gb_1, gb_2]
    dada = jnp.concatenate(late_d + near_d, axis=1)
    dcs = lax.dot_general(dada, w_ada, (((1,), (1,)), ((), ())), preferred_element_type=F32)
    mine_d, send_d = ordered([dcs[: 2 * count], dcs[2 * count :]], y_at)
    far_d = swap(send_d, 2)
    yours_f, gw_ada, gb_late, far_d = after((yours_f, gw_ada, gb_late, far_d))
    *ring_a, yours_f = after(ring_a + [yours_f])
    sides = by_x(mine_f, yours_f)
    deep = [side[: 8 * half].reshape(4, 2 * half, width) for side in sides]
    gw_1 = jnp.concatenate(
        [side[:, :half].transpose(1, 0, 2).reshape(half, hidden) for side in deep], axis=0
    ).astype(F32)
    gw_2 = jnp.concatenate(
        [side[:, half:].reshape(4 * half, width) for side in deep], axis=0
    ).T.astype(F32)
    gw_o = jnp.concatenate([side[8 * half :] for side in sides], axis=0).astype(F32)
    mine_a = tree_sum(ring_a).astype(BF16)
    yours_a = swap(mine_a, 0, 1)
    dcs = jnp.concatenate(ordered([mine_d, after(far_d, mine_a)], y_at), axis=1)
    mine_d, send_d = ordered([dcs[:count], dcs[count:]], s & 1)
    dcs = ordered([mine_d, swap(send_d, 1)], s & 1)
    dcs = [v[:, i * quarter : (i + 1) * quarter] for i in range(2) for v in dcs]
    c32 = cond.astype(F32)
    sig = 1.0 / (1.0 + jnp.exp(-c32))
    grad_cond = jnp.concatenate(dcs, axis=1) * (sig * (1.0 + c32 * (1.0 - sig)))

    tall = jnp.concatenate(
        [v.reshape(3, half, width).transpose(1, 0, 2).reshape(half, 3 * width) for v in by_x(mine_a, yours_a)],
        axis=0,
    )
    gw_qkv = tall.astype(F32)

    return (
        block_out,
        grad_tokens,
        grad_cond,
        gw_ada,
        grads_b[0],
        gw_qkv,
        grads_b[1],
        gw_o,
        grads_b[2],
        gw_1,
        grads_b[3],
        gw_2,
        grads_b[4],
    )


def solution(mesh):
    lead = P(("rep", "shard"))
    part = P("shard")
    return jax.shard_map(
        on_device,
        mesh=mesh,
        in_specs=(lead, lead) + (part,) * 10 + (lead,),
        out_specs=(lead,) * 3 + (part,) * 10,
        check_vma=False,
    )
```

```python
import functools
import math

import jax
import jax.numpy as jnp
from jax import lax
from jax.experimental import pallas as pl
from jax.experimental.pallas import tpu as pltpu
from jax.sharding import PartitionSpec as P

HEADS = 6
F32 = jnp.float32
BF16 = jnp.bfloat16
EPS = 1e-06
GELU_C = math.sqrt(2.0 / math.pi)
GELU_A = 0.044715


def nn(a, b):
    return lax.dot_general(a, b, (((1,), (0,)), ((), ())), preferred_element_type=F32)


def nt(a, b):
    return lax.dot_general(a, b, (((1,), (1,)), ((), ())), preferred_element_type=F32)


def tn(a, b):
    return lax.dot_general(a, b, (((0,), (0,)), ((), ())), preferred_element_type=F32)


def norm_parts(x):
    centred = x - jnp.mean(x, axis=-1, keepdims=True)
    rstd = lax.rsqrt(jnp.mean(centred * centred, axis=-1, keepdims=True) + EPS)
    return centred * rstd, rstd


def norm_back(normed, rstd, grad):
    inner = jnp.mean(grad, axis=-1, keepdims=True)
    along = jnp.mean(grad * normed, axis=-1, keepdims=True)
    return rstd * (grad - inner - normed * along)


def piece_copies(mine, pieces, whole, sems):
    rows = pieces[0].shape[0]
    return [
        pltpu.make_async_copy(
            piece,
            whole.at[pl.ds(pl.multiple_of(jnp.bitwise_xor(mine, k) * rows, 32), rows)],
            sems.at[k],
        )
        for k, piece in enumerate(pieces)
    ]


def half_mask(shape, half):
    lane = lax.broadcasted_iota(jnp.int32, shape, len(shape) - 1)
    return (lane < shape[-1] // 2) if half == 0 else (lane >= shape[-1] // 2)


def pack(info, w_o, w_1, w_2, tall):
    rows, width = w_o.shape
    tall[0:rows] = w_o[...]
    many = w_1.shape[1] // width
    for i in range(many):
        tall[(1 + i) * rows : (2 + i) * rows] = w_1[:, i * width : (i + 1) * width]
    tall[(1 + many) * rows :] = w_2[...]


def ada_parts(info, c0, c1, c2, c3, w_ada, b_ada, b_qv, b_o, b_1, b_2, *refs):
    outs, share, packed = refs[0:8], refs[8], refs[9]
    share[...] = jnp.zeros_like(share)
    packed[...] = jnp.zeros_like(packed)
    n = b_ada.shape[0]
    row = b_ada[...].astype(F32).reshape(1, n)
    for j in range(4):

        @pl.when(info[0] == j)
        def _():
            share[:, j * n : (j + 1) * n] = row

    for i, b in enumerate((b_qv, b_o, b_1, b_2)):
        packed[i : i + 1, 0 : b.shape[0]] = b[...].astype(F32).reshape(1, b.shape[0])
    m = w_ada.shape[1] // 3
    for cond, first, rest in zip((c0, c1, c2, c3), outs[0:4], outs[4:8]):
        c = cond[...].astype(F32)
        cs = c / (1.0 + jnp.exp(-c))
        cut = cs.shape[1] // 4
        mine = sum(
            jnp.where(info[0] == j, cs[:, j * cut : (j + 1) * cut], 0.0) for j in range(4)
        ).astype(BF16)
        part = nn(mine, w_ada[...]) + share[...]
        first[:, 0:m] = part[:, 0:m]
        first[:, m:] = packed[...]
        rest[...] = part[:, m:]


def bias_row(table, at, n):
    return jnp.concatenate([table[i, at : at + 1, 0:n] for i in range(4)], axis=1)


def attn_fwd(info, tok, *refs, per):
    parts, wq = refs[0:4], refs[4:8]
    m1_o, qkv_o, p_o, att_o, ada, table, wq_o = refs[8:15]
    wq_s, bias_s, sem_q = refs[15:]
    step = pl.program_id(0)
    width = tok.shape[-1]

    @pl.when(step == 0)
    def _():
        cq = piece_copies(info[0], wq, wq_s, sem_q)
        for copy in cq:
            copy.start()
        ada[...] = sum(v[:, 0 : 2 * width] for v in parts)
        for k in range(4):
            table[jnp.bitwise_xor(info[0], k)] = parts[k][:, 2 * width :]
        row_qv = bias_row(table, 0, width // 2)
        bias_s[:, 0:width] = row_qv[:, 0:width]
        bias_s[:, width : 2 * width] = jnp.zeros((1, width), F32)
        bias_s[:, 2 * width : 3 * width] = row_qv[:, width : 2 * width]
        for copy in cq:
            copy.wait()
        wq_o[...] = wq_s[...]

    qkvs, ss, ps, atts = {}, {}, {}, {}
    part = lambda l, at, j: qkvs[l][:, at + 128 * j : at + 128 * j + 128]

    def stage_q(l):
        row = pl.ds(step * per + l, 1)
        shift = ada[row, 0:width]
        scale = ada[row, width : 2 * width]
        n1, _ = norm_parts(tok[l].astype(F32))
        m1 = (n1 * (1.0 + scale) + shift).astype(BF16)
        m1_o[l] = m1
        qkvs[l] = (nn(m1, wq_s[...]) + bias_s[...]).astype(BF16)
        qkv_o[l] = qkvs[l]

    def stage_a(u):
        l, t = divmod(u, HEADS)
        j, h = t // 2, t % 2
        k = part(l, width, j)
        ss[u] = nt(jnp.where(half_mask(k.shape, h), k, jnp.zeros_like(k)), part(l, 0, j))

    def stage_b(u):
        l, t = divmod(u, HEADS)
        s = ss[u]
        top = jnp.max(s, axis=0, keepdims=True)
        e = jnp.exp((s - top) * 0.125)
        total = jnp.sum(e, axis=0, keepdims=True)
        ps[u] = (e * (1.0 / total)).astype(BF16)
        p_o[l, t] = ps[u]

    def stage_c(u):
        l, t = divmod(u, HEADS)
        j = t // 2
        atts[u] = tn(ps[u], part(l, 2 * width, j))
        if t % 2:
            att = jnp.where(half_mask(atts[u].shape, 0), atts[u - 1], atts[u])
            att_o[l, :, 128 * j : 128 * j + 128] = att.astype(BF16)

    n = HEADS * per
    stage_q(0)
    for u in range(n + 2):
        if u < n:
            stage_a(u)
        if u % HEADS == 1 and u // HEADS + 1 < per:
            stage_q(u // HEADS + 1)
        if 0 <= u - 1 < n:
            stage_b(u - 1)
        if 0 <= u - 2 < n:
            stage_c(u - 2)


def ffn_both(info, tok, att_i, dy_i, cond, table, *refs, per, chunk):
    ada_parts, pieces = refs[0:4], refs[4:8]
    out_o, dx1_o, datt_o, early_o, cs_o, keep_o, send_o = refs[8:15]
    wo_s, w1_s, w2_s, go_s, g1_s, g2_s, small_s, gb_s, bo_s, b1_s, b2_s, ada, sems = refs[15:]
    step = pl.program_id(0)
    length, width = tok.shape[1:]
    hidden = w1_s.shape[1]

    @pl.when(step == 0)
    def _():
        copies, n, rows = [], hidden // width + 2, width // 4
        for k, piece in enumerate(pieces):
            at = pl.multiple_of(jnp.bitwise_xor(info[0], k) * rows, 32)
            at2 = pl.multiple_of(jnp.bitwise_xor(info[0], k) * (hidden // 4), 32)
            places = [wo_s.at[pl.ds(at, rows)]]
            places += [
                w1_s.at[pl.ds(at, rows), i * width : (i + 1) * width] for i in range(n - 2)
            ]
            places += [w2_s.at[pl.ds(at2, hidden // 4)]]
            start = 0
            for i, place in enumerate(places):
                source = piece.at[start : start + place.shape[0]]
                copies.append(pltpu.make_async_copy(source, place, sems.at[n * k + i]))
                start += place.shape[0]
        for copy in copies:
            copy.start()
        go_s[...] = jnp.zeros_like(go_s)
        g1_s[...] = jnp.zeros_like(g1_s)
        g2_s[...] = jnp.zeros_like(g2_s)
        gb_s[...] = jnp.zeros_like(gb_s)
        ada[...] = sum(v[...] for v in ada_parts)
        bo_s[...] = bias_row(table, 1, width // 4)
        b1_s[...] = bias_row(table, 2, hidden // 4)
        b2_s[...] = bias_row(table, 3, width // 4)
        c = cond[...].astype(F32)
        cs_o[...] = (c / (1.0 + jnp.exp(-c))).astype(BF16)
        for copy in copies:
            copy.wait()

    def rows_of(at):
        return jnp.stack(
            [ada[pl.ds(step * per + l, 1), at * width : (at + 1) * width] for l in range(per)]
        )

    def flat(v):
        return v.reshape(per * length, v.shape[-1])

    def deep(v):
        return v.reshape(per, length, v.shape[-1])

    gate1, shift2, scale2, gate2 = rows_of(0), rows_of(1), rows_of(2), rows_of(3)
    att = flat(att_i[...])
    branch = deep(nn(att, wo_s[...]) + bo_s[...])
    x1 = tok[...].astype(F32) + gate1 * branch
    n2, rstd2 = norm_parts(x1)
    m2 = flat((n2 * (1.0 + scale2) + shift2).astype(BF16))
    dy = dy_i[...].astype(F32)
    df = flat((dy * gate2).astype(BF16))
    df_t = df.T
    m2_t = m2.T
    ffn = None
    dm2 = None
    for j in range(hidden // chunk):
        cols = slice(j * chunk, (j + 1) * chunk)
        h = nn(m2, w1_s[:, cols]) + b1_s[:, cols]
        hh = h * h
        u = h * (GELU_C + (GELU_C * GELU_A) * hh)
        half_t = 0.5 + 0.5 * jnp.tanh(u)
        g = (h * half_t).astype(BF16)
        slope = half_t * (1.0 + (1.0 - half_t) * (6.0 * u - (4.0 * GELU_C) * h))
        part = nn(g, w2_s[cols, :])
        ffn = part if ffn is None else ffn + part
        g2_s[:, cols] += nn(df_t, g)
        dh32 = nt(df, w2_s[cols, :]) * slope
        dh = dh32.astype(BF16)
        gb_s[0:1, cols] += jnp.sum(dh.astype(F32), axis=0, keepdims=True)
        g1_s[:, cols] += nn(m2_t, dh)
        part = nt(dh, w1_s[:, cols])
        dm2 = part if dm2 is None else dm2 + part
    ffn = deep(ffn + b2_s[...])
    dm2 = deep(dm2)
    out_o[...] = (x1 + gate2 * ffn).astype(BF16)
    gb_s[1:2, width : 2 * width] += jnp.sum(df.astype(F32), axis=0, keepdims=True)
    d_gate2 = jnp.sum(dy * ffn, axis=1)
    d_scale2 = jnp.sum(dm2 * n2, axis=1)
    d_shift2 = jnp.sum(dm2, axis=1)
    dx1 = dy + norm_back(n2, rstd2, dm2 * (1.0 + scale2))
    dx1_o[...] = dx1
    do = flat((dx1 * gate1).astype(BF16))
    d_gate1 = jnp.sum(dx1 * branch, axis=1)
    for l in range(per):
        row = pl.ds(step * per + l, 1)
        small_s[row, 0:width] = d_gate1[l : l + 1]
        small_s[row, width : 2 * width] = d_shift2[l : l + 1]
        small_s[row, 2 * width : 3 * width] = d_scale2[l : l + 1]
        small_s[row, 3 * width : 4 * width] = d_gate2[l : l + 1]
    gb_s[1:2, 0:width] += jnp.sum(do.astype(F32), axis=0, keepdims=True)
    go_s[...] += tn(att, do)
    datt_o[...] = deep(nt(do, wo_s[...]).astype(BF16))

    @pl.when(step == pl.num_programs(0) - 1)
    def _():
        for i in range(4):
            early_o[8 * i : 8 * i + 8, :] = small_s[:, i * width : (i + 1) * width].astype(BF16)
        pack = [gb_s[0:1, i * width : (i + 1) * width] for i in range(hidden // width)]
        pack += [gb_s[1:2, 0:width], gb_s[1:2, width : 2 * width]]
        pack += [jnp.zeros((1, width), F32)] * (8 - len(pack))
        early_o[32:40, :] = jnp.concatenate(pack, axis=0).astype(BF16)
        core = jnp.bitwise_and(info[0], 1)
        half = width // 8
        for y in range(2):
            for which, ref in enumerate((keep_o, send_o)):
                shard = 2 * y + jnp.bitwise_xor(core, which)
                for x in range(2):
                    take = pl.ds(pl.multiple_of(shard * 2 * half + x * half, 8), half)
                    wide = pl.ds(pl.multiple_of(shard * width, 128), width)
                    for z in range(4):
                        at = 2 * half * z
                        ref[y, x, at : at + half, :] = g1_s[
                            take, z * width : (z + 1) * width
                        ].astype(BF16)
                        rows = slice((4 * x + z) * half, (4 * x + z + 1) * half)
                        ref[y, x, at + half : at + 2 * half, :] = g2_s[rows, wide].astype(BF16)
                    ref[y, x, 8 * half : 9 * half, :] = go_s[take, :].astype(BF16)


def attn_bwd(info, tok, m1_i, qkv_i, p_i, datt_i, dx1_i, ada, wq_s, *refs, per, base, last):
    step = pl.program_id(0)
    length, width = tok.shape[1:]
    if last:
        _, g_i, small_i, gb_i, cs = refs[0:5]
        gtok_o, late_o, keep_o, send_o = refs[5:9]
        g_s, small_s, gb_s = refs[9:]
    else:
        gtok_o, g_s, small_s, gb_s = refs

    @pl.when(step == 0)
    def _():
        if last:
            g_s[...] = g_i[...]
            small_s[...] = small_i[...]
            gb_s[...] = gb_i[...]
        else:
            g_s[...] = jnp.zeros_like(g_s)
            small_s[...] = jnp.zeros_like(small_s)
            gb_s[...] = jnp.zeros_like(gb_s)

    part = lambda ref, l, at, j: ref[l, :, at + 128 * j : at + 128 * j + 128]
    dvs, dps, dss, dks, dqs, dqkvs, dm1s = {}, {}, {}, {}, {}, {}, {}

    def stage_a(u):
        l, t = divmod(u, HEADS)
        j, h = t // 2, t % 2
        v, datt = part(qkv_i, l, 2 * width, j), part(datt_i, l, 0, j)
        vm = jnp.where(half_mask(v.shape, h), v, jnp.zeros_like(v))
        dps[u] = nt(vm, datt)
        dvs[u] = nn(p_i[l, t], datt)

    def stage_b(u):
        l, t = divmod(u, HEADS)
        p32 = p_i[l, t].astype(F32)
        pd = p32 * dps[u]
        dss[u] = (pd - p32 * jnp.sum(pd, axis=0, keepdims=True)).astype(BF16)

    def stage_c(u):
        l, t = divmod(u, HEADS)
        j = t // 2
        dks[u] = nn(dss[u], part(qkv_i, l, 0, j)) * 0.125
        dqs[u] = tn(dss[u], part(qkv_i, l, width, j)) * 0.125

    def stage_f(l):
        grads = [
            jnp.where(half_mask(d[u].shape, 0), d[u], d[u + 1]).astype(BF16)
            for d in (dqs, dks, dvs)
            for u in range(l * HEADS, (l + 1) * HEADS, 2)
        ]
        dqkvs[l] = jnp.concatenate(grads, axis=-1)
        dm1s[l] = nt(dqkvs[l], wq_s[...])
        g_s[...] += nn(m1_i[l].T, dqkvs[l])

    def stage_g(l):
        dqkv, dm1 = dqkvs[l], dm1s[l]
        row = pl.ds(base + step * per + l, 1)
        scale = ada[row, width : 2 * width]
        n1, rstd1 = norm_parts(tok[l].astype(F32))
        sums = jnp.sum(dqkv.astype(F32), axis=0, keepdims=True)
        gb_s[0:1, :] += sums[:, 0:width]
        gb_s[1:2, :] += sums[:, 2 * width : 3 * width]
        small_s[row, 0:width] = jnp.sum(dm1, axis=0, keepdims=True)
        small_s[row, width : 2 * width] = jnp.sum(dm1 * n1, axis=0, keepdims=True)
        gtok_o[l] = dx1_i[l] + norm_back(n1, rstd1, dm1 * (1.0 + scale))

    n = HEADS * per
    for u in range(n + 2 + 0 + 0):
        if u < n:
            stage_a(u)
        if 0 <= u - 1 < n:
            stage_b(u - 1)
        if 0 <= u - 2 < n:
            stage_c(u - 2)
        f = u - 2 - 0
        if 0 <= f < n and f % HEADS == HEADS - 1:
            stage_f(f // HEADS)
        g = f - 0
        if 0 <= g < n and g % HEADS == HEADS - 1:
            stage_g(g // HEADS)

    if last:

        @pl.when(step == pl.num_programs(0) - 1)
        def _():
            for i in range(2):
                late_o[8 * i : 8 * i + 8, :] = small_s[:, i * width : (i + 1) * width].astype(BF16)
            late_o[16:24, :] = gb_s[...].astype(BF16)
            late_o[24:32, :] = cs[...]
            core = jnp.bitwise_and(info[0], 1)
            half = width // 8
            for y in range(2):
                for which, ref in enumerate((keep_o, send_o)):
                    shard = 2 * y + jnp.bitwise_xor(core, which)
                    for x in range(2):
                        take = pl.ds(pl.multiple_of(shard * 2 * half + x * half, 8), half)
                        ref[y, x] = g_s[take, :].astype(BF16)


def join(info, keep, got, *refs):
    late, outs = refs[:-4], refs[-4:]
    half, width = keep.shape[2], late[0].shape[1]
    n = late[0].shape[0]
    for k, out in enumerate(outs):
        y, x = jnp.bitwise_xor(info[1], k >> 1), jnp.bitwise_xor(info[2], k & 1)
        total = (keep[y, x].astype(F32) + got[y, x].astype(F32)).astype(BF16)
        for i in range(3):
            out[i * half : (i + 1) * half] = total[:, i * width : (i + 1) * width]
        for z, piece in enumerate(late):
            at = pl.multiple_of(3 * half + n * jnp.bitwise_xor(info[3], z), 16)
            out[pl.ds(at, n)] = piece[0:n]


def finish(info, w_late, sum_late, w_early, sum_early, few, gw, gb_ada, gb_o, gb_1, gb_2, row):
    cols, width = w_late.shape[1], few.shape[1]
    gw[:, 0:cols] = w_late[...]
    gw[:, cols:] = w_early[...]
    row[0:1, 0:cols] = sum_late[...]
    row[0:1, cols:] = sum_early[...]
    n_a, n_o, n_1 = gb_ada.shape[0], gb_o.shape[0], gb_1.shape[0]
    rest = 4 * n_1 // width
    for i in range(rest):
        row[1:2, i * width : (i + 1) * width] = few[i : i + 1]
    row[2:3, 0:width] = few[rest : rest + 1]
    row[3:4, 0:width] = few[rest + 1 : rest + 2]
    for j in range(4):

        @pl.when(info[0] == j)
        def _():
            gb_ada[...] = row[0, j * n_a : (j + 1) * n_a]
            gb_1[...] = row[1, j * n_1 : (j + 1) * n_1]
            gb_o[...] = row[2, j * n_o : (j + 1) * n_o]
            gb_2[...] = row[3, j * n_o : (j + 1) * n_o]


def tree_sum(values):
    values = [v.astype(F32) for v in values]
    while len(values) > 1:
        values = [values[2 * i] + values[2 * i + 1] for i in range(len(values) // 2)]
    return values[0]


def ordered(values, me):
    bit = 1
    while bit < len(values):
        flip = (me & bit) != 0
        values = [jnp.where(flip, values[i ^ bit], values[i]) for i in range(len(values))]
        bit *= 2
    return values


def after(values, *deps):
    flat, tree = jax.tree.flatten(values)
    out = lax.optimization_barrier(tuple(flat) + tuple(deps))
    return jax.tree.unflatten(tree, out[: len(flat)])


def full(shape):
    return pl.BlockSpec(shape, lambda *_: (0,) * len(shape))


def call(body, info, operands, specs, outs, out_specs, scratch, grid, vmem, flops, traffic, exps=0, alias=None):
    return pl.pallas_call(
        body,
        out_shape=outs,
        input_output_aliases=alias or {},
        grid_spec=pltpu.PrefetchScalarGridSpec(
            num_scalar_prefetch=1,
            grid=grid,
            in_specs=specs,
            out_specs=out_specs,
            scratch_shapes=scratch,
        ),
        compiler_params=pltpu.CompilerParams(
            dimension_semantics=("arbitrary",) * len(grid), vmem_limit_bytes=vmem << 20
        ),
        cost_estimate=pl.CostEstimate(flops=flops, bytes_accessed=traffic, transcendentals=exps),
    )(info, *operands)


def on_device(
    latent_tokens, cond, w_ada, b_ada, w_qkv, b_qv, w_o, b_o, w_1, b_1, w_2, b_2, grad_out
):
    count, length, width = latent_tokens.shape
    hidden = w_1.shape[1]
    quarter, half = width // 4, width // 8
    reps = lax.axis_size("rep")
    shards = lax.axis_size("shard")
    s = lax.axis_index("shard")
    r = lax.axis_index("rep")
    y_at, x_at, z_at = s >> 1, r & 1, r >> 1
    n_z = reps // 2
    info = jnp.stack([s, y_at, x_at, z_at]).astype(jnp.int32)

    def swap(v, shard_bits=0, rep_bits=0):
        pairs = [
            (i * shards + j, (i ^ rep_bits) * shards + (j ^ shard_bits))
            for i in range(reps)
            for j in range(shards)
        ]
        return lax.ppermute(v, ("rep", "shard"), pairs)

    whole = lambda vs: [full(v.shape) for v in vs]
    conds = [cond] + [swap(cond, k) for k in range(1, 4)]
    ins = tuple(conds) + (w_ada, b_ada, b_qv, b_o, b_1, b_2)
    outs = [jax.ShapeDtypeStruct((count, 3 * width), F32)] * 4
    outs += [jax.ShapeDtypeStruct((count, 4 * width), F32)] * 4
    scratch = [pltpu.VMEM((1, 6 * width), F32), pltpu.VMEM((8, width), F32)]
    parts = call(
        ada_parts, info, ins, whole(ins), outs, whole(outs), scratch, (1,), 60, 1 << 24, 1 << 20
    )
    near_qkv, far_qkv = after((w_qkv, w_qkv), *conds)
    near_qkv, far_qkv = swap(near_qkv, 1), swap(far_qkv, 2)
    p_qkv = (w_qkv, near_qkv, far_qkv, swap(far_qkv, 1))
    tall = quarter + quarter * hidden // width + hidden // 4
    ins = after((w_o, w_1, w_2), parts[0])
    outs = [jax.ShapeDtypeStruct((tall, width), BF16)]
    (ffn_w,) = call(pack, info, ins, whole(ins), outs, whole(outs), [], (1,), 60, 0, 1 << 20)
    near_w = swap(ffn_w, 1)
    parts, later = parts[:4], parts[4:]
    parts = [parts[0]] + [swap(parts[k], k) for k in range(1, 4)]
    *later, ffn_far = after(list(later) + [ffn_w], *parts)
    later = [later[0]] + [swap(later[k], k) for k in range(1, 4)]
    far_w = swap(ffn_far, 2)

    anyspec = pl.BlockSpec(memory_space=pl.ANY)
    dma4 = pltpu.SemaphoreType.DMA((4,))
    tokens = count * length

    per = 2
    per3 = 1
    lat = lambda *tail: pl.BlockSpec((per,) + tail, lambda i, _: (i,) + (0,) * len(tail))
    m1, qkv, probs, att, ada, table, wq_all = call(
        functools.partial(attn_fwd, per=per),
        info,
        (latent_tokens,) + tuple(parts) + p_qkv,
        [lat(length, width)] + [full(v.shape) for v in parts] + [anyspec] * 4,
        [
            jax.ShapeDtypeStruct((count, length, width), BF16),
            jax.ShapeDtypeStruct((count, length, 3 * width), BF16),
            jax.ShapeDtypeStruct((count, HEADS, length, length), BF16),
            jax.ShapeDtypeStruct((count, length, width), BF16),
            jax.ShapeDtypeStruct((count, 2 * width), F32),
            jax.ShapeDtypeStruct((4, 8, width), F32),
            jax.ShapeDtypeStruct((width, 3 * width), BF16),
        ],
        [
            lat(length, width),
            lat(length, 3 * width),
            lat(HEADS, length, length),
            lat(length, width),
            full((count, 2 * width)),
            full((4, 8, width)),
            full((width, 3 * width)),
        ],
        [pltpu.VMEM((width, 3 * width), BF16), pltpu.VMEM((1, 3 * width), F32), dma4],
        (count // per,),
        60,
        8 * tokens * width * width + 8 * tokens * length * width,
        20 * tokens * width,
        tokens * length * HEADS,
    )

    far_w, *later = after([far_w] + later, table)
    p_ffn = (ffn_w, near_w, far_w, swap(far_w, 1))

    per2 = 2 if count % 2 == 0 else 1
    lat2 = lambda *tail: pl.BlockSpec((per2,) + tail, lambda i, _: (i,) + (0,) * len(tail))
    grads = (2, 2, 9 * half, width)
    block_out, dx1, datt, early, cs_own, keep_f, send_f = call(
        functools.partial(ffn_both, per=per2, chunk=hidden),
        info,
        (latent_tokens, att, grad_out, cond, table) + tuple(later) + p_ffn,
        [lat2(length, width)] * 3
        + [full(cond.shape), full(table.shape)]
        + [full(v.shape) for v in later]
        + [anyspec] * 4,
        [
            jax.ShapeDtypeStruct((count, length, width), BF16),
            jax.ShapeDtypeStruct((count, length, width), F32),
            jax.ShapeDtypeStruct((count, length, width), BF16),
            jax.ShapeDtypeStruct((40, width), BF16),
            jax.ShapeDtypeStruct((count, width), BF16),
        ]
        + [jax.ShapeDtypeStruct(grads, BF16)] * 2,
        [lat2(length, width)] * 3 + [full((40, width)), full((count, width))] + [full(grads)] * 2,
        [
            pltpu.VMEM((width, width), BF16),
            pltpu.VMEM((width, hidden), BF16),
            pltpu.VMEM((hidden, width), BF16),
            pltpu.VMEM((width, width), F32),
            pltpu.VMEM((width, hidden), F32),
            pltpu.VMEM((width, hidden), F32),
            pltpu.VMEM((8, 4 * width), F32),
            pltpu.VMEM((8, 5 * width), F32),
            pltpu.VMEM((1, width), F32),
            pltpu.VMEM((1, hidden), F32),
            pltpu.VMEM((1, width), F32),
            pltpu.VMEM((count, 4 * width), F32),
            pltpu.SemaphoreType.DMA((4 * (hidden // width + 2),)),
        ],
        (count // per2,),
        60,
        12 * tokens * width * hidden + 6 * tokens * width * width,
        14 * tokens * width,
        tokens * hidden,
    )

    def chip_sum(keep, send):
        got = swap(send, 1)

        def part(y, x):
            both = [
                lax.dynamic_index_in_dim(
                    lax.dynamic_index_in_dim(v, y, 0, keepdims=False), x, 0, keepdims=False
                ).astype(F32)
                for v in (keep, got)
            ]
            return (both[0] + both[1]).astype(BF16)

        return [part(y_at ^ (k >> 1), x_at ^ (k & 1)) for k in range(4)]

    def backward(base, last, info, extra, extra_specs, outs, out_specs, scratch, alias):
        half_n = count // 2
        at = lambda *tail: pl.BlockSpec(
            (per3,) + tail, lambda i, _: (i + base // per3,) + (0,) * len(tail)
        )
        return call(
            functools.partial(attn_bwd, per=per3, base=base, last=last),
            info,
            (latent_tokens, m1, qkv, probs, datt, dx1, ada, wq_all) + extra,
            [
                at(length, width),
                at(length, width),
                at(length, 3 * width),
                at(HEADS, length, length),
                at(length, width),
                at(length, width),
                full(ada.shape),
                full(wq_all.shape),
            ]
            + extra_specs,
            [jax.ShapeDtypeStruct((count, length, width), F32)] + outs,
            [at(length, width)] + out_specs,
            scratch,
            (half_n // per3,),
            50,
            6 * tokens * width * width + 5 * tokens * length * width,
            15 * tokens * width,
            0,
            alias,
        )

    acc = [(width, 3 * width), (8, 2 * width), (8, width)]
    acc_shapes = [jax.ShapeDtypeStruct(v, F32) for v in acc]
    acc_specs = [full(v) for v in acc]

    def over_plane(own, sends):
        return [own] + [swap(sends[k - 1], 2 * (k >> 1), k & 1) for k in range(1, 4)]

    z_order = sorted(range(1, n_z), key=lambda k: (k & 3) % 3 if k & 3 else 4)

    def over_z(own, sends):
        got = {k: swap(sends[k - 1], 0, 2 * k) for k in z_order}
        return [own] + [got[k] for k in range(1, n_z)]

    first = x_at == 0

    def by_x(mine, yours):
        return jnp.where(first, mine, yours), jnp.where(first, yours, mine)

    def pair(v, shard_bits, rep_bits, second):
        other = swap(v, shard_bits, rep_bits)
        return jnp.concatenate(
            [jnp.where(second, other, v), jnp.where(second, v, other)], axis=0
        )

    def z_pair(v, bit):
        return pair(v, 0, 2 * bit, (z_at & bit) != 0)

    n_f, n_e = 9 * half, early.shape[0]
    parts_f = chip_sum(keep_f, send_f)

    got = over_plane(parts_f[0], parts_f[1:])
    early_y = pair(early, 2, 0, y_at == 1)
    gtok, g_half, small_half, gb_half = backward(
        0, False, after(info, *parts_f), (), [], acc_shapes, acc_specs, [], None
    )
    *got, early_y = after(got + [early_y], gb_half)
    total_f = tree_sum(got).astype(BF16)
    z_low = z_at & 3
    loads = [
        jnp.concatenate(
            [
                lax.dynamic_slice_in_dim(total_f, (z_low ^ (k & 3)) * 2 * half, 2 * half, 0),
                total_f[8 * half :],
                early_y,
            ],
            axis=0,
        )
        for k in range(n_z)
    ]

    got = over_z(loads[0], loads[1:])
    send_shape = (2, 2, half, 3 * width)
    grad_tokens, late, keep_a, send_a = backward(
        count // 2,
        True,
        after(info, *loads),
        (gtok, g_half, small_half, gb_half, cs_own),
        [anyspec] + acc_specs + [full(cs_own.shape)],
        [
            jax.ShapeDtypeStruct((32, width), BF16),
            jax.ShapeDtypeStruct(send_shape, BF16),
            jax.ShapeDtypeStruct(send_shape, BF16),
        ],
        [full((32, width)), full(send_shape), full(send_shape)],
        [pltpu.VMEM(v, F32) for v in acc],
        {9: 0},
    )
    *got, keep_a, send_a, late = after(got + [keep_a, send_a, late])
    early_g = jnp.concatenate(ordered([v[3 * half :] for v in got], z_at), axis=0)
    piece_f = tree_sum([v[: 2 * half] for v in got]).astype(BF16)
    out_f = tree_sum([v[2 * half : 3 * half] for v in got]).astype(BF16)

    n_l, n_e = late.shape[0], early.shape[0]
    got_a = swap(send_a, 1)
    both = jnp.concatenate([late, piece_f], axis=0)
    late_z = over_z(late, [both] + [late] * (n_z - 2))
    got_a, *late_z, early_g = after([got_a] + late_z + [early_g])
    first_f = late_z[1][n_l:]

    ins = (keep_a, got_a) + tuple(late_z)
    outs = [jax.ShapeDtypeStruct((3 * half + n_z * n_l, width), BF16)] * 4
    loads = call(join, info, ins, whole(ins), outs, whole(outs), [], (1,), 16, 0, 1 << 20)
    got = over_plane(loads[0], loads[1:])
    two_f = jnp.concatenate([piece_f, first_f], axis=0)
    rest_f = swap(two_f, 0, 4)
    early_g = pair(early_g, 0, 1, x_at == 1)
    *got, two_f, rest_f, early_g = after(got + [two_f, rest_f, early_g])

    total_a = tree_sum([v[: 3 * half] for v in got]).astype(BF16)
    late_g = jnp.concatenate(ordered([v[3 * half :] for v in got], 2 * y_at + x_at), axis=0)
    ring_a = over_z(total_a, [total_a] * (n_z - 1))
    blocks = [two_f[: 2 * half], two_f[2 * half :], rest_f[: 2 * half], rest_f[2 * half :]]
    mine_f = jnp.concatenate(ordered(blocks, z_low) + [out_f], axis=0)
    yours_f = swap(mine_f, 0, 1)
    n_rows = late_g.shape[0]
    both_g = pair(jnp.concatenate([late_g, early_g], axis=0), 1, 0, (s & 1) == 1)
    both_g = both_g.reshape(2, -1, width)
    late_g, early_g = both_g[:, :n_rows], both_g[:, n_rows:]

    def mine(row):
        part = row.shape[0] // shards
        return lax.dynamic_slice(row, (s * part,), (part,))

    contract = lambda a, b: lax.dot_general(
        a, b, (((0,), (0,)), ((), ())), preferred_element_type=F32
    )
    early_r = early_g.reshape(2, 2, n_z, 2, n_e // 8, 8, width)
    to_rows = lambda v, i: v[..., i, :, :].reshape(-1, width)
    late_r = late_g.reshape(2, 2, 2, n_z, n_l // 8, 8, width)
    cs_all = lax.dynamic_slice_in_dim(to_rows(late_r, 3), s * quarter, quarter, 1)
    cs_turned = cs_all.reshape(2, 2, 2, n_z, 8, quarter).transpose(0, 2, 3, 1, 4, 5)
    d_early = jnp.concatenate([to_rows(early_r, i) for i in range(4)], axis=1)
    few = jnp.sum(early_r[..., 4, :, :].astype(F32), axis=(0, 1, 2, 3))
    w_early, sum_early = contract(cs_turned.reshape(-1, quarter), d_early), jnp.sum(d_early.astype(F32), axis=0)
    group_r = lax.dynamic_index_in_dim(early_r, z_at, 2, keepdims=False)
    group_r = lax.dynamic_index_in_dim(group_r, x_at, 1, keepdims=False)
    near_d = [
        group_r[:, :, i].transpose(1, 0, 2, 3).reshape(4 * count, width) for i in range(4)
    ]
    d_late = jnp.concatenate([to_rows(late_r, i) for i in range(2)], axis=1)
    w_late, sum_late = contract(cs_all, d_late), jnp.sum(d_late.astype(F32), axis=0)
    gb_late = mine(jnp.sum(late_r[..., 2, :2, :].astype(F32), axis=(0, 1, 2, 3)).reshape(-1))
    side_r = lax.dynamic_index_in_dim(late_r, x_at, 2, keepdims=False)
    side_r = lax.dynamic_index_in_dim(side_r, z_at, 2, keepdims=False)
    late_d = [side_r[:, :, i].transpose(1, 0, 2, 3).reshape(4 * 8, width) for i in range(2)]
    ins = (w_late, sum_late.reshape(1, -1), w_early, sum_early.reshape(1, -1), few)
    outs = [
        jax.ShapeDtypeStruct(shape, F32)
        for shape in (
            (quarter, 6 * width),
            (6 * width // 4,),
            (quarter,),
            (hidden // 4,),
            (quarter,),
        )
    ]
    gw_ada, gb_ada, gb_o, gb_1, gb_2 = call(
        finish,
        info,
        ins,
        whole(ins),
        outs,
        whole(outs),
        [pltpu.VMEM((8, 6 * width), F32)],
        (1,),
        16,
        0,
        1 << 20,
    )
    grads_b = [gb_ada, gb_late, gb_o, gb_1, gb_2]
    dada = jnp.concatenate(late_d + near_d, axis=1)
    dcs = lax.dot_general(dada, w_ada, (((1,), (1,)), ((), ())), preferred_element_type=F32)
    mine_d, send_d = ordered([dcs[: 2 * count], dcs[2 * count :]], y_at)
    far_d = swap(send_d, 2)
    yours_f, gw_ada, gb_late, far_d = after((yours_f, gw_ada, gb_late, far_d))
    *ring_a, yours_f = after(ring_a + [yours_f])
    sides = by_x(mine_f, yours_f)
    deep = [side[: 8 * half].reshape(4, 2 * half, width) for side in sides]
    gw_1 = jnp.concatenate(
        [side[:, :half].transpose(1, 0, 2).reshape(half, hidden) for side in deep], axis=0
    ).astype(F32)
    gw_2 = jnp.concatenate(
        [side[:, half:].reshape(4 * half, width) for side in deep], axis=0
    ).T.astype(F32)
    gw_o = jnp.concatenate([side[8 * half :] for side in sides], axis=0).astype(F32)
    mine_a = tree_sum(ring_a).astype(BF16)
    yours_a = swap(mine_a, 0, 1)
    dcs = jnp.concatenate(ordered([mine_d, after(far_d, mine_a)], y_at), axis=1)
    mine_d, send_d = ordered([dcs[:count], dcs[count:]], s & 1)
    dcs = ordered([mine_d, swap(send_d, 1)], s & 1)
    dcs = [v[:, i * quarter : (i + 1) * quarter] for i in range(2) for v in dcs]
    c32 = cond.astype(F32)
    sig = 1.0 / (1.0 + jnp.exp(-c32))
    grad_cond = jnp.concatenate(dcs, axis=1) * (sig * (1.0 + c32 * (1.0 - sig)))

    tall = jnp.concatenate(
        [v.reshape(3, half, width).transpose(1, 0, 2).reshape(half, 3 * width) for v in by_x(mine_a, yours_a)],
        axis=0,
    )
    gw_qkv = tall.astype(F32)

    return (
        block_out,
        grad_tokens,
        grad_cond,
        gw_ada,
        grads_b[0],
        gw_qkv,
        grads_b[1],
        gw_o,
        grads_b[2],
        gw_1,
        grads_b[3],
        gw_2,
        grads_b[4],
    )


def solution(mesh):
    lead = P(("rep", "shard"))
    part = P("shard")
    return jax.shard_map(
        on_device,
        mesh=mesh,
        in_specs=(lead, lead) + (part,) * 10 + (lead,),
        out_specs=(lead,) * 3 + (part,) * 10,
        check_vma=False,
    )
```

```python
import functools
import math

import jax
import jax.numpy as jnp
from jax import lax
from jax.experimental import pallas as pl
from jax.experimental.pallas import tpu as pltpu
from jax.sharding import PartitionSpec as P

HEADS = 6
F32 = jnp.float32
BF16 = jnp.bfloat16
EPS = 1e-06
GELU_C = math.sqrt(2.0 / math.pi)
GELU_A = 0.044715


def nn(a, b):
    return lax.dot_general(a, b, (((1,), (0,)), ((), ())), preferred_element_type=F32)


def nt(a, b):
    return lax.dot_general(a, b, (((1,), (1,)), ((), ())), preferred_element_type=F32)


def tn(a, b):
    return lax.dot_general(a, b, (((0,), (0,)), ((), ())), preferred_element_type=F32)


def norm_parts(x):
    centred = x - jnp.mean(x, axis=-1, keepdims=True)
    rstd = lax.rsqrt(jnp.mean(centred * centred, axis=-1, keepdims=True) + EPS)
    return centred * rstd, rstd


def norm_back(normed, rstd, grad):
    inner = jnp.mean(grad, axis=-1, keepdims=True)
    along = jnp.mean(grad * normed, axis=-1, keepdims=True)
    return rstd * (grad - inner - normed * along)


def piece_copies(mine, pieces, whole, sems):
    rows = pieces[0].shape[0]
    return [
        pltpu.make_async_copy(
            piece,
            whole.at[pl.ds(pl.multiple_of(jnp.bitwise_xor(mine, k) * rows, 32), rows)],
            sems.at[k],
        )
        for k, piece in enumerate(pieces)
    ]


def half_mask(shape, half):
    lane = lax.broadcasted_iota(jnp.int32, shape, len(shape) - 1)
    return (lane < shape[-1] // 2) if half == 0 else (lane >= shape[-1] // 2)


def pack(info, w_o, w_1, w_2, tall):
    rows, width = w_o.shape
    tall[0:rows] = w_o[...]
    many = w_1.shape[1] // width
    for i in range(many):
        tall[(1 + i) * rows : (2 + i) * rows] = w_1[:, i * width : (i + 1) * width]
    tall[(1 + many) * rows :] = w_2[...]


def ada_parts(info, c0, c1, c2, c3, w_ada, b_ada, b_qv, b_o, b_1, b_2, *refs):
    outs, share, packed = refs[0:8], refs[8], refs[9]
    share[...] = jnp.zeros_like(share)
    packed[...] = jnp.zeros_like(packed)
    n = b_ada.shape[0]
    row = b_ada[...].astype(F32).reshape(1, n)
    for j in range(4):

        @pl.when(info[0] == j)
        def _():
            share[:, j * n : (j + 1) * n] = row

    for i, b in enumerate((b_qv, b_o, b_1, b_2)):
        packed[i : i + 1, 0 : b.shape[0]] = b[...].astype(F32).reshape(1, b.shape[0])
    m = w_ada.shape[1] // 3
    for cond, first, rest in zip((c0, c1, c2, c3), outs[0:4], outs[4:8]):
        c = cond[...].astype(F32)
        cs = c / (1.0 + jnp.exp(-c))
        cut = cs.shape[1] // 4
        mine = sum(
            jnp.where(info[0] == j, cs[:, j * cut : (j + 1) * cut], 0.0) for j in range(4)
        ).astype(BF16)
        part = nn(mine, w_ada[...]) + share[...]
        first[:, 0:m] = part[:, 0:m]
        first[:, m:] = packed[...]
        rest[...] = part[:, m:]


def bias_row(table, at, n):
    return jnp.concatenate([table[i, at : at + 1, 0:n] for i in range(4)], axis=1)


def attn_fwd(info, tok, *refs, per):
    parts, wq = refs[0:4], refs[4:8]
    m1_o, qkv_o, p_o, att_o, ada, table, wq_o = refs[8:15]
    wq_s, bias_s, sem_q = refs[15:]
    step = pl.program_id(0)
    width = tok.shape[-1]

    @pl.when(step == 0)
    def _():
        cq = piece_copies(info[0], wq, wq_s, sem_q)
        for copy in cq:
            copy.start()
        ada[...] = sum(v[:, 0 : 2 * width] for v in parts)
        for k in range(4):
            table[jnp.bitwise_xor(info[0], k)] = parts[k][:, 2 * width :]
        row_qv = bias_row(table, 0, width // 2)
        bias_s[:, 0:width] = row_qv[:, 0:width]
        bias_s[:, width : 2 * width] = jnp.zeros((1, width), F32)
        bias_s[:, 2 * width : 3 * width] = row_qv[:, width : 2 * width]
        for copy in cq:
            copy.wait()
        wq_o[...] = wq_s[...]

    qkvs, ss, ps, atts = {}, {}, {}, {}
    part = lambda l, at, j: qkvs[l][:, at + 128 * j : at + 128 * j + 128]

    def stage_q(l):
        row = pl.ds(step * per + l, 1)
        shift = ada[row, 0:width]
        scale = ada[row, width : 2 * width]
        n1, _ = norm_parts(tok[l].astype(F32))
        m1 = (n1 * (1.0 + scale) + shift).astype(BF16)
        m1_o[l] = m1
        qkvs[l] = (nn(m1, wq_s[...]) + bias_s[...]).astype(BF16)
        qkv_o[l] = qkvs[l]

    def stage_a(u):
        l, t = divmod(u, HEADS)
        j, h = t // 2, t % 2
        k = part(l, width, j)
        ss[u] = nt(jnp.where(half_mask(k.shape, h), k, jnp.zeros_like(k)), part(l, 0, j))

    def stage_b(u):
        l, t = divmod(u, HEADS)
        s = ss[u]
        top = jnp.max(s, axis=0, keepdims=True)
        e = jnp.exp((s - top) * 0.125)
        total = jnp.sum(e, axis=0, keepdims=True)
        ps[u] = (e * (1.0 / total)).astype(BF16)
        p_o[l, t] = ps[u]

    def stage_c(u):
        l, t = divmod(u, HEADS)
        j = t // 2
        atts[u] = tn(ps[u], part(l, 2 * width, j))
        if t % 2:
            att = jnp.where(half_mask(atts[u].shape, 0), atts[u - 1], atts[u])
            att_o[l, :, 128 * j : 128 * j + 128] = att.astype(BF16)

    n = HEADS * per
    stage_q(0)
    for u in range(n + 2):
        if u < n:
            stage_a(u)
        if u % HEADS == 1 and u // HEADS + 1 < per:
            stage_q(u // HEADS + 1)
        if 0 <= u - 1 < n:
            stage_b(u - 1)
        if 0 <= u - 2 < n:
            stage_c(u - 2)


def ffn_both(info, tok, att_i, dy_i, cond, table, *refs, per, chunk):
    ada_parts, pieces = refs[0:4], refs[4:8]
    out_o, dx1_o, datt_o, early_o, cs_o, keep_o, send_o = refs[8:15]
    wo_s, w1_s, w2_s, go_s, g1_s, g2_s, small_s, gb_s, bo_s, b1_s, b2_s, ada, sems = refs[15:]
    step = pl.program_id(0)
    length, width = tok.shape[1:]
    hidden = w1_s.shape[1]

    @pl.when(step == 0)
    def _():
        copies, n, rows = [], hidden // width + 2, width // 4
        for k, piece in enumerate(pieces):
            at = pl.multiple_of(jnp.bitwise_xor(info[0], k) * rows, 32)
            at2 = pl.multiple_of(jnp.bitwise_xor(info[0], k) * (hidden // 4), 32)
            places = [wo_s.at[pl.ds(at, rows)]]
            places += [
                w1_s.at[pl.ds(at, rows), i * width : (i + 1) * width] for i in range(n - 2)
            ]
            places += [w2_s.at[pl.ds(at2, hidden // 4)]]
            start = 0
            for i, place in enumerate(places):
                source = piece.at[start : start + place.shape[0]]
                copies.append(pltpu.make_async_copy(source, place, sems.at[n * k + i]))
                start += place.shape[0]
        for copy in copies:
            copy.start()
        go_s[...] = jnp.zeros_like(go_s)
        g1_s[...] = jnp.zeros_like(g1_s)
        g2_s[...] = jnp.zeros_like(g2_s)
        gb_s[...] = jnp.zeros_like(gb_s)
        ada[...] = sum(v[...] for v in ada_parts)
        bo_s[...] = bias_row(table, 1, width // 4)
        b1_s[...] = bias_row(table, 2, hidden // 4)
        b2_s[...] = bias_row(table, 3, width // 4)
        c = cond[...].astype(F32)
        cs_o[...] = (c / (1.0 + jnp.exp(-c))).astype(BF16)
        for copy in copies:
            copy.wait()

    def rows_of(at):
        return jnp.stack(
            [ada[pl.ds(step * per + l, 1), at * width : (at + 1) * width] for l in range(per)]
        )

    def flat(v):
        return v.reshape(per * length, v.shape[-1])

    def deep(v):
        return v.reshape(per, length, v.shape[-1])

    gate1, shift2, scale2, gate2 = rows_of(0), rows_of(1), rows_of(2), rows_of(3)
    att = flat(att_i[...])
    branch = deep(nn(att, wo_s[...]) + bo_s[...])
    x1 = tok[...].astype(F32) + gate1 * branch
    n2, rstd2 = norm_parts(x1)
    m2 = flat((n2 * (1.0 + scale2) + shift2).astype(BF16))
    dy = dy_i[...].astype(F32)
    df = flat((dy * gate2).astype(BF16))
    df_t = df.T
    m2_t = m2.T
    ffn = None
    dm2 = None
    for j in range(hidden // chunk):
        cols = slice(j * chunk, (j + 1) * chunk)
        h = nn(m2, w1_s[:, cols]) + b1_s[:, cols]
        hh = h * h
        u = h * (GELU_C + (GELU_C * GELU_A) * hh)
        half_t = 0.5 + 0.5 * jnp.tanh(u)
        g = (h * half_t).astype(BF16)
        slope = half_t * (1.0 + (1.0 - half_t) * (6.0 * u - (4.0 * GELU_C) * h))
        part = nn(g, w2_s[cols, :])
        ffn = part if ffn is None else ffn + part
        g2_s[:, cols] += nn(df_t, g)
        dh32 = nt(df, w2_s[cols, :]) * slope
        dh = dh32.astype(BF16)
        gb_s[0:1, cols] += jnp.sum(dh.astype(F32), axis=0, keepdims=True)
        g1_s[:, cols] += nn(m2_t, dh)
        part = nt(dh, w1_s[:, cols])
        dm2 = part if dm2 is None else dm2 + part
    ffn = deep(ffn + b2_s[...])
    dm2 = deep(dm2)
    out_o[...] = (x1 + gate2 * ffn).astype(BF16)
    gb_s[1:2, width : 2 * width] += jnp.sum(df.astype(F32), axis=0, keepdims=True)
    d_gate2 = jnp.sum(dy * ffn, axis=1)
    d_scale2 = jnp.sum(dm2 * n2, axis=1)
    d_shift2 = jnp.sum(dm2, axis=1)
    dx1 = dy + norm_back(n2, rstd2, dm2 * (1.0 + scale2))
    dx1_o[...] = dx1
    do = flat((dx1 * gate1).astype(BF16))
    d_gate1 = jnp.sum(dx1 * branch, axis=1)
    for l in range(per):
        row = pl.ds(step * per + l, 1)
        small_s[row, 0:width] = d_gate1[l : l + 1]
        small_s[row, width : 2 * width] = d_shift2[l : l + 1]
        small_s[row, 2 * width : 3 * width] = d_scale2[l : l + 1]
        small_s[row, 3 * width : 4 * width] = d_gate2[l : l + 1]
    gb_s[1:2, 0:width] += jnp.sum(do.astype(F32), axis=0, keepdims=True)
    go_s[...] += tn(att, do)
    datt_o[...] = deep(nt(do, wo_s[...]).astype(BF16))

    @pl.when(step == pl.num_programs(0) - 1)
    def _():
        for i in range(4):
            early_o[8 * i : 8 * i + 8, :] = small_s[:, i * width : (i + 1) * width].astype(BF16)
        pack = [gb_s[0:1, i * width : (i + 1) * width] for i in range(hidden // width)]
        pack += [gb_s[1:2, 0:width], gb_s[1:2, width : 2 * width]]
        pack += [jnp.zeros((1, width), F32)] * (8 - len(pack))
        early_o[32:40, :] = jnp.concatenate(pack, axis=0).astype(BF16)
        core = jnp.bitwise_and(info[0], 1)
        half = width // 8
        for y in range(2):
            for which, ref in enumerate((keep_o, send_o)):
                shard = 2 * y + jnp.bitwise_xor(core, which)
                for x in range(2):
                    take = pl.ds(pl.multiple_of(shard * 2 * half + x * half, 8), half)
                    wide = pl.ds(pl.multiple_of(shard * width, 128), width)
                    for z in range(4):
                        at = 2 * half * z
                        ref[y, x, at : at + half, :] = g1_s[
                            take, z * width : (z + 1) * width
                        ].astype(BF16)
                        rows = slice((4 * x + z) * half, (4 * x + z + 1) * half)
                        ref[y, x, at + half : at + 2 * half, :] = g2_s[rows, wide].astype(BF16)
                    ref[y, x, 8 * half : 9 * half, :] = go_s[take, :].astype(BF16)


def attn_bwd(info, tok, m1_i, qkv_i, p_i, datt_i, dx1_i, ada, wq_s, *refs, per, base, last):
    step = pl.program_id(0)
    length, width = tok.shape[1:]
    if last:
        _, g_i, small_i, gb_i, cs = refs[0:5]
        gtok_o, late_o, keep_o, send_o = refs[5:9]
        g_s, small_s, gb_s = refs[9:]
    else:
        gtok_o, g_s, small_s, gb_s = refs

    @pl.when(step == 0)
    def _():
        if last:
            g_s[...] = g_i[...]
            small_s[...] = small_i[...]
            gb_s[...] = gb_i[...]
        else:
            g_s[...] = jnp.zeros_like(g_s)
            small_s[...] = jnp.zeros_like(small_s)
            gb_s[...] = jnp.zeros_like(gb_s)

    part = lambda ref, l, at, j: ref[l, :, at + 128 * j : at + 128 * j + 128]
    dvs, dps, dss, dks, dqs, dqkvs, dm1s = {}, {}, {}, {}, {}, {}, {}

    def stage_a(u):
        l, t = divmod(u, HEADS)
        j, h = t // 2, t % 2
        v, datt = part(qkv_i, l, 2 * width, j), part(datt_i, l, 0, j)
        vm = jnp.where(half_mask(v.shape, h), v, jnp.zeros_like(v))
        dps[u] = nt(vm, datt)
        dvs[u] = nn(p_i[l, t], datt)

    def stage_b(u):
        l, t = divmod(u, HEADS)
        p32 = p_i[l, t].astype(F32)
        pd = p32 * dps[u]
        dss[u] = (pd - p32 * jnp.sum(pd, axis=0, keepdims=True)).astype(BF16)

    def stage_c(u):
        l, t = divmod(u, HEADS)
        j = t // 2
        dks[u] = nn(dss[u], part(qkv_i, l, 0, j)) * 0.125
        dqs[u] = tn(dss[u], part(qkv_i, l, width, j)) * 0.125

    def stage_f(l):
        grads = [
            jnp.where(half_mask(d[u].shape, 0), d[u], d[u + 1]).astype(BF16)
            for d in (dqs, dks, dvs)
            for u in range(l * HEADS, (l + 1) * HEADS, 2)
        ]
        dqkvs[l] = jnp.concatenate(grads, axis=-1)
        dm1s[l] = nt(dqkvs[l], wq_s[...])
        g_s[...] += nn(m1_i[l].T, dqkvs[l])

    def stage_g(l):
        dqkv, dm1 = dqkvs[l], dm1s[l]
        row = pl.ds(base + step * per + l, 1)
        scale = ada[row, width : 2 * width]
        n1, rstd1 = norm_parts(tok[l].astype(F32))
        sums = jnp.sum(dqkv.astype(F32), axis=0, keepdims=True)
        gb_s[0:1, :] += sums[:, 0:width]
        gb_s[1:2, :] += sums[:, 2 * width : 3 * width]
        small_s[row, 0:width] = jnp.sum(dm1, axis=0, keepdims=True)
        small_s[row, width : 2 * width] = jnp.sum(dm1 * n1, axis=0, keepdims=True)
        gtok_o[l] = dx1_i[l] + norm_back(n1, rstd1, dm1 * (1.0 + scale))

    n = HEADS * per
    for u in range(n + 2 + 0 + 0):
        if u < n:
            stage_a(u)
        if 0 <= u - 1 < n:
            stage_b(u - 1)
        if 0 <= u - 2 < n:
            stage_c(u - 2)
        f = u - 2 - 0
        if 0 <= f < n and f % HEADS == HEADS - 1:
            stage_f(f // HEADS)
        g = f - 0
        if 0 <= g < n and g % HEADS == HEADS - 1:
            stage_g(g // HEADS)

    if last:

        @pl.when(step == pl.num_programs(0) - 1)
        def _():
            for i in range(2):
                late_o[8 * i : 8 * i + 8, :] = small_s[:, i * width : (i + 1) * width].astype(BF16)
            late_o[16:24, :] = gb_s[...].astype(BF16)
            late_o[24:32, :] = cs[...]
            core = jnp.bitwise_and(info[0], 1)
            half = width // 8
            for y in range(2):
                for which, ref in enumerate((keep_o, send_o)):
                    shard = 2 * y + jnp.bitwise_xor(core, which)
                    for x in range(2):
                        take = pl.ds(pl.multiple_of(shard * 2 * half + x * half, 8), half)
                        ref[y, x] = g_s[take, :].astype(BF16)


def join(info, keep, got, *refs):
    late, outs = refs[:-4], refs[-4:]
    half, width = keep.shape[2], late[0].shape[1]
    n = late[0].shape[0]
    for k, out in enumerate(outs):
        y, x = jnp.bitwise_xor(info[1], k >> 1), jnp.bitwise_xor(info[2], k & 1)
        total = (keep[y, x].astype(F32) + got[y, x].astype(F32)).astype(BF16)
        for i in range(3):
            out[i * half : (i + 1) * half] = total[:, i * width : (i + 1) * width]
        for z, piece in enumerate(late):
            at = pl.multiple_of(3 * half + n * jnp.bitwise_xor(info[3], z), 16)
            out[pl.ds(at, n)] = piece[0:n]


def finish(info, w_late, sum_late, w_early, sum_early, few, gw, gb_ada, gb_o, gb_1, gb_2, row):
    cols, width = w_late.shape[1], few.shape[1]
    gw[:, 0:cols] = w_late[...]
    gw[:, cols:] = w_early[...]
    row[0:1, 0:cols] = sum_late[...]
    row[0:1, cols:] = sum_early[...]
    n_a, n_o, n_1 = gb_ada.shape[0], gb_o.shape[0], gb_1.shape[0]
    rest = 4 * n_1 // width
    for i in range(rest):
        row[1:2, i * width : (i + 1) * width] = few[i : i + 1]
    row[2:3, 0:width] = few[rest : rest + 1]
    row[3:4, 0:width] = few[rest + 1 : rest + 2]
    for j in range(4):

        @pl.when(info[0] == j)
        def _():
            gb_ada[...] = row[0, j * n_a : (j + 1) * n_a]
            gb_1[...] = row[1, j * n_1 : (j + 1) * n_1]
            gb_o[...] = row[2, j * n_o : (j + 1) * n_o]
            gb_2[...] = row[3, j * n_o : (j + 1) * n_o]


def tree_sum(values):
    values = [v.astype(F32) for v in values]
    while len(values) > 1:
        values = [values[2 * i] + values[2 * i + 1] for i in range(len(values) // 2)]
    return values[0]


def ordered(values, me):
    bit = 1
    while bit < len(values):
        flip = (me & bit) != 0
        values = [jnp.where(flip, values[i ^ bit], values[i]) for i in range(len(values))]
        bit *= 2
    return values


def after(values, *deps):
    flat, tree = jax.tree.flatten(values)
    out = lax.optimization_barrier(tuple(flat) + tuple(deps))
    return jax.tree.unflatten(tree, out[: len(flat)])


def full(shape):
    return pl.BlockSpec(shape, lambda *_: (0,) * len(shape))


def call(body, info, operands, specs, outs, out_specs, scratch, grid, vmem, flops, traffic, exps=0, alias=None):
    return pl.pallas_call(
        body,
        out_shape=outs,
        input_output_aliases=alias or {},
        grid_spec=pltpu.PrefetchScalarGridSpec(
            num_scalar_prefetch=1,
            grid=grid,
            in_specs=specs,
            out_specs=out_specs,
            scratch_shapes=scratch,
        ),
        compiler_params=pltpu.CompilerParams(
            dimension_semantics=("arbitrary",) * len(grid), vmem_limit_bytes=vmem << 20
        ),
        cost_estimate=pl.CostEstimate(flops=flops, bytes_accessed=traffic, transcendentals=exps),
    )(info, *operands)


def on_device(
    latent_tokens, cond, w_ada, b_ada, w_qkv, b_qv, w_o, b_o, w_1, b_1, w_2, b_2, grad_out
):
    count, length, width = latent_tokens.shape
    hidden = w_1.shape[1]
    quarter, half = width // 4, width // 8
    reps = lax.axis_size("rep")
    shards = lax.axis_size("shard")
    s = lax.axis_index("shard")
    r = lax.axis_index("rep")
    y_at, x_at, z_at = s >> 1, r & 1, r >> 1
    n_z = reps // 2
    info = jnp.stack([s, y_at, x_at, z_at]).astype(jnp.int32)

    def swap(v, shard_bits=0, rep_bits=0):
        pairs = [
            (i * shards + j, (i ^ rep_bits) * shards + (j ^ shard_bits))
            for i in range(reps)
            for j in range(shards)
        ]
        return lax.ppermute(v, ("rep", "shard"), pairs)

    whole = lambda vs: [full(v.shape) for v in vs]
    conds = [cond] + [swap(cond, k) for k in range(1, 4)]
    ins = tuple(conds) + (w_ada, b_ada, b_qv, b_o, b_1, b_2)
    outs = [jax.ShapeDtypeStruct((count, 3 * width), F32)] * 4
    outs += [jax.ShapeDtypeStruct((count, 4 * width), F32)] * 4
    scratch = [pltpu.VMEM((1, 6 * width), F32), pltpu.VMEM((8, width), F32)]
    parts = call(
        ada_parts, info, ins, whole(ins), outs, whole(outs), scratch, (1,), 60, 1 << 24, 1 << 20
    )
    near_qkv, far_qkv = after((w_qkv, w_qkv), *conds)
    near_qkv, far_qkv = swap(near_qkv, 1), swap(far_qkv, 2)
    p_qkv = (w_qkv, near_qkv, far_qkv, swap(far_qkv, 1))
    tall = quarter + quarter * hidden // width + hidden // 4
    ins = after((w_o, w_1, w_2), parts[0])
    outs = [jax.ShapeDtypeStruct((tall, width), BF16)]
    (ffn_w,) = call(pack, info, ins, whole(ins), outs, whole(outs), [], (1,), 60, 0, 1 << 20)
    near_w = swap(ffn_w, 1)
    parts, later = parts[:4], parts[4:]
    parts = [parts[0]] + [swap(parts[k], k) for k in range(1, 4)]
    *later, ffn_far = after(list(later) + [ffn_w], *parts)
    later = [later[0]] + [swap(later[k], k) for k in range(1, 4)]
    far_w = swap(ffn_far, 2)

    anyspec = pl.BlockSpec(memory_space=pl.ANY)
    dma4 = pltpu.SemaphoreType.DMA((4,))
    tokens = count * length

    per = 2
    per3 = 1
    lat = lambda *tail: pl.BlockSpec((per,) + tail, lambda i, _: (i,) + (0,) * len(tail))
    m1, qkv, probs, att, ada, table, wq_all = call(
        functools.partial(attn_fwd, per=per),
        info,
        (latent_tokens,) + tuple(parts) + p_qkv,
        [lat(length, width)] + [full(v.shape) for v in parts] + [anyspec] * 4,
        [
            jax.ShapeDtypeStruct((count, length, width), BF16),
            jax.ShapeDtypeStruct((count, length, 3 * width), BF16),
            jax.ShapeDtypeStruct((count, HEADS, length, length), BF16),
            jax.ShapeDtypeStruct((count, length, width), BF16),
            jax.ShapeDtypeStruct((count, 2 * width), F32),
            jax.ShapeDtypeStruct((4, 8, width), F32),
            jax.ShapeDtypeStruct((width, 3 * width), BF16),
        ],
        [
            lat(length, width),
            lat(length, 3 * width),
            lat(HEADS, length, length),
            lat(length, width),
            full((count, 2 * width)),
            full((4, 8, width)),
            full((width, 3 * width)),
        ],
        [pltpu.VMEM((width, 3 * width), BF16), pltpu.VMEM((1, 3 * width), F32), dma4],
        (count // per,),
        60,
        8 * tokens * width * width + 8 * tokens * length * width,
        20 * tokens * width,
        tokens * length * HEADS,
    )

    far_w, *later = after([far_w] + later, table)
    p_ffn = (ffn_w, near_w, far_w, swap(far_w, 1))

    per2 = 2 if count % 2 == 0 else 1
    lat2 = lambda *tail: pl.BlockSpec((per2,) + tail, lambda i, _: (i,) + (0,) * len(tail))
    grads = (2, 2, 9 * half, width)
    block_out, dx1, datt, early, cs_own, keep_f, send_f = call(
        functools.partial(ffn_both, per=per2, chunk=hidden),
        info,
        (latent_tokens, att, grad_out, cond, table) + tuple(later) + p_ffn,
        [lat2(length, width)] * 3
        + [full(cond.shape), full(table.shape)]
        + [full(v.shape) for v in later]
        + [anyspec] * 4,
        [
            jax.ShapeDtypeStruct((count, length, width), BF16),
            jax.ShapeDtypeStruct((count, length, width), F32),
            jax.ShapeDtypeStruct((count, length, width), BF16),
            jax.ShapeDtypeStruct((40, width), BF16),
            jax.ShapeDtypeStruct((count, width), BF16),
        ]
        + [jax.ShapeDtypeStruct(grads, BF16)] * 2,
        [lat2(length, width)] * 3 + [full((40, width)), full((count, width))] + [full(grads)] * 2,
        [
            pltpu.VMEM((width, width), BF16),
            pltpu.VMEM((width, hidden), BF16),
            pltpu.VMEM((hidden, width), BF16),
            pltpu.VMEM((width, width), F32),
            pltpu.VMEM((width, hidden), F32),
            pltpu.VMEM((width, hidden), F32),
            pltpu.VMEM((8, 4 * width), F32),
            pltpu.VMEM((8, 5 * width), F32),
            pltpu.VMEM((1, width), F32),
            pltpu.VMEM((1, hidden), F32),
            pltpu.VMEM((1, width), F32),
            pltpu.VMEM((count, 4 * width), F32),
            pltpu.SemaphoreType.DMA((4 * (hidden // width + 2),)),
        ],
        (count // per2,),
        60,
        12 * tokens * width * hidden + 6 * tokens * width * width,
        14 * tokens * width,
        tokens * hidden,
    )

    def chip_sum(keep, send):
        got = swap(send, 1)

        def part(y, x):
            both = [
                lax.dynamic_index_in_dim(
                    lax.dynamic_index_in_dim(v, y, 0, keepdims=False), x, 0, keepdims=False
                ).astype(F32)
                for v in (keep, got)
            ]
            return (both[0] + both[1]).astype(BF16)

        return [part(y_at ^ (k >> 1), x_at ^ (k & 1)) for k in range(4)]

    def backward(base, last, info, extra, extra_specs, outs, out_specs, scratch, alias):
        half_n = count // 2
        at = lambda *tail: pl.BlockSpec(
            (per3,) + tail, lambda i, _: (i + base // per3,) + (0,) * len(tail)
        )
        return call(
            functools.partial(attn_bwd, per=per3, base=base, last=last),
            info,
            (latent_tokens, m1, qkv, probs, datt, dx1, ada, wq_all) + extra,
            [
                at(length, width),
                at(length, width),
                at(length, 3 * width),
                at(HEADS, length, length),
                at(length, width),
                at(length, width),
                full(ada.shape),
                full(wq_all.shape),
            ]
            + extra_specs,
            [jax.ShapeDtypeStruct((count, length, width), F32)] + outs,
            [at(length, width)] + out_specs,
            scratch,
            (half_n // per3,),
            50,
            6 * tokens * width * width + 5 * tokens * length * width,
            15 * tokens * width,
            0,
            alias,
        )

    acc = [(width, 3 * width), (8, 2 * width), (8, width)]
    acc_shapes = [jax.ShapeDtypeStruct(v, F32) for v in acc]
    acc_specs = [full(v) for v in acc]

    def over_plane(own, sends):
        return [own] + [swap(sends[k - 1], 2 * (k >> 1), k & 1) for k in range(1, 4)]

    z_order = sorted(range(1, n_z), key=lambda k: (k & 3) % 3 if k & 3 else 4)

    def over_z(own, sends):
        got = {k: swap(sends[k - 1], 0, 2 * k) for k in z_order}
        return [own] + [got[k] for k in range(1, n_z)]

    first = x_at == 0

    def by_x(mine, yours):
        return jnp.where(first, mine, yours), jnp.where(first, yours, mine)

    def pair(v, shard_bits, rep_bits, second):
        other = swap(v, shard_bits, rep_bits)
        return jnp.concatenate(
            [jnp.where(second, other, v), jnp.where(second, v, other)], axis=0
        )

    def z_pair(v, bit):
        return pair(v, 0, 2 * bit, (z_at & bit) != 0)

    n_f, n_e = 9 * half, early.shape[0]
    parts_f = chip_sum(keep_f, send_f)

    got = over_plane(parts_f[0], parts_f[1:])
    early_y = pair(early, 2, 0, y_at == 1)
    gtok, g_half, small_half, gb_half = backward(
        0, False, after(info, *parts_f), (), [], acc_shapes, acc_specs, [], None
    )
    *got, early_y = after(got + [early_y], gb_half)
    total_f = tree_sum(got).astype(BF16)
    z_low = z_at & 3
    loads = [
        jnp.concatenate(
            [
                lax.dynamic_slice_in_dim(total_f, (z_low ^ (k & 3)) * 2 * half, 2 * half, 0),
                total_f[8 * half :],
                early_y,
            ],
            axis=0,
        )
        for k in range(n_z)
    ]

    got = over_z(loads[0], loads[1:])
    send_shape = (2, 2, half, 3 * width)
    grad_tokens, late, keep_a, send_a = backward(
        count // 2,
        True,
        after(info, *loads),
        (gtok, g_half, small_half, gb_half, cs_own),
        [anyspec] + acc_specs + [full(cs_own.shape)],
        [
            jax.ShapeDtypeStruct((32, width), BF16),
            jax.ShapeDtypeStruct(send_shape, BF16),
            jax.ShapeDtypeStruct(send_shape, BF16),
        ],
        [full((32, width)), full(send_shape), full(send_shape)],
        [pltpu.VMEM(v, F32) for v in acc],
        {9: 0},
    )
    *got, keep_a, send_a, late = after(got + [keep_a, send_a, late])
    early_g = jnp.concatenate(ordered([v[3 * half :] for v in got], z_at), axis=0)
    piece_f = tree_sum([v[: 2 * half] for v in got]).astype(BF16)
    out_f = tree_sum([v[2 * half : 3 * half] for v in got]).astype(BF16)

    n_l, n_e = late.shape[0], early.shape[0]
    got_a = swap(send_a, 1)
    late_z, first_f = over_z(late, [late] * (n_z - 1)), swap(piece_f, 0, 2)
    got_a, *late_z, first_f, early_g = after([got_a] + late_z + [first_f, early_g])

    ins = (keep_a, got_a) + tuple(late_z)
    outs = [jax.ShapeDtypeStruct((3 * half + n_z * n_l, width), BF16)] * 4
    loads = call(join, info, ins, whole(ins), outs, whole(outs), [], (1,), 16, 0, 1 << 20)
    got = over_plane(loads[0], loads[1:])
    two_f = jnp.concatenate([piece_f, first_f], axis=0)
    rest_f = swap(two_f, 0, 4)
    early_g = pair(early_g, 0, 1, x_at == 1)
    *got, two_f, rest_f, early_g = after(got + [two_f, rest_f, early_g])

    total_a = tree_sum([v[: 3 * half] for v in got]).astype(BF16)
    late_g = jnp.concatenate(ordered([v[3 * half :] for v in got], 2 * y_at + x_at), axis=0)
    ring_a = over_z(total_a, [total_a] * (n_z - 1))
    blocks = [two_f[: 2 * half], two_f[2 * half :], rest_f[: 2 * half], rest_f[2 * half :]]
    mine_f = jnp.concatenate(ordered(blocks, z_low) + [out_f], axis=0)
    yours_f = swap(mine_f, 0, 1)
    n_rows = late_g.shape[0]
    both_g = pair(jnp.concatenate([late_g, early_g], axis=0), 1, 0, (s & 1) == 1)
    both_g = both_g.reshape(2, -1, width)
    late_g, early_g = both_g[:, :n_rows], both_g[:, n_rows:]

    def mine(row):
        part = row.shape[0] // shards
        return lax.dynamic_slice(row, (s * part,), (part,))

    contract = lambda a, b: lax.dot_general(
        a, b, (((0,), (0,)), ((), ())), preferred_element_type=F32
    )
    early_r = early_g.reshape(2, 2, n_z, 2, n_e // 8, 8, width)
    to_rows = lambda v, i: v[..., i, :, :].reshape(-1, width)
    late_r = late_g.reshape(2, 2, 2, n_z, n_l // 8, 8, width)
    cs_all = lax.dynamic_slice_in_dim(to_rows(late_r, 3), s * quarter, quarter, 1)
    cs_turned = cs_all.reshape(2, 2, 2, n_z, 8, quarter).transpose(0, 2, 3, 1, 4, 5)
    d_early = jnp.concatenate([to_rows(early_r, i) for i in range(4)], axis=1)
    few = jnp.sum(early_r[..., 4, :, :].astype(F32), axis=(0, 1, 2, 3))
    w_early, sum_early = contract(cs_turned.reshape(-1, quarter), d_early), jnp.sum(d_early.astype(F32), axis=0)
    group_r = lax.dynamic_index_in_dim(early_r, z_at, 2, keepdims=False)
    group_r = lax.dynamic_index_in_dim(group_r, x_at, 1, keepdims=False)
    near_d = [
        group_r[:, :, i].transpose(1, 0, 2, 3).reshape(4 * count, width) for i in range(4)
    ]
    d_late = jnp.concatenate([to_rows(late_r, i) for i in range(2)], axis=1)
    w_late, sum_late = contract(cs_all, d_late), jnp.sum(d_late.astype(F32), axis=0)
    gb_late = mine(jnp.sum(late_r[..., 2, :2, :].astype(F32), axis=(0, 1, 2, 3)).reshape(-1))
    side_r = lax.dynamic_index_in_dim(late_r, x_at, 2, keepdims=False)
    side_r = lax.dynamic_index_in_dim(side_r, z_at, 2, keepdims=False)
    late_d = [side_r[:, :, i].transpose(1, 0, 2, 3).reshape(4 * 8, width) for i in range(2)]
    ins = (w_late, sum_late.reshape(1, -1), w_early, sum_early.reshape(1, -1), few)
    outs = [
        jax.ShapeDtypeStruct(shape, F32)
        for shape in (
            (quarter, 6 * width),
            (6 * width // 4,),
            (quarter,),
            (hidden // 4,),
            (quarter,),
        )
    ]
    gw_ada, gb_ada, gb_o, gb_1, gb_2 = call(
        finish,
        info,
        ins,
        whole(ins),
        outs,
        whole(outs),
        [pltpu.VMEM((8, 6 * width), F32)],
        (1,),
        16,
        0,
        1 << 20,
    )
    grads_b = [gb_ada, gb_late, gb_o, gb_1, gb_2]
    dada = jnp.concatenate(late_d + near_d, axis=1)
    dcs = lax.dot_general(dada, w_ada, (((1,), (1,)), ((), ())), preferred_element_type=F32)
    mine_d, send_d = ordered([dcs[: 2 * count], dcs[2 * count :]], y_at)
    far_d = swap(send_d, 2)
    yours_f, gw_ada, gb_late, far_d = after((yours_f, gw_ada, gb_late, far_d))
    *ring_a, yours_f = after(ring_a + [yours_f])
    sides = by_x(mine_f, yours_f)
    deep = [side[: 8 * half].reshape(4, 2 * half, width) for side in sides]
    gw_1 = jnp.concatenate(
        [side[:, :half].transpose(1, 0, 2).reshape(half, hidden) for side in deep], axis=0
    ).astype(F32)
    gw_2 = jnp.concatenate(
        [side[:, half:].reshape(4 * half, width) for side in deep], axis=0
    ).T.astype(F32)
    gw_o = jnp.concatenate([side[8 * half :] for side in sides], axis=0).astype(F32)
    mine_a = tree_sum(ring_a).astype(BF16)
    yours_a = swap(mine_a, 0, 1)
    dcs = jnp.concatenate(ordered([mine_d, after(far_d, mine_a)], y_at), axis=1)
    mine_d, send_d = ordered([dcs[:count], dcs[count:]], s & 1)
    dcs = ordered([mine_d, swap(send_d, 1)], s & 1)
    dcs = [v[:, i * quarter : (i + 1) * quarter] for i in range(2) for v in dcs]
    c32 = cond.astype(F32)
    sig = 1.0 / (1.0 + jnp.exp(-c32))
    grad_cond = jnp.concatenate(dcs, axis=1) * (sig * (1.0 + c32 * (1.0 - sig)))

    tall = jnp.concatenate(
        [v.reshape(3, half, width).transpose(1, 0, 2).reshape(half, 3 * width) for v in by_x(mine_a, yours_a)],
        axis=0,
    )
    gw_qkv = tall.astype(F32)

    return (
        block_out,
        grad_tokens,
        grad_cond,
        gw_ada,
        grads_b[0],
        gw_qkv,
        grads_b[1],
        gw_o,
        grads_b[2],
        gw_1,
        grads_b[3],
        gw_2,
        grads_b[4],
    )


def solution(mesh):
    lead = P(("rep", "shard"))
    part = P("shard")
    return jax.shard_map(
        on_device,
        mesh=mesh,
        in_specs=(lead, lead) + (part,) * 10 + (lead,),
        out_specs=(lead,) * 3 + (part,) * 10,
        check_vma=False,
    )
```
